32 devices in a mesh: groups: 1, row: 32 (over z, y, x, core).
Axes of the slice: x: 2, y: 2, z: 4, core: 2. Of those that a mesh axis runs over, the one named last changes fastest.
Arguments:
- features: bfloat16 [64, 256, 256], P('groups', 'row'), may hold values from -6 to 6
- w_conv: bfloat16 [7, 9, 32, 64], replicated, may hold values from -0.25 to 0.25
- bias_in: float32 [7, 32], replicated, may hold values from -3 to 3
- w_out: bfloat16 [7, 64, 32], replicated, may hold values from -1 to 1
- bias_out: float32 [7, 64], replicated, may hold values from -2 to 2
Outputs:
- contacts: bfloat16 [64, 256, 256], P('groups', 'row')
The draws below stay inside these ranges and needn't reach their ends.
All inputs are finite; a program needn't handle non-finite values.
Results may differ from the reference program's by a relative error of at most 0.014.
Values may be sent and summed in bfloat16 or wider, within the bound.
No kernel may reach another device: no remote copies, remote signals or barrier semaphores. Data moves between devices by JAX's collectives and lax.ppermute only.
A program may use at most 64 MiB of HBM per device.

```python
import jax
import jax.numpy as jnp
from jax import lax

CH = 64
HID = 32
SECTIONS = 2
LAYERS = 7
MAP = 256


def shard_levels(key, shape, cuts, low, largest):
    gain = 1.0
    for dim, blocks in cuts:
        heights = jax.random.uniform(jax.random.fold_in(jax.random.fold_in(key, 6), dim), (blocks,), jnp.float32, low / len(cuts), largest / len(cuts))
        gain = gain * jnp.repeat(jnp.exp(heights), shape[dim] // blocks).reshape((-1,) + (1,) * (len(shape) - 1 - dim))
    return gain


def bell_draw(stream_key, shape, spread, limit, split=(), kind=jnp.bfloat16):
    drawn = jax.random.normal(stream_key, shape, jnp.float32) * spread
    if len(split) > 0:
        drawn = shard_levels(stream_key, shape, split, -0.22, 0.18) * drawn
    return jnp.clip(drawn, min=-limit, max=limit).astype(kind)


def setup_inputs(seed: int = 0, part: int = 0) -> dict:
    streams_of = jax.random.split(jax.random.key(seed), 6)
    part_splits = jax.random.split(jax.random.fold_in(streams_of[5], part), 6)
    return {
        "features": bell_draw(part_splits[0], (CH, MAP, MAP), 1.0, 6.0, ((1, 32),)),
        "w_conv": bell_draw(streams_of[1], (LAYERS, 9, HID, CH), (9 * CH) ** -0.5, 0.25),
        "bias_in": bell_draw(streams_of[2], (LAYERS, HID), 0.5, 3.0, (), jnp.float32),
        "w_out": bell_draw(streams_of[3], (LAYERS, CH, HID), HID ** -0.5, 1.0),
        "bias_out": bell_draw(streams_of[4], (LAYERS, CH), 0.3, 2.0, (), jnp.float32),
    }


dilations = (1, 2, 4)


def block_apply(field, w_conv, bias_in, w_out, bias_out, layer, dilation):
    extent = field.shape[1]
    band_rows = min(128, extent)
    padded = jnp.pad(field, ((0, 0), (dilation, dilation), (dilation, dilation)))

    def band_out(offset):
        stripe = lax.dynamic_slice_in_dim(padded, offset, band_rows + 2 * dilation, 1).astype(jnp.float32)
        total_sum = jnp.zeros((HID, band_rows, extent), jnp.float32)
        for row_tap in range(3):
            for col_tap in range(3):
                window = stripe[:, row_tap * dilation: row_tap * dilation + band_rows, col_tap * dilation: col_tap * dilation + extent]
                kernel = w_conv[layer, row_tap * 3 + col_tap].astype(jnp.float32)
                total_sum = total_sum + jnp.einsum('hc,crm->hrm', kernel, window)
        hidden = jax.nn.relu(total_sum + bias_in[layer][:, None, None]).astype(jnp.bfloat16)
        hidden = lax.optimization_barrier(hidden)
        blended = jnp.einsum('ch,hrm->crm', w_out[layer].astype(jnp.float32), hidden.astype(jnp.float32))
        residual = lax.dynamic_slice_in_dim(field, offset, band_rows, 1).astype(jnp.float32)
        return (residual + blended + bias_out[layer][:, None, None]).astype(jnp.bfloat16)

    offsets = jnp.arange(extent // band_rows, dtype=jnp.int32) * band_rows
    result = lax.map(band_out, offsets)
    return result.transpose(1, 0, 2, 3).reshape(field.shape)


def reference(features, w_conv, bias_in, w_out, bias_out):
    field = features
    layer = 0
    for section_idx in range(SECTIONS):
        for dilation in dilations:
            field = block_apply(field, w_conv, bias_in, w_out, bias_out, layer, dilation)
            layer = layer + 1
        field = ((field.astype(jnp.float32) + field.transpose(0, 2, 1).astype(jnp.float32)) * 0.5).astype(jnp.bfloat16)
    return block_apply(field, w_conv, bias_in, w_out, bias_out, layer, 1)
```

```python
import jax
import jax.numpy as jnp
from jax import lax
from jax.experimental import pallas as pl
from jax.experimental.pallas import tpu as pltpu
from jax.sharding import PartitionSpec as P

SECTIONS = 2
DEPTH = 3

dilations = (1, 2, 4)
LANES = 128


def shifted(row, dilation):
    channels, width = row.shape
    wide = row.astype(jnp.float32)
    column = lax.broadcasted_iota(jnp.int32, (channels, width), 1)
    left = jnp.where(column >= dilation, pltpu.roll(wide, dilation, 1), 0.0)
    right = jnp.where(column < width - dilation, pltpu.roll(wide, width - dilation, 1), 0.0)
    return left.astype(jnp.bfloat16), row, right.astype(jnp.bfloat16)


def put_row(stack, index, row, dilation):
    channels = row.shape[0]
    for place, part in enumerate(shifted(row, dilation)):
        stack[index, place * channels : (place + 1) * channels, :] = part


def taps(stack, index, dilation):
    return jnp.concatenate([stack[index + tap * dilation] for tap in range(3)], axis=0)


def hidden_of(window, kernel, bias):
    inner = jnp.dot(kernel, window, preferred_element_type=jnp.float32)
    return jnp.maximum(inner + bias, 0.0).astype(jnp.bfloat16)


def output_of(residual, hidden, kernel, bias):
    blended = jnp.dot(kernel, hidden, preferred_element_type=jnp.float32)
    return (residual.astype(jnp.float32) + blended + bias).astype(jnp.bfloat16)


def masked(row, row_id, map_rows):
    inside = jnp.logical_and(row_id >= 0, row_id < map_rows)
    return jnp.where(inside, row, jnp.zeros_like(row))


def loop(count, body, unroll):
    def step(index, carry):
        body(index)
        return carry

    lax.fori_loop(0, count, step, 0, unroll=unroll)


def load_shards(place, own, across, beside, wide, stack, dilation, margin):
    odd = place[0]
    shard_rows = own.shape[1]
    channels = own.shape[0]
    slots = ((own, 1), (beside, jnp.where(odd == 1, 0, 2)), (across, jnp.where(odd == 1, 2, 0)))
    blocks = own.shape[2] // LANES
    for shard, slot in slots:
        whole = shard[...].astype(jnp.float32).reshape(channels * shard_rows, own.shape[2])
        for block in range(blocks):
            wide[slot, block] = whole[:, block * LANES : (block + 1) * LANES]
    total = 3 * shard_rows - 2 * margin

    def body(index):
        source = index + margin
        slot = source // shard_rows
        picked = pl.ds(source % shard_rows, channels, stride=shard_rows)
        row = jnp.concatenate([wide[slot, block, picked, :] for block in range(blocks)], axis=1)
        put_row(stack, index, row.astype(jnp.bfloat16), dilation)

    loop(total, body, 2)
    return total


def section_one(place, own, across, beside, w_conv, bias_in, w_out, bias_out, out, wide, first, second):
    channels, shard_rows, _ = own.shape
    margin = shard_rows - sum(dilations)
    rows = load_shards(place, own, across, beside, wide, first, dilations[0], margin)
    row_id = place[1] - sum(dilations)
    source, target = first, second
    for layer, dilation in enumerate(dilations):
        rows = rows - 2 * dilation
        row_id = row_id + dilation
        last = layer == DEPTH - 1

        def body(index, source=source, target=target, row_id=row_id, layer=layer, dilation=dilation, last=last):
            hidden = hidden_of(taps(source, index, dilation), w_conv[layer], bias_in[layer])
            residual = source[index + dilation, channels : 2 * channels, :]
            row = output_of(residual, hidden, w_out[layer], bias_out[layer])
            if last:
                out[index] = row
            else:
                put_row(target, index, masked(row, row_id + index, place[2]), dilations[layer + 1])

        loop(rows, body, 2)
        source, target = target, source


def section_two(place, own, across, beside, w_conv, w_turned, bias_in, w_out, bias_out, out, first, plain, turned, plain_2, turned_2):
    channels = own.shape[1]
    inner = w_out.shape[2]
    shard_rows = own.shape[0]
    odd = place[0]
    slots = ((own, 1), (beside, jnp.where(odd == 1, 0, 2)), (across, jnp.where(odd == 1, 2, 0)))
    for shard, slot in slots:
        def copy_row(index, shard=shard, slot=slot):
            put_row(first, slot * shard_rows + index, shard[index], dilations[0])

        loop(shard_rows, copy_row, 2)
    reach = sum(dilations) + 1
    rows = shard_rows + 2 * reach
    row_id = place[1] - reach
    base = shard_rows - reach

    dilation = dilations[0]
    rows, row_id = rows - 2 * dilation, row_id + dilation
    both = jnp.concatenate([w_conv[0], w_turned[0]], axis=0)

    def block_a(index, row_id=row_id):
        bias = jnp.concatenate([bias_in[0], bias_in[0]], axis=0)
        hidden = hidden_of(taps(first, base + index, dilations[0]), both, bias)
        residual = first[base + index + dilations[0], channels : 2 * channels, :]
        for part, target in enumerate((plain, turned)):
            row = output_of(residual, hidden[part * inner : (part + 1) * inner], w_out[0], bias_out[0])
            put_row(target, index, masked(row, row_id + index, place[2]), dilations[1])

    loop(rows, block_a, 2)

    dilation = dilations[1]
    rows, row_id = rows - 2 * dilation, row_id + dilation

    def block_b(index, row_id=row_id):
        for source, target, kernel in ((plain, plain_2, w_conv), (turned, turned_2, w_turned)):
            hidden = hidden_of(taps(source, index, dilations[1]), kernel[1], bias_in[1])
            residual = source[index + dilations[1], channels : 2 * channels, :]
            row = output_of(residual, hidden, w_out[1], bias_out[1])
            put_row(target, index, masked(row, row_id + index, place[2]), dilations[2])

    loop(rows, block_b, 2)

    dilation = dilations[2]
    rows, row_id = rows - 2 * dilation, row_id + dilation

    def block_c(index, row_id=row_id):
        halves = []
        for source, kernel in ((plain_2, w_conv), (turned_2, w_turned)):
            hidden = hidden_of(taps(source, index, dilations[2]), kernel[2], bias_in[2])
            residual = source[index + dilations[2], channels : 2 * channels, :]
            halves.append(output_of(residual, hidden, w_out[2], bias_out[2]).astype(jnp.float32))
        row = ((halves[0] + halves[1]) * 0.5).astype(jnp.bfloat16)
        put_row(first, index, masked(row, row_id + index, place[2]), dilations[0])

    loop(rows, block_c, 2)

    def block_d(index):
        hidden = hidden_of(taps(first, index, dilations[0]), w_conv[3], bias_in[3])
        residual = first[index + dilations[0], channels : 2 * channels, :]
        out[index] = output_of(residual, hidden, w_out[3], bias_out[3])

    loop(shard_rows, block_d, 2)


def neighbours(array, axis):
    size = lax.axis_size(axis)
    inside = [(i, i ^ 1) for i in range(size)]
    edges = [(i, i + 1) for i in range(1, size - 1, 2)]
    edges = edges + [(j, i) for i, j in edges]
    across = lax.ppermute(array, axis, edges)
    beside = lax.ppermute(array, axis, inside)
    return across, beside


VMEM = pl.BlockSpec(memory_space=pltpu.VMEM)
SMEM = pl.BlockSpec(memory_space=pltpu.SMEM)


def on_device(features, w_conv, bias_in, w_out, bias_out):
    channels, shard_rows, width = features.shape
    layers, _, inner, _ = w_conv.shape
    size = lax.axis_size("row")
    device = lax.axis_index("row")
    place = jnp.stack([device % 2, device * shard_rows, jnp.int32(shard_rows * size)])

    across, beside = neighbours(features, "row")
    kernels = w_conv.transpose(0, 2, 1, 3).reshape(layers, inner, 9 * channels)
    swapped = w_conv[DEPTH : 2 * DEPTH].reshape(DEPTH, 3, 3, inner, channels).transpose(0, 3, 2, 1, 4)
    swapped = swapped.reshape(DEPTH, inner, 9 * channels)
    bias_in = bias_in[:, :, None]
    bias_out = bias_out[:, :, None]

    stack = pltpu.VMEM((3 * shard_rows, 3 * channels, width), jnp.bfloat16)
    params = pltpu.CompilerParams(vmem_limit_bytes=56 * 1024 * 1024)
    one = pl.pallas_call(
        section_one,
        out_shape=jax.ShapeDtypeStruct((shard_rows, channels, width), jnp.bfloat16),
        in_specs=[SMEM] + [VMEM] * 7,
        out_specs=VMEM,
        scratch_shapes=[pltpu.VMEM((3, width // LANES, channels * shard_rows, LANES), jnp.float32), stack, stack],
        compiler_params=params,
        name="section_one",
    )
    field = one(place, features, across, beside, kernels[:DEPTH], bias_in[:DEPTH], w_out[:DEPTH], bias_out[:DEPTH])

    tiles = field.reshape(shard_rows, channels, size, shard_rows).transpose(2, 3, 0, 1)
    tiles = tiles.reshape(size, shard_rows, shard_rows * channels)
    received = lax.all_to_all(tiles, "row", split_axis=0, concat_axis=0, tiled=True)
    flipped = received.reshape(size, shard_rows, shard_rows, channels).transpose(1, 3, 0, 2)
    flipped = flipped.reshape(shard_rows, channels, width)
    field = ((field.astype(jnp.float32) + flipped.astype(jnp.float32)) * 0.5).astype(jnp.bfloat16)

    across, beside = neighbours(field, "row")
    two = pl.pallas_call(
        section_two,
        out_shape=jax.ShapeDtypeStruct((shard_rows, channels, width), jnp.bfloat16),
        in_specs=[SMEM] + [VMEM] * 8,
        out_specs=VMEM,
        scratch_shapes=[stack] * 5,
        compiler_params=params,
        name="section_two",
    )
    out = two(
        place, field, across, beside, kernels[DEPTH:], swapped, bias_in[DEPTH:], w_out[DEPTH:], bias_out[DEPTH:]
    )
    return out.transpose(1, 0, 2)


def solution(mesh):
    in_specs = (P("groups", "row", None), P(), P(), P(), P())
    out_specs = P("groups", "row", None)
    return jax.shard_map(
        on_device, mesh=mesh, in_specs=in_specs, out_specs=out_specs, check_vma=False
    )
```

```python
import jax
import jax.numpy as jnp
from jax import lax
from jax.experimental import pallas as pl
from jax.experimental.pallas import tpu as pltpu
from jax.sharding import PartitionSpec as P

SECTIONS = 2
DEPTH = 3

dilations = (1, 2, 4)
LANES = 128
LAG = 2


def column_masks(channels, width, dilation):
    column = lax.broadcasted_iota(jnp.int16, (channels, width), 1)
    return column >= jnp.int16(dilation), column < jnp.int16(width - dilation)


def put_row(stack, index, row, dilation, masks):
    channels, width = row.shape
    zeros = jnp.zeros_like(row)
    stack[index, :channels, :] = jnp.where(masks[0], pltpu.roll(row, dilation, 1), zeros)
    stack[index, channels : 2 * channels, :] = row
    stack[index, 2 * channels :, :] = jnp.where(masks[1], pltpu.roll(row, width - dilation, 1), zeros)


def pairs(rows, dilation):
    covered, starts = set(), []
    for row in range(rows):
        if row not in covered:
            start = row if row + dilation < rows else row - dilation
            starts.append(start)
            covered |= {start, start + dilation}
    return starts


def window(stack, start, dilation, channels):
    parts = []
    for place in range(3):
        for tap in range(4):
            parts.append(stack[start + tap * dilation, place * channels : (place + 1) * channels, :])
    return jnp.concatenate(parts, axis=0)


def spread_conv(banded, slot, w_conv, layer, turned, row_offset):
    inner, channels = w_conv.shape[2], w_conv.shape[3]
    zeros = jnp.zeros((inner, channels), jnp.bfloat16)
    for col_tap in range(3):
        for second in range(2):
            parts = [zeros] * 4
            for row_tap in range(3):
                tap = col_tap * 3 + row_tap if turned else row_tap * 3 + col_tap
                parts[row_tap + second] = w_conv[layer, tap]
            top = row_offset + second * inner
            left = col_tap * 4 * channels
            banded[slot, top : top + inner, left : left + 4 * channels] = jnp.concatenate(parts, axis=1)


def spread_out(doubled, slot, w_out, layer):
    channels, inner = w_out.shape[1], w_out.shape[2]
    block = w_out[layer]
    zeros = jnp.zeros_like(block)
    doubled[slot] = jnp.concatenate(
        [jnp.concatenate([block, zeros], axis=1), jnp.concatenate([zeros, block], axis=1)], axis=0
    )


def as_column(row, copies):
    size = row.shape[1]
    across = lax.broadcasted_iota(jnp.int32, (size, size), 1)
    down = lax.broadcasted_iota(jnp.int32, (size, size), 0)
    spread = jnp.where(across == down, jnp.broadcast_to(row, (size, size)), 0.0)
    column = jnp.sum(spread, axis=1, keepdims=True)
    return jnp.concatenate([column] * copies, axis=0)


def run_block(rows, dilation, hidden_of, finish):
    waiting = []
    for start in pairs(rows, dilation):
        waiting.append((start, hidden_of(start)))
        if len(waiting) > LAG:
            finish(*waiting.pop(0))
    for item in waiting:
        finish(*item)


def conv_hidden(stack, start, dilation, channels, kernel, bias):
    inner = jnp.dot(kernel, window(stack, start, dilation, channels), preferred_element_type=jnp.float32)
    return jnp.maximum(inner + bias, 0.0).astype(jnp.bfloat16)


def two_rows(stack, start, dilation, channels, hidden, kernel, bias):
    blended = jnp.dot(kernel, hidden, preferred_element_type=jnp.float32)
    here = slice(channels, 2 * channels)
    residual = [stack[start + step * dilation, here, :].astype(jnp.float32) for step in (1, 2)]
    total = jnp.concatenate(residual, axis=0) + blended + bias
    return total[:channels], total[channels:]


def masked(row, row_id, map_rows):
    inside = jnp.logical_and(row_id >= 0, row_id < map_rows)
    return jnp.where(inside, row, jnp.zeros_like(row))


def fetch(copies):
    for copy in copies:
        copy.start()
    return copies


def section_one(place, own, across, beside, w_conv, bias_in, w_out, bias_out, out,
                shards, wide, first, second, conv, proj, banded, doubled, sems):
    channels, shard_rows, width = own.shape
    inner = w_out.shape[2]
    odd = place[0]
    blocks = width // LANES
    before = jnp.where(odd == 1, 0, 2)
    weights = fetch([
        pltpu.make_async_copy(w_conv.at[pl.ds(0, DEPTH)], conv, sems.at[0]),
        pltpu.make_async_copy(w_out.at[pl.ds(0, DEPTH)], proj, sems.at[1]),
    ])
    arrays = fetch([
        pltpu.make_async_copy(own, shards.at[1], sems.at[2]),
        pltpu.make_async_copy(beside, shards.at[before], sems.at[3]),
        pltpu.make_async_copy(across, shards.at[2 - before], sems.at[4]),
    ])
    for copy in weights:
        copy.wait()
    for layer in range(DEPTH):
        spread_conv(banded, layer, conv, layer, False, 0)
        spread_out(doubled, layer, proj, layer)
    masks = {dilation: column_masks(channels, width, dilation) for dilation in dilations}
    for copy in arrays:
        copy.wait()

    for slot in range(3):
        whole = shards[slot].astype(jnp.float32).reshape(channels * shard_rows, width)
        for block in range(blocks):
            wide[slot, block] = whole[:, block * LANES : (block + 1) * LANES]
    reach = sum(dilations)
    for index in range(shard_rows + 2 * reach):
        slot, line = divmod(index + shard_rows - reach, shard_rows)
        picked = pl.ds(line, channels, stride=shard_rows)
        row = jnp.concatenate([wide[slot, block, picked, :] for block in range(blocks)], axis=1)
        put_row(first, index, row.astype(jnp.bfloat16), dilations[0], masks[dilations[0]])

    source, target = first, second
    for layer, dilation in enumerate(dilations):
        reach = reach - dilation
        kernel, kernel_out = banded[layer], doubled[layer]
        bias = as_column(bias_in[layer : layer + 1, :], 2)
        bias_2 = as_column(bias_out[layer : layer + 1, :], 2)

        def hidden_of(start):
            return conv_hidden(source, start, dilation, channels, kernel, bias)

        def finish(start, hidden):
            rows = two_rows(source, start, dilation, channels, hidden, kernel_out, bias_2)
            for index, row in zip((start, start + dilation), rows):
                row = row.astype(jnp.bfloat16)
                if layer == DEPTH - 1:
                    out[index] = row
                    continue
                if index < reach or index >= reach + shard_rows:
                    row = masked(row, place[1] - reach + index, place[2])
                put_row(target, index, row, dilations[layer + 1], masks[dilations[layer + 1]])

        run_block(shard_rows + 2 * reach, dilation, hidden_of, finish)
        source, target = target, source


def section_two(place, own, across, beside, w_conv, bias_in, w_out, bias_out, out,
                shards, wide, first, plain, turned, plain_2, turned_2, conv, proj, banded, turned_banded, doubled, sems):
    shard_rows, channels, width = own.shape
    inner = w_out.shape[2]
    odd = place[0]
    blocks = width // LANES
    before = jnp.where(odd == 1, 0, 2)
    weights = fetch([
        pltpu.make_async_copy(w_conv.at[pl.ds(DEPTH, DEPTH + 1)], conv, sems.at[0]),
        pltpu.make_async_copy(w_out.at[pl.ds(DEPTH, DEPTH + 1)], proj, sems.at[1]),
    ])
    arrays = fetch([
        pltpu.make_async_copy(own, shards.at[1], sems.at[2]),
        pltpu.make_async_copy(beside, shards.at[before], sems.at[3]),
        pltpu.make_async_copy(across, shards.at[2 - before], sems.at[4]),
    ])
    for copy in weights:
        copy.wait()
    for layer in range(DEPTH + 1):
        spread_conv(banded, layer, conv, layer, False, 0)
        spread_out(doubled, layer, proj, layer)
        if layer < DEPTH:
            spread_conv(turned_banded, layer, conv, layer, True, 0)
    masks = {dilation: column_masks(channels, width, dilation) for dilation in dilations}
    for copy in arrays:
        copy.wait()

    reach = sum(dilations) + 1
    for index in range(shard_rows + 2 * reach):
        slot, line = divmod(index + shard_rows - reach, shard_rows)
        put_row(first, index, shards[slot, line], dilations[0], masks[dilations[0]])

    sources, targets = (first, first), (plain, turned)
    for layer, dilation in enumerate(dilations):
        reach = reach - dilation
        kernels = (banded[layer], turned_banded[layer])
        kernel_out = doubled[layer]
        bias = as_column(bias_in[DEPTH + layer : DEPTH + layer + 1, :], 2)
        bias_2 = as_column(bias_out[DEPTH + layer : DEPTH + layer + 1, :], 2)

        def hidden_of(start):
            if layer == 0:
                both = conv_hidden(
                    first, start, dilation, channels,
                    jnp.concatenate(kernels, axis=0), jnp.concatenate([bias, bias], axis=0),
                )
                return both[: 2 * inner], both[2 * inner :]
            return tuple(
                conv_hidden(source, start, dilation, channels, kernel, bias)
                for source, kernel in zip(sources, kernels)
            )

        def finish(start, hiddens):
            done = [
                two_rows(source, start, dilation, channels, hidden, kernel_out, bias_2)
                for source, hidden in zip(sources, hiddens)
            ]
            for step, index in enumerate((start, start + dilation)):
                rows = [rows[step].astype(jnp.bfloat16) for rows in done]
                following = dilations[(layer + 1) % DEPTH]
                places = targets
                if layer == DEPTH - 1:
                    rows = [((rows[0].astype(jnp.float32) + rows[1].astype(jnp.float32)) * 0.5).astype(jnp.bfloat16)]
                    places = (first,)
                for row, target in zip(rows, places):
                    if index < reach or index >= reach + shard_rows:
                        row = masked(row, place[1] - reach + index, place[2])
                    put_row(target, index, row, following, masks[following])

        run_block(shard_rows + 2 * reach, dilation, hidden_of, finish)
        sources, targets = targets, (plain_2, turned_2)

    kernel, kernel_out = banded[DEPTH], doubled[DEPTH]
    bias = as_column(bias_in[2 * DEPTH : 2 * DEPTH + 1, :], 2)
    bias_2 = as_column(bias_out[2 * DEPTH : 2 * DEPTH + 1, :], 2)
    dilation = dilations[0]

    def last_hidden(start):
        return conv_hidden(first, start, dilation, channels, kernel, bias)

    def last_finish(start, hidden):
        rows = two_rows(first, start, dilation, channels, hidden, kernel_out, bias_2)
        for index, row in zip((start, start + dilation), rows):
            for block in range(blocks):
                picked = pl.ds(index, channels, stride=shard_rows)
                wide[block, picked, :] = row[:, block * LANES : (block + 1) * LANES]

    run_block(shard_rows, dilation, last_hidden, last_finish)
    whole = jnp.concatenate([wide[block] for block in range(blocks)], axis=1)
    out[...] = whole.reshape(channels, shard_rows, width).astype(jnp.bfloat16)


def neighbours(array, axis):
    size = lax.axis_size(axis)
    inside = [(i, i ^ 1) for i in range(size)]
    edges = [(i, i + 1) for i in range(1, size - 1, 2)]
    edges = edges + [(j, i) for i, j in edges]
    across = lax.ppermute(array, axis, edges)
    beside = lax.ppermute(array, axis, inside)
    return across, beside


VMEM = pl.BlockSpec(memory_space=pltpu.VMEM)
SMEM = pl.BlockSpec(memory_space=pltpu.SMEM)
HBM = pl.BlockSpec(memory_space=pl.ANY)
PARAMS = pltpu.CompilerParams(vmem_limit_bytes=60 * 1024 * 1024)
IN_SPECS = [SMEM, HBM, HBM, HBM, HBM, VMEM, HBM, VMEM]


def call_one(channels, shard_rows, width, inner):
    reach = sum(dilations)

    def stack(rows):
        return pltpu.VMEM((rows, 3 * channels, width), jnp.bfloat16)

    return pl.pallas_call(
        section_one,
        out_shape=jax.ShapeDtypeStruct((shard_rows, channels, width), jnp.bfloat16),
        in_specs=IN_SPECS,
        out_specs=VMEM,
        scratch_shapes=[
            pltpu.VMEM((3, channels, shard_rows, width), jnp.bfloat16),
            pltpu.VMEM((3, width // LANES, channels * shard_rows, LANES), jnp.float32),
            stack(shard_rows + 2 * reach),
            stack(shard_rows + 2 * reach - 2 * dilations[0]),
            pltpu.VMEM((DEPTH, 9, inner, channels), jnp.bfloat16),
            pltpu.VMEM((DEPTH, channels, inner), jnp.bfloat16),
            pltpu.VMEM((DEPTH, 2 * inner, 12 * channels), jnp.bfloat16),
            pltpu.VMEM((DEPTH, 2 * channels, 2 * inner), jnp.bfloat16),
            pltpu.SemaphoreType.DMA((5,)),
        ],
        compiler_params=PARAMS,
        name="section_one",
    )


def call_two(channels, shard_rows, width, inner):
    reach = sum(dilations) + 1

    def stack(rows):
        return pltpu.VMEM((rows, 3 * channels, width), jnp.bfloat16)

    first = shard_rows + 2 * reach
    second = first - 2 * dilations[0]
    third = second - 2 * dilations[1]
    return pl.pallas_call(
        section_two,
        out_shape=jax.ShapeDtypeStruct((channels, shard_rows, width), jnp.bfloat16),
        in_specs=IN_SPECS,
        out_specs=VMEM,
        scratch_shapes=[
            pltpu.VMEM((3, shard_rows, channels, width), jnp.bfloat16),
            pltpu.VMEM((width // LANES, channels * shard_rows, LANES), jnp.float32),
            stack(first), stack(second), stack(second), stack(third), stack(third),
            pltpu.VMEM((DEPTH + 1, 9, inner, channels), jnp.bfloat16),
            pltpu.VMEM((DEPTH + 1, channels, inner), jnp.bfloat16),
            pltpu.VMEM((DEPTH + 1, 2 * inner, 12 * channels), jnp.bfloat16),
            pltpu.VMEM((DEPTH, 2 * inner, 12 * channels), jnp.bfloat16),
            pltpu.VMEM((DEPTH + 1, 2 * channels, 2 * inner), jnp.bfloat16),
            pltpu.SemaphoreType.DMA((5,)),
        ],
        compiler_params=PARAMS,
        name="section_two",
    )


def on_device(features, w_conv, bias_in, w_out, bias_out):
    channels, shard_rows, width = features.shape
    inner = w_conv.shape[2]
    size = lax.axis_size("row")
    device = lax.axis_index("row")
    place = jnp.stack([device % 2, device * shard_rows, jnp.int32(shard_rows * size)])
    weights = (w_conv, bias_in, w_out, bias_out)

    across, beside = neighbours(features, "row")
    field = call_one(channels, shard_rows, width, inner)(place, features, across, beside, *weights)

    tiles = field.reshape(shard_rows, channels, size, shard_rows).transpose(2, 3, 0, 1)
    tiles = tiles.reshape(size, shard_rows, shard_rows * channels)
    received = lax.all_to_all(tiles, "row", split_axis=0, concat_axis=0, tiled=True)
    flipped = received.reshape(size, shard_rows, shard_rows, channels).transpose(1, 3, 0, 2)
    flipped = flipped.reshape(shard_rows, channels, width)
    field = ((field.astype(jnp.float32) + flipped.astype(jnp.float32)) * 0.5).astype(jnp.bfloat16)

    across, beside = neighbours(field, "row")
    return call_two(channels, shard_rows, width, inner)(place, field, across, beside, *weights)


def solution(mesh):
    in_specs = (P("groups", "row", None), P(), P(), P(), P())
    out_specs = P("groups", "row", None)
    return jax.shard_map(
        on_device, mesh=mesh, in_specs=in_specs, out_specs=out_specs, check_vma=False
    )
```

```python
import jax
import jax.numpy as jnp
from jax import lax
from jax.experimental import pallas as pl
from jax.experimental.pallas import tpu as pltpu
from jax.sharding import PartitionSpec as P

SECTIONS = 2
DEPTH = 3

dilations = (1, 2, 4)
LANES = 128
LAG = 2
F32 = jnp.float32
BF16 = jnp.bfloat16


class Stage:
    def __init__(self, dilation, low, high, early_low, late, early):
        self.dilation, self.low, self.high, self.early_low = dilation, low, high, early_low
        self.late, self.early = late, early
        self.keep = ()


def cover(low, high, limit, dilation):
    covered, starts = set(), []
    for row in range(low, high + 1):
        if row in covered:
            continue
        start = row
        if row + dilation > limit and row - dilation >= low:
            start = row - dilation
        starts.append(start)
        covered |= {start, start + dilation}
    return starts, covered


def plan(shard_rows, steps):
    reach = sum(steps)
    ready = 0
    stages = [Stage(0, -reach, shard_rows - 1 + reach, 0, [], [])]
    for dilation in steps:
        reach, ready = reach - dilation, ready + dilation
        low, high = -reach, shard_rows - 1 + reach
        late, covered = cover(low, min(ready - 1, high), high, dilation)
        early_low = low
        while early_low in covered and early_low <= high:
            early_low += 1
        early = cover(early_low, high, high, dilation)[0] if early_low <= high else []
        stage = Stage(dilation, low, high, early_low, late, early)
        need = min(max(covered) + dilation, stages[-1].high)
        stages[-1].keep = tuple(range(stages[-1].early_low, need + 1))
        stages.append(stage)
    return stages


def column_masks(channels, width, dilation):
    column = lax.broadcasted_iota(jnp.int16, (channels, width), 1)
    return column >= jnp.int16(dilation), column < jnp.int16(width - dilation)


class Stack:
    def __init__(self, ref, base, top, dilation, masks):
        self.ref, self.base, self.top, self.dilation, self.masks = ref, base, top, dilation, masks[dilation]

    def put(self, row, value):
        channels, width = value.shape
        index = row - self.base
        zeros = jnp.zeros_like(value)
        self.ref[index, :channels, :] = jnp.where(self.masks[0], pltpu.roll(value, self.dilation, 1), zeros)
        self.ref[index, channels : 2 * channels, :] = value
        self.ref[index, 2 * channels :, :] = jnp.where(
            self.masks[1], pltpu.roll(value, width - self.dilation, 1), zeros
        )

    def get(self, row, place):
        channels = self.ref.shape[1] // 3
        index = min(row, self.top) - self.base
        return self.ref[index, place * channels : (place + 1) * channels, :]

    def window(self, start):
        return jnp.concatenate(
            [self.get(start + (tap - 1) * self.dilation, place) for place in range(3) for tap in range(4)], axis=0
        )


def spread_conv(banded, slot, w_conv, layer, turned, odd):
    inner, channels = w_conv.shape[2], w_conv.shape[3]
    zeros = jnp.zeros((inner, channels), BF16)
    for col_tap in range(3):
        taps = []
        for row_tap in range(3):
            line = jnp.where(odd == 1, 2 - row_tap, row_tap)
            taps.append(w_conv[layer, col_tap * 3 + line if turned else line * 3 + col_tap])
        left = col_tap * 4 * channels
        banded[slot, :inner, left : left + 4 * channels] = jnp.concatenate(taps + [zeros], axis=1)
        banded[slot, inner:, left : left + 4 * channels] = jnp.concatenate([zeros] + taps, axis=1)


def spread_out(doubled, slot, w_out, layer):
    block = w_out[layer].astype(F32).T.astype(BF16)
    zeros = jnp.zeros_like(block)
    doubled[slot] = jnp.concatenate(
        [jnp.concatenate([block, zeros], axis=1), jnp.concatenate([zeros, block], axis=1)], axis=0
    )


def as_column(row, copies):
    size = row.shape[1]
    across = lax.broadcasted_iota(jnp.int32, (size, size), 1)
    down = lax.broadcasted_iota(jnp.int32, (size, size), 0)
    spread = jnp.where(across == down, jnp.broadcast_to(row, (size, size)), 0.0)
    column = jnp.sum(spread, axis=1, keepdims=True)
    return jnp.concatenate([column] * copies, axis=0)


def run_block(starts, rows, dilation, hidden_of, finish):
    waiting, done = [], set()

    def complete(start, hidden):
        steps = []
        for step, row in enumerate((start, start + dilation)):
            if row in rows and row not in done:
                steps.append((step, row))
                done.add(row)
        finish(start, hidden, steps)

    for start in starts:
        waiting.append((start, hidden_of(start)))
        if len(waiting) > LAG:
            complete(*waiting.pop(0))
    for item in waiting:
        complete(*item)


def conv_hidden(stack, start, kernel, bias):
    inner = jnp.dot(kernel, stack.window(start), preferred_element_type=F32)
    return jnp.maximum(inner + bias, 0.0).astype(BF16)


def two_rows(stack, start, hidden, kernel, bias):
    blended = jnp.dot(kernel, hidden, preferred_element_type=F32)
    residual = [stack.get(start + step * stack.dilation, 1).astype(F32) for step in range(2)]
    total = jnp.concatenate(residual, axis=0) + blended + bias
    channels = total.shape[0] // 2
    return total[:channels], total[channels:]


def fetch(pairs, sems, first):
    copies = [pltpu.make_async_copy(source, target, sems.at[first + i]) for i, (source, target) in enumerate(pairs)]
    for copy in copies:
        copy.start()
    return copies


def position():
    device = lax.axis_index("row")
    size = lax.axis_size("row")
    odd = device % 2
    edge = jnp.logical_or(device == 0, device == size - 1)
    return odd, edge


def line_of(row, shard_rows, odd):
    inside = row % shard_rows
    return jnp.where(odd == 1, shard_rows - 1 - inside, inside)


class Weights:
    def __init__(self, refs, base, layers, turned_layers, odd):
        w_conv, bias_in, w_out, bias_out, conv, proj, banded, turned, doubled, sems = refs
        copies = fetch([(w_conv.at[pl.ds(base, layers)], conv), (w_out.at[pl.ds(base, layers)], proj)], sems, 0)
        for copy in copies:
            copy.wait()
        self.bias, self.bias_out = [], []
        for layer in range(layers):
            spread_conv(banded, layer, conv, layer, False, odd)
            if layer < turned_layers:
                spread_conv(turned, layer, conv, layer, True, odd)
            spread_out(doubled, layer, proj, layer)
            self.bias.append(as_column(bias_in[base + layer : base + layer + 1, :], 2))
            self.bias_out.append(as_column(bias_out[base + layer : base + layer + 1, :], 2))
        self.banded, self.turned, self.doubled = banded, turned, doubled


def block_one(weights, layer, stage, starts, rows, source, store):
    kernel, kernel_out = weights.banded[layer], weights.doubled[layer]

    def hidden_of(start):
        return conv_hidden(source, start, kernel, weights.bias[layer])

    def finish(start, hidden, steps):
        values = two_rows(source, start, hidden, kernel_out, weights.bias_out[layer])
        for step, row in steps:
            store(row, values[step])

    run_block(starts, rows, stage.dilation, hidden_of, finish)


def block_two(weights, layer, stage, starts, rows, sources, store):
    kernels = (weights.banded[layer], weights.turned[layer])
    kernel_out, bias = weights.doubled[layer], weights.bias[layer]

    def hidden_of(start):
        if sources[0] is sources[1]:
            both = conv_hidden(
                sources[0], start, jnp.concatenate(kernels, axis=0), jnp.concatenate([bias, bias], axis=0)
            )
            half = both.shape[0] // 2
            return both[:half], both[half:]
        return tuple(conv_hidden(source, start, kernel, bias) for source, kernel in zip(sources, kernels))

    def finish(start, hiddens, steps):
        values = [
            two_rows(source, start, hidden, kernel_out, weights.bias_out[layer])
            for source, hidden in zip(sources, hiddens)
        ]
        for step, row in steps:
            store(row, [value[step].astype(BF16) for value in values])

    run_block(starts, rows, stage.dilation, hidden_of, finish)


def mean_of(first, second):
    return ((first.astype(F32) + second.astype(F32)) * 0.5).astype(BF16)


def masks_for(channels, width):
    return {dilation: column_masks(channels, width, dilation) for dilation in dilations}


def rows_of_raw(shards, wide, slots, shard_rows, channels, width):
    for slot in slots:
        whole = shards[slot].astype(F32).reshape(channels * shard_rows, width)
        for block in range(width // LANES):
            wide[slot, block] = whole[:, block * LANES : (block + 1) * LANES]


def raw_row(wide, slot, line, shard_rows, channels, width):
    picked = pl.ds(line, channels, stride=shard_rows)
    parts = [wide[slot, block, picked, :] for block in range(width // LANES)]
    return jnp.concatenate(parts, axis=1).astype(BF16)


def one_early(own, beside, w_conv, bias_in, w_out, bias_out, keep,
              shards, wide, stack_0, stack_1, conv, proj, banded, turned, doubled, sems):
    channels, shard_rows, width = own.shape
    odd, _ = position()
    stages = plan(shard_rows, dilations)
    arrays = fetch([(own, shards.at[0]), (beside, shards.at[1])], sems, 2)
    weights = Weights(
        (w_conv, bias_in, w_out, bias_out, conv, proj, banded, turned, doubled, sems), 0, DEPTH - 1, 0, odd
    )
    masks = masks_for(channels, width)
    for copy in arrays:
        copy.wait()
    rows_of_raw(shards, wide, range(2), shard_rows, channels, width)
    place = 0
    refs = (stack_0, stack_1)
    source = Stack(refs[0], 0, stages[0].high, dilations[0], masks)
    for row in range(stages[0].high + 1):
        value = raw_row(wide, row // shard_rows, line_of(row, shard_rows, odd), shard_rows, channels, width)
        source.put(row, value)
        if row in stages[0].keep:
            keep[row] = value
    place = len(stages[0].keep)
    for layer in range(DEPTH - 1):
        stage = stages[layer + 1]
        last = layer == DEPTH - 2
        target = None
        if not last:
            target = Stack(refs[layer + 1], stage.early_low, stage.high, dilations[layer + 1], masks)

        def store(row, value):
            value = value.astype(BF16)
            if target is not None:
                target.put(row, value)
            if row in stage.keep:
                keep[place + stage.keep.index(row)] = value

        block_one(weights, layer, stage, stage.early, range(stage.early_low, stage.high + 1), source, store)
        place += len(stage.keep)
        source = target


def chunks_turned(values, lines):
    values = list(values)
    chunk = lax.broadcasted_iota(jnp.int32, values[0].shape, 1) // lines
    for bit in range(3):
        step = 1 << bit
        clear = ((chunk >> bit) & 1) == 0
        for index in range(8):
            if index & step:
                continue
            first, second = values[index], values[index + step]
            values[index] = jnp.where(clear, first, pltpu.roll(second, lines * step, 1))
            values[index + step] = jnp.where(clear, pltpu.roll(first, LANES - lines * step, 1), second)
    return values


def one_late(across, keep, w_conv, bias_in, w_out, bias_out, out, tiles,
             shards, wide, kept, stack_0, stack_1, stack_2, conv, proj, banded, turned, doubled, sems):
    channels, shard_rows, width = across.shape
    odd, edge = position()
    stages = plan(shard_rows, dilations)
    arrays = fetch([(across, shards.at[0]), (keep, kept)], sems, 2)
    weights = Weights(
        (w_conv, bias_in, w_out, bias_out, conv, proj, banded, turned, doubled, sems), 0, DEPTH, 0, odd
    )
    masks = masks_for(channels, width)
    for copy in arrays:
        copy.wait()
    rows_of_raw(shards, wide, range(1), shard_rows, channels, width)
    refs = (stack_0, stack_1, stack_2)
    place = 0
    source = None
    for layer in range(DEPTH + 1):
        stage = stages[layer]
        target = None
        if layer < DEPTH:
            target = Stack(refs[layer], stage.low, stage.keep[-1], dilations[layer], masks)
            for index, row in enumerate(stage.keep):
                target.put(row, kept[place + index])
            place += len(stage.keep)
        if layer == 0:
            for row in range(stage.low, 0):
                target.put(row, raw_row(wide, 0, line_of(row, shard_rows, odd), shard_rows, channels, width))
        else:
            def store(row, value):
                value = value.astype(BF16)
                if target is None:
                    out[line_of(row, shard_rows, odd)] = value
                    return
                if row < 0:
                    value = jnp.where(edge, jnp.zeros_like(value), value)
                target.put(row, value)

            block_one(weights, layer - 1, stage, stage.late, range(stage.low, stage.early_low), source, store)
        source = target

    half = channels // 2
    low_lanes = lax.broadcasted_iota(jnp.int32, (half, LANES), 1) < LANES // 2
    for block in range(width // LANES):
        values = [out[row, :, block * LANES : (block + 1) * LANES] for row in range(shard_rows)]
        for index, value in enumerate(chunks_turned(values, shard_rows)):
            top, bottom = value[:half], value[half:]
            device = block * 16 + index
            tiles[device] = jnp.where(low_lanes, top, pltpu.roll(bottom, LANES // 2, 1))
            tiles[device + 8] = jnp.where(low_lanes, pltpu.roll(top, LANES // 2, 1), bottom)


def symmetrize(received, field, out, tiles, own, sems):
    shard_rows, channels, width = field.shape
    copies = fetch([(received, tiles), (field, own)], sems, 0)
    half = channels // 2
    low_lanes = lax.broadcasted_iota(jnp.int32, (half, LANES), 1) < LANES // 2
    lane_in = lax.broadcasted_iota(jnp.int32, (LANES, LANES), 0)
    lane_out = lax.broadcasted_iota(jnp.int32, (LANES, LANES), 1)
    size = shard_rows
    turned = (lane_out // (size * size)) * (size * size) + (lane_out % size) * size + (lane_out // size) % size
    swap = jnp.where(lane_in == turned, 1.0, 0.0).astype(BF16)
    for copy in copies:
        copy.wait()
    for block in range(width // LANES):
        values = []
        for index in range(8):
            first, second = tiles[block * 16 + index], tiles[block * 16 + index + 8]
            top = jnp.where(low_lanes, first, pltpu.roll(second, LANES // 2, 1))
            bottom = jnp.where(low_lanes, pltpu.roll(first, LANES // 2, 1), second)
            values += [top, bottom]
        stacked = jnp.concatenate(values, axis=0)
        stacked = jnp.dot(stacked, swap, preferred_element_type=F32).astype(BF16)
        values = [stacked[index * channels : (index + 1) * channels] for index in range(8)]
        lanes = slice(block * LANES, (block + 1) * LANES)
        for row, value in enumerate(chunks_turned(values, shard_rows)):
            out[row, :, lanes] = mean_of(own[row, :, lanes], value)


def two_steps():
    return dilations + (dilations[0],)


def two_early(own, beside, w_conv, bias_in, w_out, bias_out, keep,
              shards, stack_0, plain_1, turned_1, plain_2, turned_2, conv, proj, banded, turned, doubled, sems):
    shard_rows, channels, width = own.shape
    odd, _ = position()
    steps = two_steps()
    stages = plan(shard_rows, steps)
    arrays = fetch([(own, shards.at[0]), (beside, shards.at[1])], sems, 2)
    weights = Weights(
        (w_conv, bias_in, w_out, bias_out, conv, proj, banded, turned, doubled, sems), DEPTH, DEPTH, DEPTH, odd
    )
    masks = masks_for(channels, width)
    for copy in arrays:
        copy.wait()
    source = Stack(stack_0, 0, stages[0].high, steps[0], masks)
    for row in range(stages[0].high + 1):
        value = shards[row // shard_rows, line_of(row, shard_rows, odd)]
        source.put(row, value)
        if row in stages[0].keep:
            keep[row] = value
    place = len(stages[0].keep)
    sources = (source, source)
    for layer, refs in enumerate(((plain_1, turned_1), (plain_2, turned_2), ())):
        stage = stages[layer + 1]
        targets = tuple(Stack(ref, stage.early_low, stage.high, steps[layer + 1], masks) for ref in refs)

        def store(row, values):
            for target, value in zip(targets, values):
                target.put(row, value)
            if row in stage.keep:
                index = stage.keep.index(row)
                if not targets:
                    values = [mean_of(*values)]
                for copy, value in enumerate(values):
                    keep[place + copy * len(stage.keep) + index] = value

        block_two(weights, layer, stage, stage.early, range(stage.early_low, stage.high + 1), sources, store)
        place += len(stage.keep) * max(len(refs), 1)
        sources = targets


def two_late(across, keep, w_conv, bias_in, w_out, bias_out, out,
             shards, wide, kept, stack_0, plain_1, turned_1, plain_2, turned_2, stack_3,
             conv, proj, banded, turned, doubled, sems):
    shard_rows, channels, width = across.shape
    odd, edge = position()
    steps = two_steps()
    stages = plan(shard_rows, steps)
    arrays = fetch([(across, shards), (keep, kept)], sems, 2)
    weights = Weights(
        (w_conv, bias_in, w_out, bias_out, conv, proj, banded, turned, doubled, sems), DEPTH, DEPTH + 1, DEPTH, odd
    )
    masks = masks_for(channels, width)
    for copy in arrays:
        copy.wait()
    place = 0
    sources = None
    for layer, refs in enumerate(((stack_0,), (plain_1, turned_1), (plain_2, turned_2), (stack_3,))):
        stage = stages[layer]
        targets = tuple(Stack(ref, stage.low, stage.keep[-1], steps[layer], masks) for ref in refs)
        for target in targets:
            for index, row in enumerate(stage.keep):
                target.put(row, kept[place + index])
            place += len(stage.keep)
        if layer == 0:
            for row in range(stage.low, 0):
                targets[0].put(row, shards[line_of(row, shard_rows, odd)])
            targets = targets * 2
        else:
            def store(row, values):
                if layer == DEPTH:
                    values = [mean_of(*values)]
                for target, value in zip(targets, values):
                    if row < 0:
                        value = jnp.where(edge, jnp.zeros_like(value), value)
                    target.put(row, value)

            block_two(weights, layer - 1, stage, stage.late, range(stage.low, stage.early_low), sources, store)
        sources = targets

    stage = stages[DEPTH + 1]

    def store_last(row, value):
        picked = pl.ds(line_of(row, shard_rows, odd), channels, stride=shard_rows)
        for block in range(width // LANES):
            wide[block, picked, :] = value[:, block * LANES : (block + 1) * LANES]

    block_one(weights, DEPTH, stage, stage.late, range(stage.low, stage.high + 1), sources[0], store_last)
    whole = jnp.concatenate([wide[block] for block in range(width // LANES)], axis=1)
    out[...] = whole.reshape(channels, shard_rows, width).astype(BF16)


VMEM = pl.BlockSpec(memory_space=pltpu.VMEM)
HBM = pl.BlockSpec(memory_space=pltpu.HBM)
WEIGHT_SPECS = [HBM, VMEM, HBM, VMEM]


class Calls:
    def __init__(self, channels, shard_rows, width, inner, size):
        self.channels, self.shard_rows, self.width, self.inner, self.size = channels, shard_rows, width, inner, size
        self.params = pltpu.CompilerParams(vmem_limit_bytes=(10 + 6 * width // LANES) * 1024 * 1024)
        self.one = plan(shard_rows, dilations)
        self.two = plan(shard_rows, two_steps())

    def stack(self, low, high):
        return pltpu.VMEM((max(high - low + 1, 1), 3 * self.channels, self.width), BF16)

    def early(self, stage):
        return self.stack(stage.early_low, stage.high)

    def late(self, stage):
        return self.stack(stage.low, stage.keep[-1])

    def rows(self, count):
        return (count, self.channels, self.width)

    def weights(self, layers):
        inner, channels = self.inner, self.channels
        return [
            pltpu.VMEM((layers, 9, inner, channels), BF16),
            pltpu.VMEM((layers, inner, channels), BF16),
            pltpu.VMEM((layers, 2 * inner, 12 * channels), BF16),
            pltpu.VMEM((layers, 2 * inner, 12 * channels), BF16),
            pltpu.VMEM((layers, 2 * channels, 2 * inner), BF16),
            pltpu.SemaphoreType.DMA((4,)),
        ]

    def raw(self, shards):
        channels, rows, width = self.channels, self.shard_rows, self.width
        return [
            pltpu.VMEM((shards, channels, rows, width), BF16),
            pltpu.VMEM((shards, width // LANES, channels * rows, LANES), F32),
        ]

    def call(self, body, in_specs, shapes, scratch):
        shapes = [jax.ShapeDtypeStruct(shape, BF16) for shape in shapes]
        single = len(shapes) == 1
        return pl.pallas_call(
            body,
            out_shape=shapes[0] if single else shapes,
            in_specs=in_specs,
            out_specs=VMEM if single else [VMEM] * len(shapes),
            scratch_shapes=scratch,
            compiler_params=self.params,
            name=body.__name__,
        )

    def one_early(self, *args):
        kept = sum(len(stage.keep) for stage in self.one)
        scratch = self.raw(2) + [self.early(self.one[0]), self.early(self.one[1])] + self.weights(DEPTH - 1)
        return self.call(one_early, [HBM, HBM] + WEIGHT_SPECS, [self.rows(kept)], scratch)(*args)

    def one_late(self, *args):
        kept = sum(len(stage.keep) for stage in self.one)
        scratch = self.raw(1) + [pltpu.VMEM(self.rows(kept), BF16)]
        scratch += [self.late(stage) for stage in self.one[:DEPTH]] + self.weights(DEPTH)
        shapes = [self.rows(self.shard_rows), (self.size, self.channels // 2, LANES)]
        return self.call(one_late, [HBM, HBM] + WEIGHT_SPECS, shapes, scratch)(*args)

    def symmetrize(self, *args):
        scratch = [
            pltpu.VMEM((self.size, self.channels // 2, LANES), BF16),
            pltpu.VMEM(self.rows(self.shard_rows), BF16),
            pltpu.SemaphoreType.DMA((2,)),
        ]
        return self.call(symmetrize, [HBM, HBM], [self.rows(self.shard_rows)], scratch)(*args)

    def kept_two(self):
        copies = (1, 2, 2, 1, 0)
        return self.rows(sum(count * len(stage.keep) for count, stage in zip(copies, self.two)))

    def two_early(self, *args):
        scratch = [pltpu.VMEM((2,) + self.rows(self.shard_rows), BF16)]
        scratch += [self.early(self.two[index]) for index in (0, 1, 1, 2, 2)] + self.weights(DEPTH)
        return self.call(two_early, [HBM, HBM] + WEIGHT_SPECS, [self.kept_two()], scratch)(*args)

    def two_late(self, *args):
        channels, rows, width = self.channels, self.shard_rows, self.width
        scratch = [
            pltpu.VMEM(self.rows(rows), BF16),
            pltpu.VMEM((width // LANES, channels * rows, LANES), F32),
            pltpu.VMEM(self.kept_two(), BF16),
        ]
        scratch += [self.late(self.two[index]) for index in (0, 1, 1, 2, 2, 3)] + self.weights(DEPTH + 1)
        return self.call(two_late, [HBM, HBM] + WEIGHT_SPECS, [(channels, rows, width)], scratch)(*args)


def neighbours(array, axis):
    size = lax.axis_size(axis)
    inside = [(i, i ^ 1) for i in range(size)]
    edges = [(i, i + 1) for i in range(1, size - 1, 2)]
    edges = edges + [(j, i) for i, j in edges]
    across = lax.ppermute(array, axis, edges)
    beside = lax.ppermute(array, axis, inside)
    return across, beside


def on_device(features, w_conv, bias_in, w_out, bias_out):
    channels, shard_rows, width = features.shape
    calls = Calls(channels, shard_rows, width, w_conv.shape[2], lax.axis_size("row"))
    weights = (w_conv, bias_in, w_out.transpose(0, 2, 1), bias_out)

    across, beside = neighbours(features, "row")
    keep = calls.one_early(features, beside, *weights)
    field, tiles = calls.one_late(across, keep, *weights)
    received = lax.all_to_all(tiles, "row", split_axis=0, concat_axis=0, tiled=True)
    field = calls.symmetrize(received, field)
    across, beside = neighbours(field, "row")
    keep = calls.two_early(field, beside, *weights)
    return calls.two_late(across, keep, *weights)


def solution(mesh):
    in_specs = (P("groups", "row", None), P(), P(), P(), P())
    out_specs = P("groups", "row", None)
    return jax.shard_map(
        on_device, mesh=mesh, in_specs=in_specs, out_specs=out_specs, check_vma=False
    )
```

```python
import jax
import jax.numpy as jnp
from jax import lax
from jax.experimental import pallas as pl
from jax.experimental.pallas import tpu as pltpu
from jax.sharding import PartitionSpec as P

SECTIONS = 2
DEPTH = 3

dilations = (1, 2, 4)
LANES = 128
LAG = 2
F32 = jnp.float32
BF16 = jnp.bfloat16


class Stage:
    def __init__(self, dilation, low, high, early_low, late, early):
        self.dilation, self.low, self.high, self.early_low = dilation, low, high, early_low
        self.late, self.early = late, early
        self.keep = ()


def cover(low, high, limit, dilation):
    covered, starts = set(), []
    for row in range(low, high + 1):
        if row in covered:
            continue
        start = row
        if row + dilation > limit and row - dilation >= low:
            start = row - dilation
        starts.append(start)
        covered |= {start, start + dilation}
    return starts, covered


def plan(shard_rows, steps):
    reach = sum(steps)
    ready = 0
    stages = [Stage(0, -reach, shard_rows - 1 + reach, 0, [], [])]
    for dilation in steps:
        reach, ready = reach - dilation, ready + dilation
        low, high = -reach, shard_rows - 1 + reach
        late, covered = cover(low, min(ready - 1, high), high, dilation)
        early_low = low
        while early_low in covered and early_low <= high:
            early_low += 1
        early = cover(early_low, high, high, dilation)[0] if early_low <= high else []
        stage = Stage(dilation, low, high, early_low, late, early)
        need = min(max(covered) + dilation, stages[-1].high)
        stages[-1].keep = tuple(range(stages[-1].early_low, need + 1))
        stages.append(stage)
    return stages


def column_masks(channels, width, dilation):
    column = lax.broadcasted_iota(jnp.int16, (channels, width), 1)
    return column >= jnp.int16(dilation), column < jnp.int16(width - dilation)


class Stack:
    def __init__(self, parts, top, dilation, masks):
        self.parts, self.top, self.dilation, self.masks = parts, top, dilation, masks[dilation]

    def find(self, row):
        for ref, base in self.parts:
            if row >= base:
                return ref, row - base
        raise ValueError(row)

    def put(self, row, value):
        channels, width = value.shape
        ref, index = self.find(row)
        zeros = jnp.zeros_like(value)
        ref[index, :channels, :] = jnp.where(self.masks[0], pltpu.roll(value, self.dilation, 1), zeros)
        ref[index, channels : 2 * channels, :] = value
        ref[index, 2 * channels :, :] = jnp.where(
            self.masks[1], pltpu.roll(value, width - self.dilation, 1), zeros
        )

    def get(self, row, place):
        ref, index = self.find(min(row, self.top))
        channels = ref.shape[1] // 3
        return ref[index, place * channels : (place + 1) * channels, :]

    def window(self, start):
        return jnp.concatenate(
            [self.get(start + (tap - 1) * self.dilation, place) for place in range(3) for tap in range(4)], axis=0
        )


def spread_conv(banded, slot, w_conv, layer, turned, odd):
    inner, channels = w_conv.shape[2], w_conv.shape[3]
    zeros = jnp.zeros((inner, channels), BF16)
    for col_tap in range(3):
        taps = []
        for row_tap in range(3):
            line = jnp.where(odd == 1, 2 - row_tap, row_tap)
            taps.append(w_conv[layer, col_tap * 3 + line if turned else line * 3 + col_tap])
        left = col_tap * 4 * channels
        banded[slot, :inner, left : left + 4 * channels] = jnp.concatenate(taps + [zeros], axis=1)
        banded[slot, inner:, left : left + 4 * channels] = jnp.concatenate([zeros] + taps, axis=1)


def spread_out(doubled, slot, w_out, layer):
    block = w_out[layer].astype(F32).T.astype(BF16)
    zeros = jnp.zeros_like(block)
    doubled[slot] = jnp.concatenate(
        [jnp.concatenate([block, zeros], axis=1), jnp.concatenate([zeros, block], axis=1)], axis=0
    )


def as_column(row, copies):
    size = row.shape[1]
    across = lax.broadcasted_iota(jnp.int32, (size, size), 1)
    down = lax.broadcasted_iota(jnp.int32, (size, size), 0)
    spread = jnp.where(across == down, jnp.broadcast_to(row, (size, size)), 0.0)
    column = jnp.sum(spread, axis=1, keepdims=True)
    return jnp.concatenate([column] * copies, axis=0)


def run_block(starts, rows, dilation, hidden_of, finish):
    waiting, done = [], set()

    def complete(start, hidden):
        steps = []
        for step, row in enumerate((start, start + dilation)):
            if row in rows and row not in done:
                steps.append((step, row))
                done.add(row)
        finish(start, hidden, steps)

    for start in starts:
        waiting.append((start, hidden_of(start)))
        if len(waiting) > LAG:
            complete(*waiting.pop(0))
    for item in waiting:
        complete(*item)


def conv_hidden(stack, start, kernel, bias):
    inner = jnp.dot(kernel, stack.window(start), preferred_element_type=F32)
    return jnp.maximum(inner + bias, 0.0).astype(BF16)


def two_rows(stack, start, hidden, kernel, bias):
    blended = jnp.dot(kernel, hidden, preferred_element_type=F32)
    residual = [stack.get(start + step * stack.dilation, 1).astype(F32) for step in range(2)]
    total = jnp.concatenate(residual, axis=0) + blended + bias
    channels = total.shape[0] // 2
    return total[:channels], total[channels:]


def fetch(pairs, sems):
    copies = [pltpu.make_async_copy(source, target, sems.at[i]) for i, (source, target) in enumerate(pairs)]
    for copy in copies:
        copy.start()
    return copies


def position():
    device = lax.axis_index("row")
    size = lax.axis_size("row")
    odd = device % 2
    edge = jnp.logical_or(device == 0, device == size - 1)
    return odd, edge


def line_of(row, shard_rows, odd):
    inside = row % shard_rows
    return jnp.where(odd == 1, shard_rows - 1 - inside, inside)


def prepare(w_conv, bias_in, w_out, bias_out, banded, turned, doubled, bias, bias_last, conv, proj, sems):
    odd, _ = position()
    for copy in fetch([(w_conv, conv), (w_out, proj)], sems):
        copy.wait()
    layers = w_conv.shape[0]
    for layer in range(layers):
        spread_conv(banded, layer, conv, layer, False, odd)
        spread_out(doubled, layer, proj, layer)
        bias[layer] = jnp.broadcast_to(as_column(bias_in[layer : layer + 1, :], 2), bias.shape[1:])
        bias_last[layer] = jnp.broadcast_to(as_column(bias_out[layer : layer + 1, :], 2), bias_last.shape[1:])
    for layer in range(turned.shape[0]):
        spread_conv(turned, layer, conv, layers - 1 - DEPTH + layer, True, odd)


class Weights:
    def __init__(self, refs, base, width):
        self.refs, self.base, self.blocks = refs, base, width // LANES

    def conv(self, layer):
        return self.refs[0][self.base + layer]

    def conv_turned(self, layer):
        return self.refs[1][layer]

    def out(self, layer):
        return self.refs[2][self.base + layer]

    def bias(self, layer):
        return jnp.concatenate([self.refs[3][self.base + layer]] * self.blocks, axis=1)

    def bias_out(self, layer):
        return jnp.concatenate([self.refs[4][self.base + layer]] * self.blocks, axis=1)


def block_one(weights, layer, stage, starts, rows, source, store):
    kernel, kernel_out = weights.conv(layer), weights.out(layer)
    bias, bias_out = weights.bias(layer), weights.bias_out(layer)

    def hidden_of(start):
        return conv_hidden(source, start, kernel, bias)

    def finish(start, hidden, steps):
        values = two_rows(source, start, hidden, kernel_out, bias_out)
        for step, row in steps:
            store(row, values[step])

    run_block(starts, rows, stage.dilation, hidden_of, finish)


def block_two(weights, layer, stage, starts, rows, sources, store):
    kernels = (weights.conv(layer), weights.conv_turned(layer))
    kernel_out, bias, bias_out = weights.out(layer), weights.bias(layer), weights.bias_out(layer)

    def hidden_of(start):
        if sources[0] is sources[1]:
            both = conv_hidden(
                sources[0], start, jnp.concatenate(kernels, axis=0), jnp.concatenate([bias, bias], axis=0)
            )
            half = both.shape[0] // 2
            return both[:half], both[half:]
        return tuple(conv_hidden(source, start, kernel, bias) for source, kernel in zip(sources, kernels))

    def finish(start, hiddens, steps):
        values = [
            two_rows(source, start, hidden, kernel_out, bias_out)
            for source, hidden in zip(sources, hiddens)
        ]
        for step, row in steps:
            store(row, [value[step].astype(BF16) for value in values])

    run_block(starts, rows, stage.dilation, hidden_of, finish)


def mean_of(first, second):
    return ((first.astype(F32) + second.astype(F32)) * 0.5).astype(BF16)


def masks_for(channels, width):
    return {dilation: column_masks(channels, width, dilation) for dilation in dilations}


def rows_of_raw(shards, wide, shard_rows, channels, width):
    for slot, shard in enumerate(shards):
        whole = shard[...].astype(F32).reshape(channels * shard_rows, width)
        for block in range(width // LANES):
            wide[slot, block] = whole[:, block * LANES : (block + 1) * LANES]


def raw_row(wide, slot, line, shard_rows, channels, width):
    picked = pl.ds(line, channels, stride=shard_rows)
    parts = [wide[slot, block, picked, :] for block in range(width // LANES)]
    return jnp.concatenate(parts, axis=1).astype(BF16)


def one_early(own, beside, *refs):
    weight_refs, (stack_0, stack_1, stack_2, wide) = refs[:5], refs[5:]
    channels, shard_rows, width = own.shape
    odd, _ = position()
    stages = plan(shard_rows, dilations)
    weights = Weights(weight_refs, 0, width)
    masks = masks_for(channels, width)
    rows_of_raw((own, beside), wide, shard_rows, channels, width)
    stacks = [
        Stack([(ref, stage.early_low)], stage.high, dilation, masks)
        for ref, stage, dilation in zip((stack_0, stack_1, stack_2), stages, dilations)
    ]
    for row in range(stages[0].high + 1):
        line = line_of(row, shard_rows, odd)
        stacks[0].put(row, raw_row(wide, row // shard_rows, line, shard_rows, channels, width))
    for layer in range(DEPTH - 1):
        stage = stages[layer + 1]

        def store(row, value):
            stacks[layer + 1].put(row, value.astype(BF16))

        block_one(weights, layer, stage, stage.early, range(stage.early_low, stage.high + 1), stacks[layer], store)


def chunks_turned(values, lines):
    values = list(values)
    chunk = lax.broadcasted_iota(jnp.int32, values[0].shape, 1) // lines
    for bit in range(3):
        step = 1 << bit
        clear = ((chunk >> bit) & 1) == 0
        for index in range(8):
            if index & step:
                continue
            first, second = values[index], values[index + step]
            values[index] = jnp.where(clear, first, pltpu.roll(second, lines * step, 1))
            values[index + step] = jnp.where(clear, pltpu.roll(first, LANES - lines * step, 1), second)
    return values


def one_late(across, kept_0, kept_1, kept_2, *refs):
    weight_refs, (out, tiles, stack_0, stack_1, stack_2, wide) = refs[:5], refs[5:]
    channels, shard_rows, width = across.shape
    odd, edge = position()
    stages = plan(shard_rows, dilations)
    weights = Weights(weight_refs, 0, width)
    masks = masks_for(channels, width)
    rows_of_raw((across,), wide, shard_rows, channels, width)
    stacks = [
        Stack([(early, stage.early_low), (late, stage.low)], stage.high, dilation, masks)
        for early, late, stage, dilation in zip(
            (kept_0, kept_1, kept_2), (stack_0, stack_1, stack_2), stages, dilations
        )
    ]
    for row in range(stages[0].low, 0):
        stacks[0].put(row, raw_row(wide, 0, line_of(row, shard_rows, odd), shard_rows, channels, width))
    for layer in range(DEPTH):
        stage = stages[layer + 1]

        def store(row, value):
            value = value.astype(BF16)
            if layer == DEPTH - 1:
                out[line_of(row, shard_rows, odd)] = value
                return
            if row < 0:
                value = jnp.where(edge, jnp.zeros_like(value), value)
            stacks[layer + 1].put(row, value)

        block_one(weights, layer, stage, stage.late, range(stage.low, stage.early_low), stacks[layer], store)

    half = channels // 2
    low_lanes = lax.broadcasted_iota(jnp.int32, (half, LANES), 1) < LANES // 2
    for block in range(width // LANES):
        values = [out[row, :, block * LANES : (block + 1) * LANES] for row in range(shard_rows)]
        for index, value in enumerate(chunks_turned(values, shard_rows)):
            top, bottom = value[:half], value[half:]
            device = block * 16 + index
            tiles[device] = jnp.where(low_lanes, top, pltpu.roll(bottom, LANES // 2, 1))
            tiles[device + 8] = jnp.where(low_lanes, pltpu.roll(top, LANES // 2, 1), bottom)


def symmetrize(tiles, own, out):
    shard_rows, channels, width = own.shape
    half = channels // 2
    low_lanes = lax.broadcasted_iota(jnp.int32, (half, LANES), 1) < LANES // 2
    lane_in = lax.broadcasted_iota(jnp.int32, (LANES, LANES), 0)
    lane_out = lax.broadcasted_iota(jnp.int32, (LANES, LANES), 1)
    size = shard_rows
    turned = (lane_out // (size * size)) * (size * size) + (lane_out % size) * size + (lane_out // size) % size
    swap = jnp.where(lane_in == turned, 1.0, 0.0).astype(BF16)
    for block in range(width // LANES):
        values = []
        for index in range(8):
            first, second = tiles[block * 16 + index], tiles[block * 16 + index + 8]
            top = jnp.where(low_lanes, first, pltpu.roll(second, LANES // 2, 1))
            bottom = jnp.where(low_lanes, pltpu.roll(first, LANES // 2, 1), second)
            values += [top, bottom]
        stacked = jnp.concatenate(values, axis=0)
        stacked = jnp.dot(stacked, swap, preferred_element_type=F32).astype(BF16)
        values = [stacked[index * channels : (index + 1) * channels] for index in range(8)]
        lanes = slice(block * LANES, (block + 1) * LANES)
        for row, value in enumerate(chunks_turned(values, shard_rows)):
            out[row, :, lanes] = mean_of(own[row, :, lanes], value)


def two_steps():
    return dilations + (dilations[0],)


LAYERS_OF = (0, 1, 1, 2, 2, 3)


def two_early(own, beside, *refs):
    weight_refs, stack_refs = refs[:5], refs[5:]
    shard_rows, channels, width = own.shape
    odd, _ = position()
    steps = two_steps()
    stages = plan(shard_rows, steps)
    weights = Weights(weight_refs, DEPTH, width)
    masks = masks_for(channels, width)
    stacks = [[], [], [], []]
    for ref, index in zip(stack_refs, LAYERS_OF):
        stacks[index].append(Stack([(ref, stages[index].early_low)], stages[index].high, steps[index], masks))
    for row in range(stages[0].high + 1):
        shard = (own, beside)[row // shard_rows]
        stacks[0][0].put(row, shard[line_of(row, shard_rows, odd)])
    sources = stacks[0] * 2
    for layer in range(DEPTH):
        stage = stages[layer + 1]

        def store(row, values):
            if layer == DEPTH - 1:
                values = [mean_of(*values)]
            for target, value in zip(stacks[layer + 1], values):
                target.put(row, value)

        block_two(weights, layer, stage, stage.early, range(stage.early_low, stage.high + 1), sources, store)
        sources = stacks[layer + 1]


def two_late(across, *refs):
    kept_refs, weight_refs, out, stack_refs, wide = refs[:6], refs[6:11], refs[11], refs[12:18], refs[18]
    shard_rows, channels, width = across.shape
    odd, edge = position()
    steps = two_steps()
    stages = plan(shard_rows, steps)
    weights = Weights(weight_refs, DEPTH, width)
    masks = masks_for(channels, width)
    stacks = [[], [], [], []]
    for early, late, index in zip(kept_refs, stack_refs, LAYERS_OF):
        stage = stages[index]
        stacks[index].append(Stack([(early, stage.early_low), (late, stage.low)], stage.high, steps[index], masks))
    for row in range(stages[0].low, 0):
        stacks[0][0].put(row, across[line_of(row, shard_rows, odd)])
    sources = stacks[0] * 2
    for layer in range(DEPTH):
        stage = stages[layer + 1]

        def store(row, values):
            if layer == DEPTH - 1:
                values = [mean_of(*values)]
            for target, value in zip(stacks[layer + 1], values):
                if row < 0:
                    value = jnp.where(edge, jnp.zeros_like(value), value)
                target.put(row, value)

        block_two(weights, layer, stage, stage.late, range(stage.low, stage.early_low), sources, store)
        sources = stacks[layer + 1]

    stage = stages[DEPTH + 1]

    def store_last(row, value):
        picked = pl.ds(line_of(row, shard_rows, odd), channels, stride=shard_rows)
        for block in range(width // LANES):
            wide[block, picked, :] = value[:, block * LANES : (block + 1) * LANES]

    block_one(weights, DEPTH, stage, stage.late, range(stage.low, stage.high + 1), sources[0], store_last)
    whole = jnp.concatenate([wide[block] for block in range(width // LANES)], axis=1)
    out[...] = whole.reshape(channels, shard_rows, width).astype(BF16)


VMEM = pl.BlockSpec(memory_space=pltpu.VMEM)
ANY = pl.BlockSpec(memory_space=pl.ANY)


class Calls:
    def __init__(self, channels, shard_rows, width, inner, size):
        self.channels, self.shard_rows, self.width, self.inner, self.size = channels, shard_rows, width, inner, size
        self.one = plan(shard_rows, dilations)
        self.two = plan(shard_rows, two_steps())

    def stack(self, low, high):
        return (max(high - low + 1, 1), 3 * self.channels, self.width)

    def early(self, stage):
        return self.stack(stage.early_low, stage.high)

    def late(self, stage):
        return pltpu.VMEM(self.stack(stage.low, stage.early_low - 1), BF16)

    def wide(self, *shards):
        return pltpu.VMEM(shards + (self.width // LANES, self.channels * self.shard_rows, LANES), F32)

    def call(self, body, args, shapes, scratch, specs=None):
        shapes = [shape if isinstance(shape, jax.ShapeDtypeStruct) else jax.ShapeDtypeStruct(shape, BF16) for shape in shapes]
        single = len(shapes) == 1
        return pl.pallas_call(
            body,
            out_shape=shapes[0] if single else shapes,
            in_specs=specs or [VMEM] * len(args),
            out_specs=VMEM if single else [VMEM] * len(shapes),
            scratch_shapes=scratch,
            compiler_params=pltpu.CompilerParams(vmem_limit_bytes=(10 + 6 * self.width // LANES) * 1024 * 1024),
            name=body.__name__,
        )(*args)

    def prepare(self, w_conv, bias_in, w_out, bias_out):
        layers, inner, channels = w_conv.shape[0], self.inner, self.channels
        shapes = [
            (layers, 2 * inner, 12 * channels),
            (DEPTH, 2 * inner, 12 * channels),
            (layers, 2 * channels, 2 * inner),
            jax.ShapeDtypeStruct((layers, 2 * inner, LANES), F32),
            jax.ShapeDtypeStruct((layers, 2 * channels, LANES), F32),
        ]
        scratch = [
            pltpu.VMEM(w_conv.shape, BF16), pltpu.VMEM(w_out.shape, BF16), pltpu.SemaphoreType.DMA((2,)),
        ]
        return self.call(
            prepare, (w_conv, bias_in, w_out, bias_out), shapes, scratch, [ANY, VMEM, ANY, VMEM]
        )

    def one_early(self, *args):
        return self.call(one_early, args, [self.early(stage) for stage in self.one[:DEPTH]], [self.wide(2)])

    def one_late(self, *args):
        shapes = [(self.shard_rows, self.channels, self.width), (self.size, self.channels // 2, LANES)]
        return self.call(one_late, args, shapes, [self.late(stage) for stage in self.one[:DEPTH]] + [self.wide(1)])

    def symmetrize(self, *args):
        return self.call(symmetrize, args, [(self.shard_rows, self.channels, self.width)], [])

    def two_early(self, *args):
        return self.call(two_early, args, [self.early(self.two[index]) for index in LAYERS_OF], [])

    def two_late(self, *args):
        scratch = [self.late(self.two[index]) for index in LAYERS_OF] + [self.wide()]
        return self.call(two_late, args, [(self.channels, self.shard_rows, self.width)], scratch)


def neighbours(array, axis):
    size = lax.axis_size(axis)
    inside = [(i, i ^ 1) for i in range(size)]
    edges = [(i, i + 1) for i in range(1, size - 1, 2)]
    edges = edges + [(j, i) for i, j in edges]
    across = lax.ppermute(array, axis, edges)
    beside = lax.ppermute(array, axis, inside)
    return across, beside


def on_device(features, w_conv, bias_in, w_out, bias_out):
    channels, shard_rows, width = features.shape
    calls = Calls(channels, shard_rows, width, w_conv.shape[2], lax.axis_size("row"))
    across, beside = neighbours(features, "row")
    weights = calls.prepare(w_conv, bias_in, w_out.transpose(0, 2, 1), bias_out)
    kept = calls.one_early(features, beside, *weights)
    field, tiles = calls.one_late(across, *kept, *weights)
    received = lax.all_to_all(tiles, "row", split_axis=0, concat_axis=0, tiled=True)
    field = calls.symmetrize(received, field)
    across, beside = neighbours(field, "row")
    kept = calls.two_early(field, beside, *weights)
    return calls.two_late(across, *kept, *weights)


def solution(mesh):
    in_specs = (P("groups", "row", None), P(), P(), P(), P())
    out_specs = P("groups", "row", None)
    return jax.shard_map(
        on_device, mesh=mesh, in_specs=in_specs, out_specs=out_specs, check_vma=False
    )
```

```python
import jax
import jax.numpy as jnp
from jax import lax
from jax.experimental import pallas as pl
from jax.experimental.pallas import tpu as pltpu
from jax.sharding import PartitionSpec as P

SECTIONS = 2
DEPTH = 3

dilations = (1, 2, 4)
LANES = 128
LAG = 2
F32 = jnp.float32
BF16 = jnp.bfloat16


class Stage:
    def __init__(self, dilation, low, high, early_low, late, early):
        self.dilation, self.low, self.high, self.early_low = dilation, low, high, early_low
        self.late, self.early = late, early
        self.keep = ()


def cover(low, high, limit, dilation):
    covered, starts = set(), []
    for row in range(low, high + 1):
        if row in covered:
            continue
        start = row
        if row + dilation > limit and row - dilation >= low:
            start = row - dilation
        starts.append(start)
        covered |= {start, start + dilation}
    return starts, covered


def plan(shard_rows, steps):
    reach = sum(steps)
    ready = 0
    stages = [Stage(0, -reach, shard_rows - 1 + reach, 0, [], [])]
    for dilation in steps:
        reach, ready = reach - dilation, ready + dilation
        low, high = -reach, shard_rows - 1 + reach
        late, covered = cover(low, min(ready - 1, high), high, dilation)
        early_low = low
        while early_low in covered and early_low <= high:
            early_low += 1
        early = cover(early_low, high, high, dilation)[0] if early_low <= high else []
        stage = Stage(dilation, low, high, early_low, late, early)
        need = min(max(covered) + dilation, stages[-1].high)
        stages[-1].keep = tuple(range(stages[-1].early_low, need + 1))
        stages.append(stage)
    return stages


def column_masks(channels, width, dilation):
    column = lax.broadcasted_iota(jnp.int16, (channels, width), 1)
    return column >= jnp.int16(dilation), column < jnp.int16(width - dilation)


class Stack:
    def __init__(self, parts, top, dilation, masks):
        self.parts, self.top, self.dilation, self.masks = parts, top, dilation, masks[dilation]

    def find(self, row):
        for ref, base in self.parts:
            if row >= base:
                return ref, row - base
        raise ValueError(row)

    def put(self, row, value):
        channels, width = value.shape
        ref, index = self.find(row)
        zeros = jnp.zeros_like(value)
        ref[index, :channels, :] = jnp.where(self.masks[0], pltpu.roll(value, self.dilation, 1), zeros)
        ref[index, channels : 2 * channels, :] = value
        ref[index, 2 * channels :, :] = jnp.where(
            self.masks[1], pltpu.roll(value, width - self.dilation, 1), zeros
        )

    def get(self, row, place):
        ref, index = self.find(min(row, self.top))
        channels = ref.shape[1] // 3
        return ref[index, place * channels : (place + 1) * channels, :]

    def window(self, start):
        return jnp.concatenate(
            [self.get(start + (tap - 1) * self.dilation, place) for place in range(3) for tap in range(4)], axis=0
        )


def spread_conv(banded, slot, w_conv, layer, turned, odd):
    inner, channels = w_conv.shape[2], w_conv.shape[3]
    zeros = jnp.zeros((inner, channels), BF16)
    for col_tap in range(3):
        taps = []
        for row_tap in range(3):
            line = jnp.where(odd == 1, 2 - row_tap, row_tap)
            taps.append(w_conv[layer, col_tap * 3 + line if turned else line * 3 + col_tap])
        left = col_tap * 4 * channels
        banded[slot, :inner, left : left + 4 * channels] = jnp.concatenate(taps + [zeros], axis=1)
        banded[slot, inner:, left : left + 4 * channels] = jnp.concatenate([zeros] + taps, axis=1)


def spread_out(doubled, slot, w_out, layer):
    block = w_out[layer].astype(F32).T.astype(BF16)
    zeros = jnp.zeros_like(block)
    doubled[slot] = jnp.concatenate(
        [jnp.concatenate([block, zeros], axis=1), jnp.concatenate([zeros, block], axis=1)], axis=0
    )


def as_column(row, copies):
    size = row.shape[1]
    across = lax.broadcasted_iota(jnp.int32, (size, size), 1)
    down = lax.broadcasted_iota(jnp.int32, (size, size), 0)
    spread = jnp.where(across == down, jnp.broadcast_to(row, (size, size)), 0.0)
    column = jnp.sum(spread, axis=1, keepdims=True)
    return jnp.concatenate([column] * copies, axis=0)


def run_block(starts, rows, dilation, hidden_of, finish):
    waiting, done = [], set()

    def complete(start, hidden):
        steps = []
        for step, row in enumerate((start, start + dilation)):
            if row in rows and row not in done:
                steps.append((step, row))
                done.add(row)
        finish(start, hidden, steps)

    for start in starts:
        waiting.append((start, hidden_of(start)))
        if len(waiting) > LAG:
            complete(*waiting.pop(0))
    for item in waiting:
        complete(*item)


def conv_hidden(stack, start, kernel, bias):
    inner = jnp.dot(kernel, stack.window(start), preferred_element_type=F32)
    return jnp.maximum(inner + bias, 0.0).astype(BF16)


def two_rows(stack, start, hidden, kernel, bias):
    blended = jnp.dot(kernel, hidden, preferred_element_type=F32)
    residual = [stack.get(start + step * stack.dilation, 1).astype(F32) for step in range(2)]
    total = jnp.concatenate(residual, axis=0) + blended + bias
    channels = total.shape[0] // 2
    return total[:channels], total[channels:]


def fetch(pairs, sems):
    copies = [pltpu.make_async_copy(source, target, sems.at[i]) for i, (source, target) in enumerate(pairs)]
    for copy in copies:
        copy.start()
    return copies


def position():
    device = lax.axis_index("row")
    size = lax.axis_size("row")
    odd = device % 2
    edge = jnp.logical_or(device == 0, device == size - 1)
    return odd, edge


def line_of(row, shard_rows, odd):
    inside = row % shard_rows
    return jnp.where(odd == 1, shard_rows - 1 - inside, inside)


def prepare(w_conv, bias_in, w_out, bias_out, banded, turned, doubled, bias, bias_last, conv, proj, sems):
    odd, _ = position()
    for copy in fetch([(w_conv, conv), (w_out, proj)], sems):
        copy.wait()
    layers = w_conv.shape[0]
    for layer in range(layers):
        spread_conv(banded, layer, conv, layer, False, odd)
        spread_out(doubled, layer, proj, layer)
        bias[layer] = jnp.broadcast_to(as_column(bias_in[layer : layer + 1, :], 2), bias.shape[1:])
        bias_last[layer] = jnp.broadcast_to(as_column(bias_out[layer : layer + 1, :], 2), bias_last.shape[1:])
    for layer in range(turned.shape[0]):
        spread_conv(turned, layer, conv, layers - 1 - DEPTH + layer, True, odd)


class Weights:
    def __init__(self, refs, base, width):
        self.refs, self.base, self.blocks = refs, base, width // LANES

    def conv(self, layer):
        return self.refs[0][self.base + layer]

    def conv_turned(self, layer):
        return self.refs[1][layer]

    def out(self, layer):
        return self.refs[2][self.base + layer]

    def bias(self, layer):
        return jnp.concatenate([self.refs[3][self.base + layer]] * self.blocks, axis=1)

    def bias_out(self, layer):
        return jnp.concatenate([self.refs[4][self.base + layer]] * self.blocks, axis=1)


def block_one(weights, layer, stage, starts, rows, source, store):
    kernel, kernel_out = weights.conv(layer), weights.out(layer)
    bias, bias_out = weights.bias(layer), weights.bias_out(layer)

    def hidden_of(start):
        return conv_hidden(source, start, kernel, bias)

    def finish(start, hidden, steps):
        values = two_rows(source, start, hidden, kernel_out, bias_out)
        for step, row in steps:
            store(row, values[step])

    run_block(starts, rows, stage.dilation, hidden_of, finish)


def block_two(weights, layer, stage, starts, rows, sources, store):
    kernels = (weights.conv(layer), weights.conv_turned(layer))
    kernel_out, bias, bias_out = weights.out(layer), weights.bias(layer), weights.bias_out(layer)

    def hidden_of(start):
        if sources[0] is sources[1]:
            both = conv_hidden(
                sources[0], start, jnp.concatenate(kernels, axis=0), jnp.concatenate([bias, bias], axis=0)
            )
            half = both.shape[0] // 2
            return both[:half], both[half:]
        return tuple(conv_hidden(source, start, kernel, bias) for source, kernel in zip(sources, kernels))

    def finish(start, hiddens, steps):
        values = [
            two_rows(source, start, hidden, kernel_out, bias_out)
            for source, hidden in zip(sources, hiddens)
        ]
        for step, row in steps:
            store(row, [value[step].astype(BF16) for value in values])

    run_block(starts, rows, stage.dilation, hidden_of, finish)


def mean_of(first, second):
    return ((first.astype(F32) + second.astype(F32)) * 0.5).astype(BF16)


def masks_for(channels, width):
    return {dilation: column_masks(channels, width, dilation) for dilation in dilations}


def rows_of_raw(shards, count, wide, shard_rows, channels, width):
    for slot in range(count):
        whole = shards[slot][...].astype(F32).reshape(channels * shard_rows, width)
        for block in range(width // LANES):
            wide[slot, block] = whole[:, block * LANES : (block + 1) * LANES]


def raw_row(wide, slot, line, shard_rows, channels, width):
    picked = pl.ds(line, channels, stride=shard_rows)
    parts = [wide[slot, block, picked, :] for block in range(width // LANES)]
    return jnp.concatenate(parts, axis=1).astype(BF16)


def one_early(chip, *refs):
    weight_refs, (stack_0, stack_1, stack_2, wide) = refs[:5], refs[5:]
    _, channels, shard_rows, width = chip.shape
    odd, _ = position()
    stages = plan(shard_rows, dilations)
    weights = Weights(weight_refs, 0, width)
    masks = masks_for(channels, width)
    rows_of_raw(chip, 2, wide, shard_rows, channels, width)
    stacks = [
        Stack([(ref, stage.early_low)], stage.high, dilation, masks)
        for ref, stage, dilation in zip((stack_0, stack_1, stack_2), stages, dilations)
    ]
    for row in range(stages[0].high + 1):
        line = line_of(row, shard_rows, odd)
        slot = jnp.where(odd == 1, 1 - row // shard_rows, row // shard_rows)
        stacks[0].put(row, raw_row(wide, slot, line, shard_rows, channels, width))
    for layer in range(DEPTH - 1):
        stage = stages[layer + 1]

        def store(row, value):
            stacks[layer + 1].put(row, value.astype(BF16))

        block_one(weights, layer, stage, stage.early, range(stage.early_low, stage.high + 1), stacks[layer], store)


def chunks_turned(values, lines):
    values = list(values)
    chunk = lax.broadcasted_iota(jnp.int32, values[0].shape, 1) // lines
    for bit in range(3):
        step = 1 << bit
        clear = ((chunk >> bit) & 1) == 0
        for index in range(8):
            if index & step:
                continue
            first, second = values[index], values[index + step]
            values[index] = jnp.where(clear, first, pltpu.roll(second, lines * step, 1))
            values[index + step] = jnp.where(clear, pltpu.roll(first, LANES - lines * step, 1), second)
    return values


def one_late(across, kept_0, kept_1, kept_2, *refs):
    weight_refs, (out, tiles, stack_0, stack_1, stack_2, wide) = refs[:5], refs[5:]
    channels, shard_rows, width = across.shape
    odd, edge = position()
    stages = plan(shard_rows, dilations)
    weights = Weights(weight_refs, 0, width)
    masks = masks_for(channels, width)
    rows_of_raw([across], 1, wide, shard_rows, channels, width)
    stacks = [
        Stack([(early, stage.early_low), (late, stage.low)], stage.high, dilation, masks)
        for early, late, stage, dilation in zip(
            (kept_0, kept_1, kept_2), (stack_0, stack_1, stack_2), stages, dilations
        )
    ]
    for row in range(stages[0].low, 0):
        stacks[0].put(row, raw_row(wide, 0, line_of(row, shard_rows, odd), shard_rows, channels, width))
    for layer in range(DEPTH):
        stage = stages[layer + 1]

        def store(row, value):
            value = value.astype(BF16)
            if layer == DEPTH - 1:
                out[line_of(row, shard_rows, odd)] = value
                return
            if row < 0:
                value = jnp.where(edge, jnp.zeros_like(value), value)
            stacks[layer + 1].put(row, value)

        block_one(weights, layer, stage, stage.late, range(stage.low, stage.early_low), stacks[layer], store)

    half = channels // 2
    low_lanes = lax.broadcasted_iota(jnp.int32, (half, LANES), 1) < LANES // 2
    for block in range(width // LANES):
        values = [out[row, :, block * LANES : (block + 1) * LANES] for row in range(shard_rows)]
        for index, value in enumerate(chunks_turned(values, shard_rows)):
            top, bottom = value[:half], value[half:]
            device = block * 16 + index
            tiles[device] = jnp.where(low_lanes, top, pltpu.roll(bottom, LANES // 2, 1))
            tiles[device + 8] = jnp.where(low_lanes, pltpu.roll(top, LANES // 2, 1), bottom)


def symmetrize(tiles, own, out):
    shard_rows, channels, width = own.shape
    half = channels // 2
    low_lanes = lax.broadcasted_iota(jnp.int32, (half, LANES), 1) < LANES // 2
    lane_in = lax.broadcasted_iota(jnp.int32, (LANES, LANES), 0)
    lane_out = lax.broadcasted_iota(jnp.int32, (LANES, LANES), 1)
    size = shard_rows
    turned = (lane_out // (size * size)) * (size * size) + (lane_out % size) * size + (lane_out // size) % size
    swap = jnp.where(lane_in == turned, 1.0, 0.0).astype(BF16)
    for block in range(width // LANES):
        values = []
        for index in range(8):
            first, second = tiles[block * 16 + index], tiles[block * 16 + index + 8]
            top = jnp.where(low_lanes, first, pltpu.roll(second, LANES // 2, 1))
            bottom = jnp.where(low_lanes, pltpu.roll(first, LANES // 2, 1), second)
            values += [top, bottom]
        stacked = jnp.concatenate(values, axis=0)
        stacked = jnp.dot(stacked, swap, preferred_element_type=F32).astype(BF16)
        values = [stacked[index * channels : (index + 1) * channels] for index in range(8)]
        lanes = slice(block * LANES, (block + 1) * LANES)
        for row, value in enumerate(chunks_turned(values, shard_rows)):
            out[row, :, lanes] = mean_of(own[row, :, lanes], value)


def two_steps():
    return dilations + (dilations[0],)


LAYERS_OF = (0, 1, 1, 2, 2, 3)


def two_early(chip, *refs):
    weight_refs, stack_refs = refs[:5], refs[5:]
    _, shard_rows, channels, width = chip.shape
    odd, _ = position()
    steps = two_steps()
    stages = plan(shard_rows, steps)
    weights = Weights(weight_refs, DEPTH, width)
    masks = masks_for(channels, width)
    stacks = [[], [], [], []]
    for ref, index in zip(stack_refs, LAYERS_OF):
        stacks[index].append(Stack([(ref, stages[index].early_low)], stages[index].high, steps[index], masks))
    for row in range(stages[0].high + 1):
        slot = jnp.where(odd == 1, 1 - row // shard_rows, row // shard_rows)
        stacks[0][0].put(row, chip[slot, line_of(row, shard_rows, odd)])
    sources = stacks[0] * 2
    for layer in range(DEPTH):
        stage = stages[layer + 1]

        def store(row, values):
            if layer == DEPTH - 1:
                values = [mean_of(*values)]
            for target, value in zip(stacks[layer + 1], values):
                target.put(row, value)

        block_two(weights, layer, stage, stage.early, range(stage.early_low, stage.high + 1), sources, store)
        sources = stacks[layer + 1]


def two_late(across, *refs):
    kept_refs, weight_refs, out, stack_refs, wide = refs[:6], refs[6:11], refs[11], refs[12:18], refs[18]
    shard_rows, channels, width = across.shape
    odd, edge = position()
    steps = two_steps()
    stages = plan(shard_rows, steps)
    weights = Weights(weight_refs, DEPTH, width)
    masks = masks_for(channels, width)
    stacks = [[], [], [], []]
    for early, late, index in zip(kept_refs, stack_refs, LAYERS_OF):
        stage = stages[index]
        stacks[index].append(Stack([(early, stage.early_low), (late, stage.low)], stage.high, steps[index], masks))
    for row in range(stages[0].low, 0):
        stacks[0][0].put(row, across[line_of(row, shard_rows, odd)])
    sources = stacks[0] * 2
    for layer in range(DEPTH):
        stage = stages[layer + 1]

        def store(row, values):
            if layer == DEPTH - 1:
                values = [mean_of(*values)]
            for target, value in zip(stacks[layer + 1], values):
                if row < 0:
                    value = jnp.where(edge, jnp.zeros_like(value), value)
                target.put(row, value)

        block_two(weights, layer, stage, stage.late, range(stage.low, stage.early_low), sources, store)
        sources = stacks[layer + 1]

    stage = stages[DEPTH + 1]

    def store_last(row, value):
        picked = pl.ds(line_of(row, shard_rows, odd), channels, stride=shard_rows)
        for block in range(width // LANES):
            wide[block, picked, :] = value[:, block * LANES : (block + 1) * LANES]

    block_one(weights, DEPTH, stage, stage.late, range(stage.low, stage.high + 1), sources[0], store_last)
    whole = jnp.concatenate([wide[block] for block in range(width // LANES)], axis=1)
    out[...] = whole.reshape(channels, shard_rows, width).astype(BF16)


VMEM = pl.BlockSpec(memory_space=pltpu.VMEM)
ANY = pl.BlockSpec(memory_space=pl.ANY)


class Calls:
    def __init__(self, channels, shard_rows, width, inner, size):
        self.channels, self.shard_rows, self.width, self.inner, self.size = channels, shard_rows, width, inner, size
        self.one = plan(shard_rows, dilations)
        self.two = plan(shard_rows, two_steps())

    def stack(self, low, high):
        return (max(high - low + 1, 1), 3 * self.channels, self.width)

    def early(self, stage):
        return self.stack(stage.early_low, stage.high)

    def late(self, stage):
        return pltpu.VMEM(self.stack(stage.low, stage.early_low - 1), BF16)

    def wide(self, *shards):
        return pltpu.VMEM(shards + (self.width // LANES, self.channels * self.shard_rows, LANES), F32)

    def call(self, body, args, shapes, scratch, specs=None):
        shapes = [shape if isinstance(shape, jax.ShapeDtypeStruct) else jax.ShapeDtypeStruct(shape, BF16) for shape in shapes]
        single = len(shapes) == 1
        return pl.pallas_call(
            body,
            out_shape=shapes[0] if single else shapes,
            in_specs=specs or [VMEM] * len(args),
            out_specs=VMEM if single else [VMEM] * len(shapes),
            scratch_shapes=scratch,
            compiler_params=pltpu.CompilerParams(vmem_limit_bytes=(10 + 6 * self.width // LANES) * 1024 * 1024),
            name=body.__name__,
        )(*args)

    def prepare(self, w_conv, bias_in, w_out, bias_out):
        layers, inner, channels = w_conv.shape[0], self.inner, self.channels
        shapes = [
            (layers, 2 * inner, 12 * channels),
            (DEPTH, 2 * inner, 12 * channels),
            (layers, 2 * channels, 2 * inner),
            jax.ShapeDtypeStruct((layers, 2 * inner, LANES), F32),
            jax.ShapeDtypeStruct((layers, 2 * channels, LANES), F32),
        ]
        scratch = [
            pltpu.VMEM(w_conv.shape, BF16), pltpu.VMEM(w_out.shape, BF16), pltpu.SemaphoreType.DMA((2,)),
        ]
        return self.call(
            prepare, (w_conv, bias_in, w_out, bias_out), shapes, scratch, [ANY, VMEM, ANY, VMEM]
        )

    def one_early(self, *args):
        return self.call(one_early, args, [self.early(stage) for stage in self.one[:DEPTH]], [self.wide(2)])

    def one_late(self, *args):
        shapes = [(self.shard_rows, self.channels, self.width), (self.size, self.channels // 2, LANES)]
        return self.call(one_late, args, shapes, [self.late(stage) for stage in self.one[:DEPTH]] + [self.wide(1)])

    def symmetrize(self, *args):
        return self.call(symmetrize, args, [(self.shard_rows, self.channels, self.width)], [])

    def two_early(self, *args):
        return self.call(two_early, args, [self.early(self.two[index]) for index in LAYERS_OF], [])

    def two_late(self, *args):
        scratch = [self.late(self.two[index]) for index in LAYERS_OF] + [self.wide()]
        return self.call(two_late, args, [(self.channels, self.shard_rows, self.width)], scratch)


def neighbours(array, axis):
    size = lax.axis_size(axis)
    edges = [(i, i + 1) for i in range(1, size - 1, 2)]
    edges = edges + [(j, i) for i, j in edges]
    across = lax.ppermute(array, axis, edges)
    chip = lax.all_gather(array, axis, axis_index_groups=[[i, i + 1] for i in range(0, size, 2)])
    return across, chip


def on_device(features, w_conv, bias_in, w_out, bias_out):
    channels, shard_rows, width = features.shape
    calls = Calls(channels, shard_rows, width, w_conv.shape[2], lax.axis_size("row"))
    across, chip = neighbours(features, "row")
    weights = calls.prepare(w_conv, bias_in, w_out.transpose(0, 2, 1), bias_out)
    kept = calls.one_early(chip, *weights)
    field, tiles = calls.one_late(across, *kept, *weights)
    received = lax.all_to_all(tiles, "row", split_axis=0, concat_axis=0, tiled=True)
    field = calls.symmetrize(received, field)
    across, chip = neighbours(field, "row")
    kept = calls.two_early(chip, *weights)
    return calls.two_late(across, *kept, *weights)


def solution(mesh):
    in_specs = (P("groups", "row", None), P(), P(), P(), P())
    out_specs = P("groups", "row", None)
    return jax.shard_map(
        on_device, mesh=mesh, in_specs=in_specs, out_specs=out_specs, check_vma=False
    )
```

```python
import jax
import jax.numpy as jnp
from jax import lax
from jax.experimental import pallas as pl
from jax.experimental.pallas import tpu as pltpu
from jax.sharding import PartitionSpec as P

SECTIONS = 2
DEPTH = 3

dilations = (1, 2, 4)
LANES = 128
LAG = 2
F32 = jnp.float32
BF16 = jnp.bfloat16


class Stage:
    def __init__(self, dilation, low, high, early_low, late, early):
        self.dilation, self.low, self.high, self.early_low = dilation, low, high, early_low
        self.late, self.early = late, early
        self.keep = ()


def cover(low, high, limit, dilation):
    covered, starts = set(), []
    for row in range(low, high + 1):
        if row in covered:
            continue
        start = row
        if row + dilation > limit and row - dilation >= low:
            start = row - dilation
        starts.append(start)
        covered |= {start, start + dilation}
    return starts, covered


def plan(shard_rows, steps):
    reach = sum(steps)
    ready = 0
    stages = [Stage(0, -reach, shard_rows - 1 + reach, 0, [], [])]
    for dilation in steps:
        reach, ready = reach - dilation, ready + dilation
        low, high = -reach, shard_rows - 1 + reach
        late, covered = cover(low, min(ready - 1, high), high, dilation)
        early_low = low
        while early_low in covered and early_low <= high:
            early_low += 1
        early = cover(early_low, high, high, dilation)[0] if early_low <= high else []
        stage = Stage(dilation, low, high, early_low, late, early)
        need = min(max(covered) + dilation, stages[-1].high)
        stages[-1].keep = tuple(range(stages[-1].early_low, need + 1))
        stages.append(stage)
    return stages


def column_masks(channels, width, dilation):
    column = lax.broadcasted_iota(jnp.int16, (channels, width), 1)
    return column >= jnp.int16(dilation), column < jnp.int16(width - dilation)


class Stack:
    def __init__(self, parts, top, dilation, masks):
        self.parts, self.top, self.dilation, self.masks = parts, top, dilation, masks[dilation]

    def find(self, row):
        for ref, base in self.parts:
            if row >= base:
                return ref, row - base
        raise ValueError(row)

    def put(self, row, value):
        channels, width = value.shape
        ref, index = self.find(row)
        zeros = jnp.zeros_like(value)
        ref[index, :channels, :] = jnp.where(self.masks[0], pltpu.roll(value, self.dilation, 1), zeros)
        ref[index, channels : 2 * channels, :] = value
        ref[index, 2 * channels :, :] = jnp.where(
            self.masks[1], pltpu.roll(value, width - self.dilation, 1), zeros
        )

    def get(self, row, place):
        ref, index = self.find(min(row, self.top))
        channels = ref.shape[1] // 3
        return ref[index, place * channels : (place + 1) * channels, :]

    def window(self, start):
        return jnp.concatenate(
            [self.get(start + (tap - 1) * self.dilation, place) for place in range(3) for tap in range(4)], axis=0
        )


def spread_conv(banded, slot, w_conv, layer, turned, odd):
    inner, channels = w_conv.shape[2], w_conv.shape[3]
    zeros = jnp.zeros((inner, channels), BF16)
    for col_tap in range(3):
        taps = []
        for row_tap in range(3):
            line = jnp.where(odd == 1, 2 - row_tap, row_tap)
            taps.append(w_conv[layer, col_tap * 3 + line if turned else line * 3 + col_tap])
        left = col_tap * 4 * channels
        banded[slot, :inner, left : left + 4 * channels] = jnp.concatenate(taps + [zeros], axis=1)
        banded[slot, inner:, left : left + 4 * channels] = jnp.concatenate([zeros] + taps, axis=1)


def spread_out(doubled, slot, w_out, layer):
    block = w_out[layer].astype(F32).T.astype(BF16)
    zeros = jnp.zeros_like(block)
    doubled[slot] = jnp.concatenate(
        [jnp.concatenate([block, zeros], axis=1), jnp.concatenate([zeros, block], axis=1)], axis=0
    )


def as_column(row, copies):
    size = row.shape[1]
    across = lax.broadcasted_iota(jnp.int32, (size, size), 1)
    down = lax.broadcasted_iota(jnp.int32, (size, size), 0)
    spread = jnp.where(across == down, jnp.broadcast_to(row, (size, size)), 0.0)
    column = jnp.sum(spread, axis=1, keepdims=True)
    return jnp.concatenate([column] * copies, axis=0)


def run_block(starts, rows, dilation, hidden_of, finish):
    waiting, done = [], set()

    def complete(start, hidden):
        steps = []
        for step, row in enumerate((start, start + dilation)):
            if row in rows and row not in done:
                steps.append((step, row))
                done.add(row)
        finish(start, hidden, steps)

    for start in starts:
        waiting.append((start, hidden_of(start)))
        if len(waiting) > LAG:
            complete(*waiting.pop(0))
    for item in waiting:
        complete(*item)


def conv_hidden(stack, start, kernel, bias):
    inner = jnp.dot(kernel, stack.window(start), preferred_element_type=F32)
    return jnp.maximum(inner + bias, 0.0).astype(BF16)


def two_rows(stack, start, hidden, kernel, bias):
    blended = jnp.dot(kernel, hidden, preferred_element_type=F32)
    residual = [stack.get(start + step * stack.dilation, 1).astype(F32) for step in range(2)]
    total = jnp.concatenate(residual, axis=0) + blended + bias
    channels = total.shape[0] // 2
    return total[:channels], total[channels:]


def fetch(pairs, sems):
    copies = [pltpu.make_async_copy(source, target, sems.at[i]) for i, (source, target) in enumerate(pairs)]
    for copy in copies:
        copy.start()
    return copies


def position():
    device = lax.axis_index("row")
    size = lax.axis_size("row")
    odd = device % 2
    edge = jnp.logical_or(device == 0, device == size - 1)
    return odd, edge


def line_of(row, shard_rows, odd):
    inside = row % shard_rows
    return jnp.where(odd == 1, shard_rows - 1 - inside, inside)


def prepare(w_conv, bias_in, w_out, bias_out, banded, turned, doubled, bias, bias_last,
            conv, proj, first_bias, last_bias, sems):
    odd, _ = position()
    pairs = [(w_conv, conv), (w_out, proj), (bias_in, first_bias), (bias_out, last_bias)]
    for copy in fetch(pairs, sems):
        copy.wait()
    bias_in, bias_out = first_bias, last_bias
    layers = w_conv.shape[0]
    for layer in range(layers):
        spread_conv(banded, layer, conv, layer, False, odd)
        spread_out(doubled, layer, proj, layer)
        bias[layer] = jnp.broadcast_to(as_column(bias_in[layer : layer + 1, :], 2), bias.shape[1:])
        bias_last[layer] = jnp.broadcast_to(as_column(bias_out[layer : layer + 1, :], 2), bias_last.shape[1:])
    for layer in range(turned.shape[0]):
        spread_conv(turned, layer, conv, layers - 1 - DEPTH + layer, True, odd)


class Weights:
    def __init__(self, refs, base, width):
        self.refs, self.base, self.blocks = refs, base, width // LANES

    def conv(self, layer):
        return self.refs[0][self.base + layer]

    def conv_turned(self, layer):
        return self.refs[1][layer]

    def out(self, layer):
        return self.refs[2][self.base + layer]

    def bias(self, layer):
        return jnp.concatenate([self.refs[3][self.base + layer]] * self.blocks, axis=1)

    def bias_out(self, layer):
        return jnp.concatenate([self.refs[4][self.base + layer]] * self.blocks, axis=1)


def block_one(weights, layer, stage, starts, rows, source, store):
    kernel, kernel_out = weights.conv(layer), weights.out(layer)
    bias, bias_out = weights.bias(layer), weights.bias_out(layer)

    def hidden_of(start):
        return conv_hidden(source, start, kernel, bias)

    def finish(start, hidden, steps):
        values = two_rows(source, start, hidden, kernel_out, bias_out)
        for step, row in steps:
            store(row, values[step])

    run_block(starts, rows, stage.dilation, hidden_of, finish)


def block_two(weights, layer, stage, starts, rows, sources, store):
    kernels = (weights.conv(layer), weights.conv_turned(layer))
    kernel_out, bias, bias_out = weights.out(layer), weights.bias(layer), weights.bias_out(layer)

    def hidden_of(start):
        if sources[0] is sources[1]:
            both = conv_hidden(
                sources[0], start, jnp.concatenate(kernels, axis=0), jnp.concatenate([bias, bias], axis=0)
            )
            half = both.shape[0] // 2
            return both[:half], both[half:]
        return tuple(conv_hidden(source, start, kernel, bias) for source, kernel in zip(sources, kernels))

    def finish(start, hiddens, steps):
        values = [
            two_rows(source, start, hidden, kernel_out, bias_out)
            for source, hidden in zip(sources, hiddens)
        ]
        for step, row in steps:
            store(row, [value[step].astype(BF16) for value in values])

    run_block(starts, rows, stage.dilation, hidden_of, finish)


def mean_of(first, second):
    return ((first.astype(F32) + second.astype(F32)) * 0.5).astype(BF16)


def masks_for(channels, width):
    return {dilation: column_masks(channels, width, dilation) for dilation in dilations}


def rows_of_raw(shards, count, wide, shard_rows, channels, width):
    for slot in range(count):
        whole = shards[slot][...].astype(F32).reshape(channels * shard_rows, width)
        for block in range(width // LANES):
            wide[slot, block] = whole[:, block * LANES : (block + 1) * LANES]


def raw_row(wide, slot, line, shard_rows, channels, width):
    picked = pl.ds(line, channels, stride=shard_rows)
    parts = [wide[slot, block, picked, :] for block in range(width // LANES)]
    return jnp.concatenate(parts, axis=1).astype(BF16)


def one_early(chip, *refs):
    weight_refs, (stack_0, stack_1, stack_2, wide) = refs[:5], refs[5:]
    _, channels, shard_rows, width = chip.shape
    odd, _ = position()
    stages = plan(shard_rows, dilations)
    weights = Weights(weight_refs, 0, width)
    masks = masks_for(channels, width)
    rows_of_raw(chip, 2, wide, shard_rows, channels, width)
    stacks = [
        Stack([(ref, stage.early_low)], stage.high, dilation, masks)
        for ref, stage, dilation in zip((stack_0, stack_1, stack_2), stages, dilations)
    ]
    for row in range(stages[0].high + 1):
        line = line_of(row, shard_rows, odd)
        slot = jnp.where(odd == 1, 1 - row // shard_rows, row // shard_rows)
        stacks[0].put(row, raw_row(wide, slot, line, shard_rows, channels, width))
    for layer in range(DEPTH - 1):
        stage = stages[layer + 1]

        def store(row, value):
            stacks[layer + 1].put(row, value.astype(BF16))

        block_one(weights, layer, stage, stage.early, range(stage.early_low, stage.high + 1), stacks[layer], store)


def chunks_turned(values, lines):
    values = list(values)
    chunk = lax.broadcasted_iota(jnp.int32, values[0].shape, 1) // lines
    for bit in range(3):
        step = 1 << bit
        clear = ((chunk >> bit) & 1) == 0
        for index in range(8):
            if index & step:
                continue
            first, second = values[index], values[index + step]
            values[index] = jnp.where(clear, first, pltpu.roll(second, lines * step, 1))
            values[index + step] = jnp.where(clear, pltpu.roll(first, LANES - lines * step, 1), second)
    return values


def one_late(across, kept_0, kept_1, kept_2, *refs):
    weight_refs, (out, tiles, stack_0, stack_1, stack_2, wide) = refs[:5], refs[5:]
    channels, shard_rows, width = across.shape
    odd, edge = position()
    stages = plan(shard_rows, dilations)
    weights = Weights(weight_refs, 0, width)
    masks = masks_for(channels, width)
    rows_of_raw([across], 1, wide, shard_rows, channels, width)
    stacks = [
        Stack([(early, stage.early_low), (late, stage.low)], stage.high, dilation, masks)
        for early, late, stage, dilation in zip(
            (kept_0, kept_1, kept_2), (stack_0, stack_1, stack_2), stages, dilations
        )
    ]
    for row in range(stages[0].low, 0):
        stacks[0].put(row, raw_row(wide, 0, line_of(row, shard_rows, odd), shard_rows, channels, width))
    for layer in range(DEPTH):
        stage = stages[layer + 1]

        def store(row, value):
            value = value.astype(BF16)
            if layer == DEPTH - 1:
                out[line_of(row, shard_rows, odd)] = value
                return
            if row < 0:
                value = jnp.where(edge, jnp.zeros_like(value), value)
            stacks[layer + 1].put(row, value)

        block_one(weights, layer, stage, stage.late, range(stage.low, stage.early_low), stacks[layer], store)

    half = channels // 2
    low_lanes = lax.broadcasted_iota(jnp.int32, (half, LANES), 1) < LANES // 2
    for block in range(width // LANES):
        values = [out[row, :, block * LANES : (block + 1) * LANES] for row in range(shard_rows)]
        for index, value in enumerate(chunks_turned(values, shard_rows)):
            top, bottom = value[:half], value[half:]
            device = block * 16 + index
            tiles[device] = jnp.where(low_lanes, top, pltpu.roll(bottom, LANES // 2, 1))
            tiles[device + 8] = jnp.where(low_lanes, pltpu.roll(top, LANES // 2, 1), bottom)


def symmetrize(tiles, own, out):
    shard_rows, channels, width = own.shape
    half = channels // 2
    low_lanes = lax.broadcasted_iota(jnp.int32, (half, LANES), 1) < LANES // 2
    lane_in = lax.broadcasted_iota(jnp.int32, (LANES, LANES), 0)
    lane_out = lax.broadcasted_iota(jnp.int32, (LANES, LANES), 1)
    size = shard_rows
    turned = (lane_out // (size * size)) * (size * size) + (lane_out % size) * size + (lane_out // size) % size
    swap = jnp.where(lane_in == turned, 1.0, 0.0).astype(BF16)
    for block in range(width // LANES):
        values = []
        for index in range(8):
            first, second = tiles[block * 16 + index], tiles[block * 16 + index + 8]
            top = jnp.where(low_lanes, first, pltpu.roll(second, LANES // 2, 1))
            bottom = jnp.where(low_lanes, pltpu.roll(first, LANES // 2, 1), second)
            values += [top, bottom]
        stacked = jnp.concatenate(values, axis=0)
        stacked = jnp.dot(stacked, swap, preferred_element_type=F32).astype(BF16)
        values = [stacked[index * channels : (index + 1) * channels] for index in range(8)]
        lanes = slice(block * LANES, (block + 1) * LANES)
        for row, value in enumerate(chunks_turned(values, shard_rows)):
            out[row, :, lanes] = mean_of(own[row, :, lanes], value)


def two_steps():
    return dilations + (dilations[0],)


LAYERS_OF = (0, 1, 1, 2, 2, 3)


def two_early(chip, *refs):
    weight_refs, stack_refs = refs[:5], refs[5:]
    _, shard_rows, channels, width = chip.shape
    odd, _ = position()
    steps = two_steps()
    stages = plan(shard_rows, steps)
    weights = Weights(weight_refs, DEPTH, width)
    masks = masks_for(channels, width)
    stacks = [[], [], [], []]
    for ref, index in zip(stack_refs, LAYERS_OF):
        stacks[index].append(Stack([(ref, stages[index].early_low)], stages[index].high, steps[index], masks))
    for row in range(stages[0].high + 1):
        slot = jnp.where(odd == 1, 1 - row // shard_rows, row // shard_rows)
        stacks[0][0].put(row, chip[slot, line_of(row, shard_rows, odd)])
    sources = stacks[0] * 2
    for layer in range(DEPTH):
        stage = stages[layer + 1]

        def store(row, values):
            if layer == DEPTH - 1:
                values = [mean_of(*values)]
            for target, value in zip(stacks[layer + 1], values):
                target.put(row, value)

        block_two(weights, layer, stage, stage.early, range(stage.early_low, stage.high + 1), sources, store)
        sources = stacks[layer + 1]


def two_late(across, *refs):
    kept_refs, weight_refs, out, stack_refs, wide = refs[:6], refs[6:11], refs[11], refs[12:18], refs[18]
    shard_rows, channels, width = across.shape
    odd, edge = position()
    steps = two_steps()
    stages = plan(shard_rows, steps)
    weights = Weights(weight_refs, DEPTH, width)
    masks = masks_for(channels, width)
    stacks = [[], [], [], []]
    for early, late, index in zip(kept_refs, stack_refs, LAYERS_OF):
        stage = stages[index]
        stacks[index].append(Stack([(early, stage.early_low), (late, stage.low)], stage.high, steps[index], masks))
    for row in range(stages[0].low, 0):
        stacks[0][0].put(row, across[line_of(row, shard_rows, odd)])
    sources = stacks[0] * 2
    for layer in range(DEPTH):
        stage = stages[layer + 1]

        def store(row, values):
            if layer == DEPTH - 1:
                values = [mean_of(*values)]
            for target, value in zip(stacks[layer + 1], values):
                if row < 0:
                    value = jnp.where(edge, jnp.zeros_like(value), value)
                target.put(row, value)

        block_two(weights, layer, stage, stage.late, range(stage.low, stage.early_low), sources, store)
        sources = stacks[layer + 1]

    stage = stages[DEPTH + 1]

    def store_last(row, value):
        picked = pl.ds(line_of(row, shard_rows, odd), channels, stride=shard_rows)
        for block in range(width // LANES):
            wide[block, picked, :] = value[:, block * LANES : (block + 1) * LANES]

    block_one(weights, DEPTH, stage, stage.late, range(stage.low, stage.high + 1), sources[0], store_last)
    whole = jnp.concatenate([wide[block] for block in range(width // LANES)], axis=1)
    out[...] = whole.reshape(channels, shard_rows, width).astype(BF16)


VMEM = pl.BlockSpec(memory_space=pltpu.VMEM)
HBM = pl.BlockSpec(memory_space=pltpu.HBM)


class Calls:
    def __init__(self, channels, shard_rows, width, inner, size):
        self.channels, self.shard_rows, self.width, self.inner, self.size = channels, shard_rows, width, inner, size
        self.one = plan(shard_rows, dilations)
        self.two = plan(shard_rows, two_steps())

    def stack(self, low, high):
        return (max(high - low + 1, 1), 3 * self.channels, self.width)

    def early(self, stage):
        return self.stack(stage.early_low, stage.high)

    def late(self, stage):
        return pltpu.VMEM(self.stack(stage.low, stage.early_low - 1), BF16)

    def wide(self, *shards):
        return pltpu.VMEM(shards + (self.width // LANES, self.channels * self.shard_rows, LANES), F32)

    def call(self, body, args, shapes, scratch, specs=None):
        shapes = [shape if isinstance(shape, jax.ShapeDtypeStruct) else jax.ShapeDtypeStruct(shape, BF16) for shape in shapes]
        single = len(shapes) == 1
        return pl.pallas_call(
            body,
            out_shape=shapes[0] if single else shapes,
            in_specs=specs or [VMEM] * len(args),
            out_specs=VMEM if single else [VMEM] * len(shapes),
            scratch_shapes=scratch,
            compiler_params=pltpu.CompilerParams(vmem_limit_bytes=(10 + 6 * self.width // LANES) * 1024 * 1024),
            name=body.__name__,
        )(*args)

    def prepare(self, w_conv, bias_in, w_out, bias_out):
        layers, inner, channels = w_conv.shape[0], self.inner, self.channels
        shapes = [
            (layers, 2 * inner, 12 * channels),
            (DEPTH, 2 * inner, 12 * channels),
            (layers, 2 * channels, 2 * inner),
            jax.ShapeDtypeStruct((layers, 2 * inner, LANES), F32),
            jax.ShapeDtypeStruct((layers, 2 * channels, LANES), F32),
        ]
        scratch = [
            pltpu.VMEM(w_conv.shape, BF16), pltpu.VMEM(w_out.shape, BF16),
            pltpu.VMEM(bias_in.shape, F32), pltpu.VMEM(bias_out.shape, F32), pltpu.SemaphoreType.DMA((4,)),
        ]
        args = [pltpu.with_memory_space_constraint(arg, pltpu.HBM) for arg in (w_conv, bias_in, w_out, bias_out)]
        return self.call(
            prepare, args, shapes, scratch, [HBM] * 4
        )

    def one_early(self, *args):
        return self.call(one_early, args, [self.early(stage) for stage in self.one[:DEPTH]], [self.wide(2)])

    def one_late(self, *args):
        shapes = [(self.shard_rows, self.channels, self.width), (self.size, self.channels // 2, LANES)]
        return self.call(one_late, args, shapes, [self.late(stage) for stage in self.one[:DEPTH]] + [self.wide(1)])

    def symmetrize(self, *args):
        return self.call(symmetrize, args, [(self.shard_rows, self.channels, self.width)], [])

    def two_early(self, *args):
        return self.call(two_early, args, [self.early(self.two[index]) for index in LAYERS_OF], [])

    def two_late(self, *args):
        scratch = [self.late(self.two[index]) for index in LAYERS_OF] + [self.wide()]
        return self.call(two_late, args, [(self.channels, self.shard_rows, self.width)], scratch)


def neighbours(array, axis):
    size = lax.axis_size(axis)
    edges = [(i, i + 1) for i in range(1, size - 1, 2)]
    edges = edges + [(j, i) for i, j in edges]
    across = lax.ppermute(array, axis, edges)
    chip = lax.all_gather(array, axis, axis_index_groups=[[i, i + 1] for i in range(0, size, 2)])
    return across, chip


def on_device(features, w_conv, bias_in, w_out, bias_out):
    channels, shard_rows, width = features.shape
    calls = Calls(channels, shard_rows, width, w_conv.shape[2], lax.axis_size("row"))
    across, chip = neighbours(features, "row")
    weights = calls.prepare(w_conv, bias_in, w_out.transpose(0, 2, 1), bias_out)
    kept = calls.one_early(chip, *weights)
    field, tiles = calls.one_late(across, *kept, *weights)
    received = lax.all_to_all(tiles, "row", split_axis=0, concat_axis=0, tiled=True)
    field = calls.symmetrize(received, field)
    across, chip = neighbours(field, "row")
    kept = calls.two_early(chip, *weights)
    return calls.two_late(across, *kept, *weights)


def solution(mesh):
    in_specs = (P("groups", "row", None), P(), P(), P(), P())
    out_specs = P("groups", "row", None)
    return jax.shard_map(
        on_device, mesh=mesh, in_specs=in_specs, out_specs=out_specs, check_vma=False
    )
```

```python
import jax
import jax.numpy as jnp
from jax import lax
from jax.experimental import pallas as pl
from jax.experimental.pallas import tpu as pltpu
from jax.sharding import PartitionSpec as P

SECTIONS = 2
DEPTH = 3

dilations = (1, 2, 4)
LANES = 128
LAG = 3
F32 = jnp.float32
BF16 = jnp.bfloat16


class Stage:
    def __init__(self, dilation, low, high, early_low, late, early):
        self.dilation, self.low, self.high, self.early_low = dilation, low, high, early_low
        self.late, self.early = late, early
        self.keep = ()


def group_of(dilation):
    return 4 if dilation < dilations[-1] else 2


def cover(low, high, limit, dilation):
    covered, starts = set(), []
    count = group_of(dilation)
    for row in range(low, high + 1):
        if row in covered:
            continue
        start = row
        for back in range(count):
            candidate = row - back * dilation
            if candidate >= low and candidate + (count - 1) * dilation <= limit:
                start = candidate
                break
        starts.append(start)
        covered |= {start + step * dilation for step in range(count)}
    return starts, covered


def plan(shard_rows, steps):
    reach = sum(steps)
    ready = 0
    stages = [Stage(0, -reach, shard_rows - 1 + reach, 0, [], [])]
    for dilation in steps:
        reach, ready = reach - dilation, ready + dilation
        low, high = -reach, shard_rows - 1 + reach
        late, covered = cover(low, min(ready - 1, high), high, dilation)
        early_low = low
        while early_low in covered and early_low <= high:
            early_low += 1
        early = cover(early_low, high, high, dilation)[0] if early_low <= high else []
        stage = Stage(dilation, low, high, early_low, late, early)
        need = min(max(covered) + dilation, stages[-1].high)
        stages[-1].keep = tuple(range(stages[-1].early_low, need + 1))
        stages.append(stage)
    return stages


def column_masks(channels, width, dilation):
    column = lax.broadcasted_iota(jnp.int16, (channels, width), 1)
    return column >= jnp.int16(dilation), column < jnp.int16(width - dilation)


class Stack:
    def __init__(self, parts, top, dilation, masks):
        self.parts, self.top, self.dilation, self.masks = parts, top, dilation, masks[dilation]

    def find(self, row):
        for ref, base in self.parts:
            if row >= base:
                return ref, row - base
        raise ValueError(row)

    def put(self, row, value):
        channels, width = value.shape
        ref, index = self.find(row)
        zeros = jnp.zeros_like(value)
        ref[index, :channels, :] = jnp.where(self.masks[0], pltpu.roll(value, self.dilation, 1), zeros)
        ref[index, channels : 2 * channels, :] = value
        ref[index, 2 * channels :, :] = jnp.where(
            self.masks[1], pltpu.roll(value, width - self.dilation, 1), zeros
        )

    def get(self, row, place):
        ref, index = self.find(min(row, self.top))
        channels = ref.shape[1] // 3
        return ref[index, place * channels : (place + 1) * channels, :]

    def window(self, start):
        return jnp.concatenate(
            [
                self.get(start + (tap - 1) * self.dilation, place)
                for place in range(3)
                for tap in range(group_of(self.dilation) + 2)
            ],
            axis=0,
        )


def spread_conv(banded, slot, w_conv, layer, turned, odd):
    inner, channels = w_conv.shape[2], w_conv.shape[3]
    count = banded.shape[1] // inner
    zeros = jnp.zeros((inner, channels), BF16)
    for col_tap in range(3):
        taps = []
        for row_tap in range(3):
            line = jnp.where(odd == 1, 2 - row_tap, row_tap)
            taps.append(w_conv[layer, col_tap * 3 + line if turned else line * 3 + col_tap])
        left = col_tap * (count + 2) * channels
        for row in range(count):
            parts = [zeros] * row + taps + [zeros] * (count - 1 - row)
            banded[slot, row * inner : (row + 1) * inner, left : left + (count + 2) * channels] = jnp.concatenate(
                parts, axis=1
            )


def spread_out(doubled, slot, w_out, layer):
    block = w_out[layer].astype(F32).T.astype(BF16)
    zeros = jnp.zeros_like(block)
    doubled[slot] = jnp.concatenate(
        [jnp.concatenate([block, zeros], axis=1), jnp.concatenate([zeros, block], axis=1)], axis=0
    )


def as_column(row, copies):
    size = row.shape[1]
    across = lax.broadcasted_iota(jnp.int32, (size, size), 1)
    down = lax.broadcasted_iota(jnp.int32, (size, size), 0)
    spread = jnp.where(across == down, jnp.broadcast_to(row, (size, size)), 0.0)
    column = jnp.sum(spread, axis=1, keepdims=True)
    return jnp.concatenate([column] * copies, axis=0)


def run_block(starts, rows, dilation, hidden_of, finish):
    waiting, done = [], set()

    def complete(start, hidden):
        steps = []
        for step in range(group_of(dilation)):
            row = start + step * dilation
            if row in rows and row not in done:
                steps.append((step, row))
                done.add(row)
        finish(start, hidden, steps)

    for start in starts:
        waiting.append((start, hidden_of(start)))
        if len(waiting) > LAG:
            complete(*waiting.pop(0))
    for item in waiting:
        complete(*item)


def conv_hidden(stack, start, kernel, bias):
    inner = jnp.dot(kernel, stack.window(start), preferred_element_type=F32)
    return jnp.maximum(inner + bias, 0.0).astype(BF16)


def group_rows(stack, start, hidden, kernel, bias):
    half = kernel.shape[1]
    values = []
    for pair in range(hidden.shape[0] // half):
        blended = jnp.dot(kernel, hidden[pair * half : (pair + 1) * half], preferred_element_type=F32)
        residual = [stack.get(start + (2 * pair + step) * stack.dilation, 1).astype(F32) for step in range(2)]
        total = jnp.concatenate(residual, axis=0) + blended + bias
        channels = total.shape[0] // 2
        values += [total[:channels], total[channels:]]
    return values


def fetch(pairs, sems):
    copies = [pltpu.make_async_copy(source, target, sems.at[i]) for i, (source, target) in enumerate(pairs)]
    for copy in copies:
        copy.start()
    return copies


def position():
    device = lax.axis_index("row")
    size = lax.axis_size("row")
    odd = device % 2
    edge = jnp.logical_or(device == 0, device == size - 1)
    return odd, edge


def line_of(row, shard_rows, odd):
    inside = row % shard_rows
    return jnp.where(odd == 1, shard_rows - 1 - inside, inside)


def layer_steps():
    return dilations * SECTIONS + (dilations[0],)


def slot_of(steps, layer):
    return sum(1 for step in steps[:layer] if group_of(step) == group_of(steps[layer]))


def prepare(w_conv, bias_in, w_out, bias_out, small, large, small_turned, large_turned, doubled, bias, bias_last,
            conv, proj, first_bias, last_bias, sems):
    odd, _ = position()
    pairs = [(w_conv, conv), (w_out, proj), (bias_in, first_bias), (bias_out, last_bias)]
    for copy in fetch(pairs, sems):
        copy.wait()
    steps = layer_steps()
    base = len(steps) - 1 - DEPTH
    for layer, step in enumerate(steps):
        spread_conv(small if group_of(step) == 2 else large, slot_of(steps, layer), conv, layer, False, odd)
        spread_out(doubled, layer, proj, layer)
        bias[layer] = jnp.broadcast_to(as_column(first_bias[layer : layer + 1, :], 4), bias.shape[1:])
        bias_last[layer] = jnp.broadcast_to(as_column(last_bias[layer : layer + 1, :], 2), bias_last.shape[1:])
    for layer, step in enumerate(dilations):
        place = small_turned if group_of(step) == 2 else large_turned
        spread_conv(place, slot_of(dilations, layer), conv, base + layer, True, odd)


class Weights:
    def __init__(self, refs, base, width):
        self.refs, self.base, self.blocks = refs, base, width // LANES

    def conv(self, layer):
        steps = layer_steps()
        layer = self.base + layer
        return self.refs[0 if group_of(steps[layer]) == 2 else 1][slot_of(steps, layer)]

    def conv_turned(self, layer):
        return self.refs[2 if group_of(dilations[layer]) == 2 else 3][slot_of(dilations, layer)]

    def out(self, layer):
        return self.refs[4][self.base + layer]

    def bias(self, layer):
        inner = self.refs[5].shape[1] // 4
        rows = group_of(layer_steps()[self.base + layer]) * inner
        return jnp.concatenate([self.refs[5][self.base + layer, :rows]] * self.blocks, axis=1)

    def bias_out(self, layer):
        return jnp.concatenate([self.refs[6][self.base + layer]] * self.blocks, axis=1)


def block_one(weights, layer, stage, starts, rows, source, store):
    kernel, kernel_out = weights.conv(layer), weights.out(layer)
    bias, bias_out = weights.bias(layer), weights.bias_out(layer)

    def hidden_of(start):
        return conv_hidden(source, start, kernel, bias)

    def finish(start, hidden, steps):
        values = group_rows(source, start, hidden, kernel_out, bias_out)
        for step, row in steps:
            store(row, values[step])

    run_block(starts, rows, stage.dilation, hidden_of, finish)


def block_two(weights, layer, stage, starts, rows, sources, store):
    kernels = (weights.conv(layer), weights.conv_turned(layer))
    kernel_out, bias, bias_out = weights.out(layer), weights.bias(layer), weights.bias_out(layer)

    def hidden_of(start):
        if sources[0] is sources[1]:
            both = conv_hidden(
                sources[0], start, jnp.concatenate(kernels, axis=0), jnp.concatenate([bias, bias], axis=0)
            )
            half = both.shape[0] // 2
            return both[:half], both[half:]
        return tuple(conv_hidden(source, start, kernel, bias) for source, kernel in zip(sources, kernels))

    def finish(start, hiddens, steps):
        values = [
            group_rows(source, start, hidden, kernel_out, bias_out)
            for source, hidden in zip(sources, hiddens)
        ]
        for step, row in steps:
            store(row, [value[step].astype(BF16) for value in values])

    run_block(starts, rows, stage.dilation, hidden_of, finish)


def mean_of(first, second):
    return ((first.astype(F32) + second.astype(F32)) * 0.5).astype(BF16)


def masks_for(channels, width):
    return {dilation: column_masks(channels, width, dilation) for dilation in dilations}


def rows_of_raw(shards, count, wide, shard_rows, channels, width):
    for slot in range(count):
        whole = shards[slot][...].astype(F32).reshape(channels * shard_rows, width)
        for block in range(width // LANES):
            wide[slot, block] = whole[:, block * LANES : (block + 1) * LANES]


def raw_row(wide, slot, line, shard_rows, channels, width):
    picked = pl.ds(line, channels, stride=shard_rows)
    parts = [wide[slot, block, picked, :] for block in range(width // LANES)]
    return jnp.concatenate(parts, axis=1).astype(BF16)


def one_early(chip, *refs):
    weight_refs, (stack_0, stack_1, stack_2, wide) = refs[:7], refs[7:]
    _, channels, shard_rows, width = chip.shape
    odd, _ = position()
    stages = plan(shard_rows, dilations)
    weights = Weights(weight_refs, 0, width)
    masks = masks_for(channels, width)
    rows_of_raw(chip, 2, wide, shard_rows, channels, width)
    stacks = [
        Stack([(ref, stage.early_low)], stage.high, dilation, masks)
        for ref, stage, dilation in zip((stack_0, stack_1, stack_2), stages, dilations)
    ]
    for row in range(stages[0].high + 1):
        line = line_of(row, shard_rows, odd)
        slot = jnp.where(odd == 1, 1 - row // shard_rows, row // shard_rows)
        stacks[0].put(row, raw_row(wide, slot, line, shard_rows, channels, width))
    for layer in range(DEPTH - 1):
        stage = stages[layer + 1]

        def store(row, value):
            stacks[layer + 1].put(row, value.astype(BF16))

        block_one(weights, layer, stage, stage.early, range(stage.early_low, stage.high + 1), stacks[layer], store)


def chunks_turned(values, lines):
    values = list(values)
    chunk = lax.broadcasted_iota(jnp.int32, values[0].shape, 1) // lines
    for bit in range(3):
        step = 1 << bit
        clear = ((chunk >> bit) & 1) == 0
        for index in range(8):
            if index & step:
                continue
            first, second = values[index], values[index + step]
            values[index] = jnp.where(clear, first, pltpu.roll(second, lines * step, 1))
            values[index + step] = jnp.where(clear, pltpu.roll(first, LANES - lines * step, 1), second)
    return values


def one_late(across, kept_0, kept_1, kept_2, *refs):
    weight_refs, (out, tiles, stack_0, stack_1, stack_2, wide) = refs[:7], refs[7:]
    channels, shard_rows, width = across.shape
    odd, edge = position()
    stages = plan(shard_rows, dilations)
    weights = Weights(weight_refs, 0, width)
    masks = masks_for(channels, width)
    rows_of_raw([across], 1, wide, shard_rows, channels, width)
    stacks = [
        Stack([(early, stage.early_low), (late, stage.low)], stage.high, dilation, masks)
        for early, late, stage, dilation in zip(
            (kept_0, kept_1, kept_2), (stack_0, stack_1, stack_2), stages, dilations
        )
    ]
    for row in range(stages[0].low, 0):
        stacks[0].put(row, raw_row(wide, 0, line_of(row, shard_rows, odd), shard_rows, channels, width))
    for layer in range(DEPTH):
        stage = stages[layer + 1]

        def store(row, value):
            value = value.astype(BF16)
            if layer == DEPTH - 1:
                out[line_of(row, shard_rows, odd)] = value
                return
            if row < 0:
                value = jnp.where(edge, jnp.zeros_like(value), value)
            stacks[layer + 1].put(row, value)

        block_one(weights, layer, stage, stage.late, range(stage.low, stage.early_low), stacks[layer], store)

    half = channels // 2
    low_lanes = lax.broadcasted_iota(jnp.int32, (half, LANES), 1) < LANES // 2
    for block in range(width // LANES):
        values = [out[row, :, block * LANES : (block + 1) * LANES] for row in range(shard_rows)]
        for index, value in enumerate(chunks_turned(values, shard_rows)):
            top, bottom = value[:half], value[half:]
            device = block * 16 + index
            tiles[device] = jnp.where(low_lanes, top, pltpu.roll(bottom, LANES // 2, 1))
            tiles[device + 8] = jnp.where(low_lanes, pltpu.roll(top, LANES // 2, 1), bottom)


def symmetrize(tiles, own, out):
    shard_rows, channels, width = own.shape
    half = channels // 2
    low_lanes = lax.broadcasted_iota(jnp.int32, (half, LANES), 1) < LANES // 2
    lane_in = lax.broadcasted_iota(jnp.int32, (LANES, LANES), 0)
    lane_out = lax.broadcasted_iota(jnp.int32, (LANES, LANES), 1)
    size = shard_rows
    turned = (lane_out // (size * size)) * (size * size) + (lane_out % size) * size + (lane_out // size) % size
    swap = jnp.where(lane_in == turned, 1.0, 0.0).astype(BF16)
    for block in range(width // LANES):
        values = []
        for index in range(8):
            first, second = tiles[block * 16 + index], tiles[block * 16 + index + 8]
            top = jnp.where(low_lanes, first, pltpu.roll(second, LANES // 2, 1))
            bottom = jnp.where(low_lanes, pltpu.roll(first, LANES // 2, 1), second)
            values += [top, bottom]
        stacked = jnp.concatenate(values, axis=0)
        stacked = jnp.dot(stacked, swap, preferred_element_type=F32).astype(BF16)
        values = [stacked[index * channels : (index + 1) * channels] for index in range(8)]
        lanes = slice(block * LANES, (block + 1) * LANES)
        for row, value in enumerate(chunks_turned(values, shard_rows)):
            out[row, :, lanes] = mean_of(own[row, :, lanes], value)


def two_steps():
    return dilations + (dilations[0],)


LAYERS_OF = (0, 1, 1, 2, 2, 3)


def two_early(chip, *refs):
    weight_refs, stack_refs = refs[:7], refs[7:]
    _, shard_rows, channels, width = chip.shape
    odd, _ = position()
    steps = two_steps()
    stages = plan(shard_rows, steps)
    weights = Weights(weight_refs, DEPTH, width)
    masks = masks_for(channels, width)
    stacks = [[], [], [], []]
    for ref, index in zip(stack_refs, LAYERS_OF):
        stacks[index].append(Stack([(ref, stages[index].early_low)], stages[index].high, steps[index], masks))
    for row in range(stages[0].high + 1):
        slot = jnp.where(odd == 1, 1 - row // shard_rows, row // shard_rows)
        stacks[0][0].put(row, chip[slot, line_of(row, shard_rows, odd)])
    sources = stacks[0] * 2
    for layer in range(DEPTH):
        stage = stages[layer + 1]

        def store(row, values):
            if layer == DEPTH - 1:
                values = [mean_of(*values)]
            for target, value in zip(stacks[layer + 1], values):
                target.put(row, value)

        block_two(weights, layer, stage, stage.early, range(stage.early_low, stage.high + 1), sources, store)
        sources = stacks[layer + 1]


def two_late(across, *refs):
    kept_refs, weight_refs, out, stack_refs, wide = refs[:6], refs[6:13], refs[13], refs[14:20], refs[20]
    shard_rows, channels, width = across.shape
    odd, edge = position()
    steps = two_steps()
    stages = plan(shard_rows, steps)
    weights = Weights(weight_refs, DEPTH, width)
    masks = masks_for(channels, width)
    stacks = [[], [], [], []]
    for early, late, index in zip(kept_refs, stack_refs, LAYERS_OF):
        stage = stages[index]
        stacks[index].append(Stack([(early, stage.early_low), (late, stage.low)], stage.high, steps[index], masks))
    for row in range(stages[0].low, 0):
        stacks[0][0].put(row, across[line_of(row, shard_rows, odd)])
    sources = stacks[0] * 2
    for layer in range(DEPTH):
        stage = stages[layer + 1]

        def store(row, values):
            if layer == DEPTH - 1:
                values = [mean_of(*values)]
            for target, value in zip(stacks[layer + 1], values):
                if row < 0:
                    value = jnp.where(edge, jnp.zeros_like(value), value)
                target.put(row, value)

        block_two(weights, layer, stage, stage.late, range(stage.low, stage.early_low), sources, store)
        sources = stacks[layer + 1]

    stage = stages[DEPTH + 1]

    def store_last(row, value):
        picked = pl.ds(line_of(row, shard_rows, odd), channels, stride=shard_rows)
        for block in range(width // LANES):
            wide[block, picked, :] = value[:, block * LANES : (block + 1) * LANES]

    block_one(weights, DEPTH, stage, stage.late, range(stage.low, stage.high + 1), sources[0], store_last)
    whole = jnp.concatenate([wide[block] for block in range(width // LANES)], axis=1)
    out[...] = whole.reshape(channels, shard_rows, width).astype(BF16)


VMEM = pl.BlockSpec(memory_space=pltpu.VMEM)
HBM = pl.BlockSpec(memory_space=pltpu.HBM)


class Calls:
    def __init__(self, channels, shard_rows, width, inner, size):
        self.channels, self.shard_rows, self.width, self.inner, self.size = channels, shard_rows, width, inner, size
        self.one = plan(shard_rows, dilations)
        self.two = plan(shard_rows, two_steps())

    def stack(self, low, high):
        return (max(high - low + 1, 1), 3 * self.channels, self.width)

    def early(self, stage):
        return self.stack(stage.early_low, stage.high)

    def late(self, stage):
        return pltpu.VMEM(self.stack(stage.low, stage.early_low - 1), BF16)

    def wide(self, *shards):
        return pltpu.VMEM(shards + (self.width // LANES, self.channels * self.shard_rows, LANES), F32)

    def call(self, body, args, shapes, scratch, specs=None):
        shapes = [shape if isinstance(shape, jax.ShapeDtypeStruct) else jax.ShapeDtypeStruct(shape, BF16) for shape in shapes]
        single = len(shapes) == 1
        return pl.pallas_call(
            body,
            out_shape=shapes[0] if single else shapes,
            in_specs=specs or [VMEM] * len(args),
            out_specs=VMEM if single else [VMEM] * len(shapes),
            scratch_shapes=scratch,
            compiler_params=pltpu.CompilerParams(vmem_limit_bytes=(10 + 6 * self.width // LANES) * 1024 * 1024),
            name=body.__name__,
        )(*args)

    def prepare(self, w_conv, bias_in, w_out, bias_out):
        layers, inner, channels = w_conv.shape[0], self.inner, self.channels

        def banded(steps, count):
            return (sum(1 for step in steps if group_of(step) == count), count * inner, 3 * (count + 2) * channels)

        shapes = [
            banded(layer_steps(), 2), banded(layer_steps(), 4), banded(dilations, 2), banded(dilations, 4),
            (layers, 2 * channels, 2 * inner),
            jax.ShapeDtypeStruct((layers, 4 * inner, LANES), F32),
            jax.ShapeDtypeStruct((layers, 2 * channels, LANES), F32),
        ]
        scratch = [
            pltpu.VMEM(w_conv.shape, BF16), pltpu.VMEM(w_out.shape, BF16),
            pltpu.VMEM(bias_in.shape, F32), pltpu.VMEM(bias_out.shape, F32), pltpu.SemaphoreType.DMA((4,)),
        ]
        args = [pltpu.with_memory_space_constraint(arg, pltpu.HBM) for arg in (w_conv, bias_in, w_out, bias_out)]
        return self.call(
            prepare, args, shapes, scratch, [HBM] * 4
        )

    def one_early(self, *args):
        return self.call(one_early, args, [self.early(stage) for stage in self.one[:DEPTH]], [self.wide(2)])

    def one_late(self, *args):
        shapes = [(self.shard_rows, self.channels, self.width), (self.size, self.channels // 2, LANES)]
        return self.call(one_late, args, shapes, [self.late(stage) for stage in self.one[:DEPTH]] + [self.wide(1)])

    def symmetrize(self, *args):
        return self.call(symmetrize, args, [(self.shard_rows, self.channels, self.width)], [])

    def two_early(self, *args):
        return self.call(two_early, args, [self.early(self.two[index]) for index in LAYERS_OF], [])

    def two_late(self, *args):
        scratch = [self.late(self.two[index]) for index in LAYERS_OF] + [self.wide()]
        return self.call(two_late, args, [(self.channels, self.shard_rows, self.width)], scratch)


def neighbours(array, axis):
    size = lax.axis_size(axis)
    edges = [(i, i + 1) for i in range(1, size - 1, 2)]
    edges = edges + [(j, i) for i, j in edges]
    across = lax.ppermute(array, axis, edges)
    chip = lax.all_gather(array, axis, axis_index_groups=[[i, i + 1] for i in range(0, size, 2)])
    return across, chip


def on_device(features, w_conv, bias_in, w_out, bias_out):
    channels, shard_rows, width = features.shape
    calls = Calls(channels, shard_rows, width, w_conv.shape[2], lax.axis_size("row"))
    across, chip = neighbours(features, "row")
    weights = calls.prepare(w_conv, bias_in, w_out.transpose(0, 2, 1), bias_out)
    kept = calls.one_early(chip, *weights)
    field, tiles = calls.one_late(across, *kept, *weights)
    received = lax.all_to_all(tiles, "row", split_axis=0, concat_axis=0, tiled=True)
    field = calls.symmetrize(received, field)
    across, chip = neighbours(field, "row")
    kept = calls.two_early(chip, *weights)
    return calls.two_late(across, *kept, *weights)


def solution(mesh):
    in_specs = (P("groups", "row", None), P(), P(), P(), P())
    out_specs = P("groups", "row", None)
    return jax.shard_map(
        on_device, mesh=mesh, in_specs=in_specs, out_specs=out_specs, check_vma=False
    )
```

```python
import jax
import jax.numpy as jnp
from jax import lax
from jax.experimental import pallas as pl
from jax.experimental.pallas import tpu as pltpu
from jax.sharding import PartitionSpec as P

SECTIONS = 2
DEPTH = 3

dilations = (1, 2, 4)
LANES = 128
LAG = 3
F32 = jnp.float32
BF16 = jnp.bfloat16


class Stage:
    def __init__(self, dilation, low, high, early_low, late, early):
        self.dilation, self.low, self.high, self.early_low = dilation, low, high, early_low
        self.late, self.early = late, early
        self.keep = ()


def group_of(dilation):
    return 4 if dilation < dilations[-1] else 2


def cover(low, high, limit, dilation):
    covered, starts = set(), []
    count = group_of(dilation)
    for row in range(low, high + 1):
        if row in covered:
            continue
        start = row
        for back in range(count):
            candidate = row - back * dilation
            if candidate >= low and candidate + (count - 1) * dilation <= limit:
                start = candidate
                break
        starts.append(start)
        covered |= {start + step * dilation for step in range(count)}
    return starts, covered


def plan(shard_rows, steps):
    reach = sum(steps)
    ready = 0
    stages = [Stage(0, -reach, shard_rows - 1 + reach, 0, [], [])]
    for dilation in steps:
        reach, ready = reach - dilation, ready + dilation
        low, high = -reach, shard_rows - 1 + reach
        late, covered = cover(low, min(ready - 1, high), high, dilation)
        early_low = low
        while early_low in covered and early_low <= high:
            early_low += 1
        early = cover(early_low, high, high, dilation)[0] if early_low <= high else []
        stage = Stage(dilation, low, high, early_low, late, early)
        need = min(max(covered) + dilation, stages[-1].high)
        stages[-1].keep = tuple(range(stages[-1].early_low, need + 1))
        stages.append(stage)
    return stages


def column_masks(channels, width, dilation):
    column = lax.broadcasted_iota(jnp.int16, (channels, width), 1)
    return column >= jnp.int16(dilation), column < jnp.int16(width - dilation)


class Stack:
    def __init__(self, parts, top, dilation, masks):
        self.parts, self.top, self.dilation, self.masks = parts, top, dilation, masks[dilation]

    def find(self, row):
        for ref, base in self.parts:
            if row >= base:
                return ref, row - base
        raise ValueError(row)

    def put(self, row, value):
        channels, width = value.shape
        ref, index = self.find(row)
        zeros = jnp.zeros_like(value)
        ref[index, :channels, :] = jnp.where(self.masks[0], pltpu.roll(value, self.dilation, 1), zeros)
        ref[index, channels : 2 * channels, :] = value
        ref[index, 2 * channels :, :] = jnp.where(
            self.masks[1], pltpu.roll(value, width - self.dilation, 1), zeros
        )

    def get(self, row, place):
        ref, index = self.find(min(row, self.top))
        channels = ref.shape[1] // 3
        return ref[index, place * channels : (place + 1) * channels, :]

    def window(self, start, taps):
        slabs = []
        for tap in taps:
            ref, index = self.find(min(start + (tap - 1) * self.dilation, self.top))
            slabs.append(ref[index])
        return jnp.concatenate(slabs, axis=0)


def late_groups(stages, layer):
    stage, source = stages[layer + 1], stages[layer]
    count = group_of(stage.dilation) + 2
    groups = {}
    place = 0
    for start in stage.late:
        first = 0
        while first < count and start + (first - 1) * stage.dilation < source.early_low:
            first += 1
        first = min(first + first % 2, count)
        groups[start] = (first, place)
        place += first < count
    return groups, place


def spread_conv(banded, slot, w_conv, layer, turned, odd):
    inner, channels = w_conv.shape[2], w_conv.shape[3]
    count = banded.shape[1] // inner
    zeros = jnp.zeros((inner, channels), BF16)
    taps = []
    for row_tap in range(3):
        line = jnp.where(odd == 1, 2 - row_tap, row_tap)
        for col_tap in range(3):
            taps.append(w_conv[layer, col_tap * 3 + line if turned else line * 3 + col_tap])
    for row in range(count):
        parts = [zeros] * (3 * row) + taps + [zeros] * (3 * (count - 1 - row))
        banded[slot, row * inner : (row + 1) * inner, :] = jnp.concatenate(parts, axis=1)


def spread_out(doubled, slot, w_out, layer):
    block = w_out[layer].astype(F32).T.astype(BF16)
    zeros = jnp.zeros_like(block)
    doubled[slot] = jnp.concatenate(
        [jnp.concatenate([block, zeros], axis=1), jnp.concatenate([zeros, block], axis=1)], axis=0
    )


def as_column(row, copies):
    size = row.shape[1]
    across = lax.broadcasted_iota(jnp.int32, (size, size), 1)
    down = lax.broadcasted_iota(jnp.int32, (size, size), 0)
    spread = jnp.where(across == down, jnp.broadcast_to(row, (size, size)), 0.0)
    column = jnp.sum(spread, axis=1, keepdims=True)
    return jnp.concatenate([column] * copies, axis=0)


def run_block(starts, rows, dilation, hidden_of, finish):
    waiting, done = [], set()

    def complete(start, hidden):
        steps = []
        for step in range(group_of(dilation)):
            row = start + step * dilation
            if row in rows and row not in done:
                steps.append((step, row))
                done.add(row)
        finish(start, hidden, steps)

    for start in starts:
        waiting.append((start, hidden_of(start)))
        if len(waiting) > LAG:
            complete(*waiting.pop(0))
    for item in waiting:
        complete(*item)


def conv_sum(stack, start, kernel, bias, taps):
    slab = stack.parts[0][0].shape[1]
    columns = slice(taps[0] * slab, (taps[-1] + 1) * slab)
    return jnp.dot(kernel[:, columns], stack.window(start, taps), preferred_element_type=F32) + bias


def conv_hidden(stack, start, kernel, bias, groups=None, sums=None):
    count = group_of(stack.dilation) + 2
    first, place = groups[start] if groups else (count, 0)
    if first < count:
        bias = sums[place]
    inner = conv_sum(stack, start, kernel, bias, range(first))
    return jnp.maximum(inner, 0.0).astype(BF16)


def early_sums(stack, kernel, bias, groups, sums):
    count = group_of(stack.dilation) + 2
    for start, (first, place) in groups.items():
        if first < count:
            sums[place] = conv_sum(stack, start, kernel, bias, range(first, count))


def group_rows(stack, start, hidden, kernel, bias):
    half = kernel.shape[1]
    values = []
    for pair in range(hidden.shape[0] // half):
        blended = jnp.dot(kernel, hidden[pair * half : (pair + 1) * half], preferred_element_type=F32)
        residual = [stack.get(start + (2 * pair + step) * stack.dilation, 1).astype(F32) for step in range(2)]
        total = jnp.concatenate(residual, axis=0) + blended + bias
        channels = total.shape[0] // 2
        values += [total[:channels], total[channels:]]
    return values


def fetch(pairs, sems):
    copies = [pltpu.make_async_copy(source, target, sems.at[i]) for i, (source, target) in enumerate(pairs)]
    for copy in copies:
        copy.start()
    return copies


def position():
    device = lax.axis_index("row")
    size = lax.axis_size("row")
    odd = device % 2
    edge = jnp.logical_or(device == 0, device == size - 1)
    return odd, edge


def line_of(row, shard_rows, odd):
    inside = row % shard_rows
    return jnp.where(odd == 1, shard_rows - 1 - inside, inside)


def layer_steps():
    return dilations * SECTIONS + (dilations[0],)


def slot_of(steps, layer):
    return sum(1 for step in steps[:layer] if group_of(step) == group_of(steps[layer]))


def prepare(w_conv, bias_in, w_out, bias_out, small, large, small_turned, large_turned, doubled, bias, bias_last,
            conv, proj, first_bias, last_bias, sems):
    odd, _ = position()
    pairs = [(w_conv, conv), (w_out, proj), (bias_in, first_bias), (bias_out, last_bias)]
    for copy in fetch(pairs, sems):
        copy.wait()
    steps = layer_steps()
    base = len(steps) - 1 - DEPTH
    for layer, step in enumerate(steps):
        spread_conv(small if group_of(step) == 2 else large, slot_of(steps, layer), conv, layer, False, odd)
        spread_out(doubled, layer, proj, layer)
        bias[layer] = jnp.broadcast_to(as_column(first_bias[layer : layer + 1, :], 4), bias.shape[1:])
        bias_last[layer] = jnp.broadcast_to(as_column(last_bias[layer : layer + 1, :], 2), bias_last.shape[1:])
    for layer, step in enumerate(dilations):
        place = small_turned if group_of(step) == 2 else large_turned
        spread_conv(place, slot_of(dilations, layer), conv, base + layer, True, odd)


class Weights:
    def __init__(self, refs, base, width):
        self.refs, self.base, self.blocks = refs, base, width // LANES

    def conv(self, layer):
        steps = layer_steps()
        layer = self.base + layer
        return self.refs[0 if group_of(steps[layer]) == 2 else 1][slot_of(steps, layer)]

    def conv_turned(self, layer):
        return self.refs[2 if group_of(dilations[layer]) == 2 else 3][slot_of(dilations, layer)]

    def out(self, layer):
        return self.refs[4][self.base + layer]

    def bias(self, layer):
        inner = self.refs[5].shape[1] // 4
        rows = group_of(layer_steps()[self.base + layer]) * inner
        return jnp.concatenate([self.refs[5][self.base + layer, :rows]] * self.blocks, axis=1)

    def bias_out(self, layer):
        return jnp.concatenate([self.refs[6][self.base + layer]] * self.blocks, axis=1)


def block_one(weights, layer, stage, starts, rows, source, store, groups=None, sums=None):
    kernel, kernel_out = weights.conv(layer), weights.out(layer)
    bias, bias_out = weights.bias(layer), weights.bias_out(layer)

    def hidden_of(start):
        return conv_hidden(source, start, kernel, bias, groups, sums)

    def finish(start, hidden, steps):
        values = group_rows(source, start, hidden, kernel_out, bias_out)
        for step, row in steps:
            store(row, values[step])

    run_block(starts, rows, stage.dilation, hidden_of, finish)


def block_two(weights, layer, stage, starts, rows, sources, store, groups=None, sums=(None, None)):
    kernels = (weights.conv(layer), weights.conv_turned(layer))
    kernel_out, bias, bias_out = weights.out(layer), weights.bias(layer), weights.bias_out(layer)

    def hidden_of(start):
        if sources[0] is sources[1]:
            both = conv_hidden(
                sources[0], start, jnp.concatenate(kernels, axis=0), jnp.concatenate([bias, bias], axis=0),
                groups, sums[0],
            )
            half = both.shape[0] // 2
            return both[:half], both[half:]
        return tuple(
            conv_hidden(source, start, kernel, bias, groups, part)
            for source, kernel, part in zip(sources, kernels, sums)
        )

    def finish(start, hiddens, steps):
        values = [
            group_rows(source, start, hidden, kernel_out, bias_out)
            for source, hidden in zip(sources, hiddens)
        ]
        for step, row in steps:
            store(row, [value[step].astype(BF16) for value in values])

    run_block(starts, rows, stage.dilation, hidden_of, finish)


def mean_of(first, second):
    return ((first.astype(F32) + second.astype(F32)) * 0.5).astype(BF16)


def masks_for(channels, width):
    return {dilation: column_masks(channels, width, dilation) for dilation in dilations}


def rows_of_raw(shards, count, wide, shard_rows, channels, width):
    for slot in range(count):
        whole = shards[slot][...].astype(F32).reshape(channels * shard_rows, width)
        for block in range(width // LANES):
            wide[slot, block] = whole[:, block * LANES : (block + 1) * LANES]


def raw_row(wide, slot, line, shard_rows, channels, width):
    picked = pl.ds(line, channels, stride=shard_rows)
    parts = [wide[slot, block, picked, :] for block in range(width // LANES)]
    return jnp.concatenate(parts, axis=1).astype(BF16)


def one_early(chip, *refs):
    weight_refs, (stack_0, stack_1, stack_2), sums, wide = refs[:7], refs[7:10], refs[10:13], refs[13]
    _, channels, shard_rows, width = chip.shape
    odd, _ = position()
    stages = plan(shard_rows, dilations)
    weights = Weights(weight_refs, 0, width)
    masks = masks_for(channels, width)
    rows_of_raw(chip, 2, wide, shard_rows, channels, width)
    stacks = [
        Stack([(ref, stage.early_low)], stage.high, dilation, masks)
        for ref, stage, dilation in zip((stack_0, stack_1, stack_2), stages, dilations)
    ]
    for row in range(stages[0].high + 1):
        line = line_of(row, shard_rows, odd)
        slot = jnp.where(odd == 1, 1 - row // shard_rows, row // shard_rows)
        stacks[0].put(row, raw_row(wide, slot, line, shard_rows, channels, width))
    for layer in range(DEPTH - 1):
        stage = stages[layer + 1]

        def store(row, value):
            stacks[layer + 1].put(row, value.astype(BF16))

        block_one(weights, layer, stage, stage.early, range(stage.early_low, stage.high + 1), stacks[layer], store)
    for layer in range(DEPTH):
        groups, _ = late_groups(stages, layer)
        early_sums(stacks[layer], weights.conv(layer), weights.bias(layer), groups, sums[layer])


def chunks_turned(values, lines):
    values = list(values)
    chunk = lax.broadcasted_iota(jnp.int32, values[0].shape, 1) // lines
    for bit in range(3):
        step = 1 << bit
        clear = ((chunk >> bit) & 1) == 0
        for index in range(8):
            if index & step:
                continue
            first, second = values[index], values[index + step]
            values[index] = jnp.where(clear, first, pltpu.roll(second, lines * step, 1))
            values[index + step] = jnp.where(clear, pltpu.roll(first, LANES - lines * step, 1), second)
    return values


def one_late(across, kept_0, kept_1, kept_2, *refs):
    sums, weight_refs, (out, tiles, stack_0, stack_1, stack_2, wide) = refs[:3], refs[3:10], refs[10:]
    channels, shard_rows, width = across.shape
    odd, edge = position()
    stages = plan(shard_rows, dilations)
    weights = Weights(weight_refs, 0, width)
    masks = masks_for(channels, width)
    rows_of_raw([across], 1, wide, shard_rows, channels, width)
    stacks = [
        Stack([(early, stage.early_low), (late, stage.low)], stage.high, dilation, masks)
        for early, late, stage, dilation in zip(
            (kept_0, kept_1, kept_2), (stack_0, stack_1, stack_2), stages, dilations
        )
    ]
    for row in range(stages[0].low, 0):
        stacks[0].put(row, raw_row(wide, 0, line_of(row, shard_rows, odd), shard_rows, channels, width))
    for layer in range(DEPTH):
        stage = stages[layer + 1]

        def store(row, value):
            value = value.astype(BF16)
            if layer == DEPTH - 1:
                out[line_of(row, shard_rows, odd)] = value
                return
            if row < 0:
                value = jnp.where(edge, jnp.zeros_like(value), value)
            stacks[layer + 1].put(row, value)

        groups, _ = late_groups(stages, layer)
        rows = range(stage.low, stage.early_low)
        block_one(weights, layer, stage, stage.late, rows, stacks[layer], store, groups, sums[layer])

    half = channels // 2
    low_lanes = lax.broadcasted_iota(jnp.int32, (half, LANES), 1) < LANES // 2
    for block in range(width // LANES):
        values = [out[row, :, block * LANES : (block + 1) * LANES] for row in range(shard_rows)]
        for index, value in enumerate(chunks_turned(values, shard_rows)):
            top, bottom = value[:half], value[half:]
            device = block * 16 + index
            tiles[device] = jnp.where(low_lanes, top, pltpu.roll(bottom, LANES // 2, 1))
            tiles[device + 8] = jnp.where(low_lanes, pltpu.roll(top, LANES // 2, 1), bottom)


def symmetrize(tiles, own, out):
    shard_rows, channels, width = own.shape
    half = channels // 2
    low_lanes = lax.broadcasted_iota(jnp.int32, (half, LANES), 1) < LANES // 2
    lane_in = lax.broadcasted_iota(jnp.int32, (LANES, LANES), 0)
    lane_out = lax.broadcasted_iota(jnp.int32, (LANES, LANES), 1)
    size = shard_rows
    turned = (lane_out // (size * size)) * (size * size) + (lane_out % size) * size + (lane_out // size) % size
    swap = jnp.where(lane_in == turned, 1.0, 0.0).astype(BF16)
    for block in range(width // LANES):
        values = []
        for index in range(8):
            first, second = tiles[block * 16 + index], tiles[block * 16 + index + 8]
            top = jnp.where(low_lanes, first, pltpu.roll(second, LANES // 2, 1))
            bottom = jnp.where(low_lanes, pltpu.roll(first, LANES // 2, 1), second)
            values += [top, bottom]
        stacked = jnp.concatenate(values, axis=0)
        stacked = jnp.dot(stacked, swap, preferred_element_type=F32).astype(BF16)
        values = [stacked[index * channels : (index + 1) * channels] for index in range(8)]
        lanes = slice(block * LANES, (block + 1) * LANES)
        for row, value in enumerate(chunks_turned(values, shard_rows)):
            out[row, :, lanes] = mean_of(own[row, :, lanes], value)


def two_steps():
    return dilations + (dilations[0],)


LAYERS_OF = (0, 1, 1, 2, 2, 3)
SUMS_OF = (0, 1, 1, 2, 2, 3)


def two_early(chip, *refs):
    weight_refs, stack_refs, sums = refs[:7], refs[7:13], refs[13:]
    _, shard_rows, channels, width = chip.shape
    odd, _ = position()
    steps = two_steps()
    stages = plan(shard_rows, steps)
    weights = Weights(weight_refs, DEPTH, width)
    masks = masks_for(channels, width)
    stacks = [[], [], [], []]
    for ref, index in zip(stack_refs, LAYERS_OF):
        stacks[index].append(Stack([(ref, stages[index].early_low)], stages[index].high, steps[index], masks))
    for row in range(stages[0].high + 1):
        slot = jnp.where(odd == 1, 1 - row // shard_rows, row // shard_rows)
        stacks[0][0].put(row, chip[slot, line_of(row, shard_rows, odd)])
    sources = stacks[0] * 2
    for layer in range(DEPTH):
        stage = stages[layer + 1]

        def store(row, values):
            if layer == DEPTH - 1:
                values = [mean_of(*values)]
            for target, value in zip(stacks[layer + 1], values):
                target.put(row, value)

        block_two(weights, layer, stage, stage.early, range(stage.early_low, stage.high + 1), sources, store)
        sources = stacks[layer + 1]
    for ref, layer, turn in zip(sums, SUMS_OF, (0, 0, 1, 0, 1, 0)):
        groups, _ = late_groups(stages, layer)
        kernel = weights.conv_turned(layer) if turn else weights.conv(layer)
        bias = weights.bias(layer)
        if layer == 0:
            kernel = jnp.concatenate([kernel, weights.conv_turned(layer)], axis=0)
            bias = jnp.concatenate([bias, bias], axis=0)
        early_sums(stacks[layer][turn], kernel, bias, groups, ref)


def two_late(across, *refs):
    kept_refs, sums, weight_refs = refs[:6], refs[6:12], refs[12:19]
    out, stack_refs, wide = refs[19], refs[20:26], refs[26]
    shard_rows, channels, width = across.shape
    odd, edge = position()
    steps = two_steps()
    stages = plan(shard_rows, steps)
    weights = Weights(weight_refs, DEPTH, width)
    masks = masks_for(channels, width)
    stacks = [[], [], [], []]
    for early, late, index in zip(kept_refs, stack_refs, LAYERS_OF):
        stage = stages[index]
        stacks[index].append(Stack([(early, stage.early_low), (late, stage.low)], stage.high, steps[index], masks))
    for row in range(stages[0].low, 0):
        stacks[0][0].put(row, across[line_of(row, shard_rows, odd)])
    sources = stacks[0] * 2
    for layer in range(DEPTH):
        stage = stages[layer + 1]

        def store(row, values):
            if layer == DEPTH - 1:
                values = [mean_of(*values)]
            for target, value in zip(stacks[layer + 1], values):
                if row < 0:
                    value = jnp.where(edge, jnp.zeros_like(value), value)
                target.put(row, value)

        groups, _ = late_groups(stages, layer)
        parts = [ref for ref, place in zip(sums, SUMS_OF) if place == layer]
        block_two(
            weights, layer, stage, stage.late, range(stage.low, stage.early_low), sources, store, groups,
            parts if len(parts) == 2 else parts * 2,
        )
        sources = stacks[layer + 1]

    stage = stages[DEPTH + 1]

    def store_last(row, value):
        picked = pl.ds(line_of(row, shard_rows, odd), channels, stride=shard_rows)
        for block in range(width // LANES):
            wide[block, picked, :] = value[:, block * LANES : (block + 1) * LANES]

    groups, _ = late_groups(stages, DEPTH)
    rows = range(stage.low, stage.high + 1)
    block_one(weights, DEPTH, stage, stage.late, rows, sources[0], store_last, groups, sums[-1])
    whole = jnp.concatenate([wide[block] for block in range(width // LANES)], axis=1)
    out[...] = whole.reshape(channels, shard_rows, width).astype(BF16)


VMEM = pl.BlockSpec(memory_space=pltpu.VMEM)
HBM = pl.BlockSpec(memory_space=pltpu.HBM)


class Calls:
    def __init__(self, channels, shard_rows, width, inner, size):
        self.channels, self.shard_rows, self.width, self.inner, self.size = channels, shard_rows, width, inner, size
        self.one = plan(shard_rows, dilations)
        self.two = plan(shard_rows, two_steps())

    def stack(self, low, high):
        return (max(high - low + 1, 1), 3 * self.channels, self.width)

    def early(self, stage):
        return self.stack(stage.early_low, stage.high)

    def late(self, stage):
        return pltpu.VMEM(self.stack(stage.low, stage.early_low - 1), BF16)

    def sums(self, stages, layer, copies=1):
        rows = copies * group_of(stages[layer + 1].dilation) * self.inner
        return jax.ShapeDtypeStruct((max(late_groups(stages, layer)[1], 1), rows, self.width), F32)

    def wide(self, *shards):
        return pltpu.VMEM(shards + (self.width // LANES, self.channels * self.shard_rows, LANES), F32)

    def call(self, body, args, shapes, scratch, specs=None):
        shapes = [shape if isinstance(shape, jax.ShapeDtypeStruct) else jax.ShapeDtypeStruct(shape, BF16) for shape in shapes]
        single = len(shapes) == 1
        return pl.pallas_call(
            body,
            out_shape=shapes[0] if single else shapes,
            in_specs=specs or [VMEM] * len(args),
            out_specs=VMEM if single else [VMEM] * len(shapes),
            scratch_shapes=scratch,
            compiler_params=pltpu.CompilerParams(vmem_limit_bytes=(10 + 6 * self.width // LANES) * 1024 * 1024),
            name=body.__name__,
        )(*args)

    def prepare(self, w_conv, bias_in, w_out, bias_out):
        layers, inner, channels = w_conv.shape[0], self.inner, self.channels

        def banded(steps, count):
            return (sum(1 for step in steps if group_of(step) == count), count * inner, 3 * (count + 2) * channels)

        shapes = [
            banded(layer_steps(), 2), banded(layer_steps(), 4), banded(dilations, 2), banded(dilations, 4),
            (layers, 2 * channels, 2 * inner),
            jax.ShapeDtypeStruct((layers, 4 * inner, LANES), F32),
            jax.ShapeDtypeStruct((layers, 2 * channels, LANES), F32),
        ]
        scratch = [
            pltpu.VMEM(w_conv.shape, BF16), pltpu.VMEM(w_out.shape, BF16),
            pltpu.VMEM(bias_in.shape, F32), pltpu.VMEM(bias_out.shape, F32), pltpu.SemaphoreType.DMA((4,)),
        ]
        args = [pltpu.with_memory_space_constraint(arg, pltpu.HBM) for arg in (w_conv, bias_in, w_out, bias_out)]
        return self.call(
            prepare, args, shapes, scratch, [HBM] * 4
        )

    def one_early(self, *args):
        shapes = [self.early(stage) for stage in self.one[:DEPTH]]
        shapes += [self.sums(self.one, layer) for layer in range(DEPTH)]
        return self.call(one_early, args, shapes, [self.wide(2)])

    def one_late(self, *args):
        shapes = [(self.shard_rows, self.channels, self.width), (self.size, self.channels // 2, LANES)]
        return self.call(one_late, args, shapes, [self.late(stage) for stage in self.one[:DEPTH]] + [self.wide(1)])

    def symmetrize(self, *args):
        return self.call(symmetrize, args, [(self.shard_rows, self.channels, self.width)], [])

    def two_early(self, *args):
        shapes = [self.early(self.two[index]) for index in LAYERS_OF]
        shapes += [self.sums(self.two, layer, 2 if layer == 0 else 1) for layer in SUMS_OF]
        return self.call(two_early, args, shapes, [])

    def two_late(self, *args):
        scratch = [self.late(self.two[index]) for index in LAYERS_OF] + [self.wide()]
        return self.call(two_late, args, [(self.channels, self.shard_rows, self.width)], scratch)


def neighbours(array, axis):
    size = lax.axis_size(axis)
    edges = [(i, i + 1) for i in range(1, size - 1, 2)]
    edges = edges + [(j, i) for i, j in edges]
    across = lax.ppermute(array, axis, edges)
    chip = lax.all_gather(array, axis, axis_index_groups=[[i, i + 1] for i in range(0, size, 2)])
    return across, chip


def on_device(features, w_conv, bias_in, w_out, bias_out):
    channels, shard_rows, width = features.shape
    calls = Calls(channels, shard_rows, width, w_conv.shape[2], lax.axis_size("row"))
    across, chip = neighbours(features, "row")
    weights = calls.prepare(w_conv, bias_in, w_out.transpose(0, 2, 1), bias_out)
    kept = calls.one_early(chip, *weights)
    field, tiles = calls.one_late(across, *kept, *weights)
    received = lax.all_to_all(tiles, "row", split_axis=0, concat_axis=0, tiled=True)
    field = calls.symmetrize(received, field)
    across, chip = neighbours(field, "row")
    kept = calls.two_early(chip, *weights)
    return calls.two_late(across, *kept, *weights)


def solution(mesh):
    in_specs = (P("groups", "row", None), P(), P(), P(), P())
    out_specs = P("groups", "row", None)
    return jax.shard_map(
        on_device, mesh=mesh, in_specs=in_specs, out_specs=out_specs, check_vma=False
    )
```

```python
import jax
import jax.numpy as jnp
from jax import lax
from jax.experimental import pallas as pl
from jax.experimental.pallas import tpu as pltpu
from jax.sharding import PartitionSpec as P

SECTIONS = 2
DEPTH = 3

dilations = (1, 2, 4)
LANES = 128
LAG = 3
F32 = jnp.float32
BF16 = jnp.bfloat16


class Stage:
    def __init__(self, dilation, low, high, early_low, late, early):
        self.dilation, self.low, self.high, self.early_low = dilation, low, high, early_low
        self.late, self.early = late, early
        self.keep = ()


def group_of(dilation):
    return 4 if dilation == dilations[1] else 2


def cover(low, high, limit, dilation):
    covered, starts = set(), []
    count = group_of(dilation)
    for row in range(low, high + 1):
        if row in covered:
            continue
        start = row
        for back in range(count):
            candidate = row - back * dilation
            if candidate >= low and candidate + (count - 1) * dilation <= limit:
                start = candidate
                break
        starts.append(start)
        covered |= {start + step * dilation for step in range(count)}
    return starts, covered


def plan(shard_rows, steps):
    reach = sum(steps)
    ready = 0
    stages = [Stage(0, -reach, shard_rows - 1 + reach, 0, [], [])]
    for dilation in steps:
        reach, ready = reach - dilation, ready + dilation
        low, high = -reach, shard_rows - 1 + reach
        late, covered = cover(low, min(ready - 1, high), high, dilation)
        early_low = low
        while early_low in covered and early_low <= high:
            early_low += 1
        early = cover(early_low, high, high, dilation)[0] if early_low <= high else []
        stage = Stage(dilation, low, high, early_low, late, early)
        need = min(max(covered) + dilation, stages[-1].high)
        stages[-1].keep = tuple(range(stages[-1].early_low, need + 1))
        stages.append(stage)
    return stages


def column_masks(channels, width, dilation):
    column = lax.broadcasted_iota(jnp.int16, (channels, width), 1)
    return column >= jnp.int16(dilation), column < jnp.int16(width - dilation)


class Stack:
    def __init__(self, parts, top, dilation, masks):
        self.parts, self.top, self.dilation, self.masks = parts, top, dilation, masks[dilation]

    def find(self, row):
        for ref, base in self.parts:
            if row >= base:
                return ref, row - base
        raise ValueError(row)

    def put(self, row, value):
        channels, width = value.shape
        ref, index = self.find(row)
        zeros = jnp.zeros_like(value)
        ref[index, :channels, :] = jnp.where(self.masks[0], pltpu.roll(value, self.dilation, 1), zeros)
        ref[index, channels : 2 * channels, :] = value
        ref[index, 2 * channels :, :] = jnp.where(
            self.masks[1], pltpu.roll(value, width - self.dilation, 1), zeros
        )

    def get(self, row, place):
        ref, index = self.find(min(row, self.top))
        channels = ref.shape[1] // 3
        return ref[index, place * channels : (place + 1) * channels, :]

    def window(self, start, taps):
        slabs = []
        for tap in taps:
            ref, index = self.find(min(start + (tap - 1) * self.dilation, self.top))
            slabs.append(ref[index])
        return jnp.concatenate(slabs, axis=0)


def late_groups(stages, layer):
    stage, source = stages[layer + 1], stages[layer]
    count = group_of(stage.dilation) + 2
    groups = {}
    place = 0
    for start in stage.late:
        first = 0
        while first < count and start + (first - 1) * stage.dilation < source.early_low:
            first += 1
        first = min(first + first % 2, count)
        groups[start] = (first, place)
        place += first < count
    return groups, place


def spread_conv(banded, slot, w_conv, layer, turned, odd):
    inner, channels = w_conv.shape[2], w_conv.shape[3]
    count = banded.shape[1] // inner
    zeros = jnp.zeros((inner, channels), BF16)
    taps = []
    for row_tap in range(3):
        line = jnp.where(odd == 1, 2 - row_tap, row_tap)
        for col_tap in range(3):
            taps.append(w_conv[layer, col_tap * 3 + line if turned else line * 3 + col_tap])
    for row in range(count):
        parts = [zeros] * (3 * row) + taps + [zeros] * (3 * (count - 1 - row))
        banded[slot, row * inner : (row + 1) * inner, :] = jnp.concatenate(parts, axis=1)


def spread_out(doubled, slot, w_out, layer):
    block = w_out[layer].astype(F32).T.astype(BF16)
    zeros = jnp.zeros_like(block)
    doubled[slot] = jnp.concatenate(
        [jnp.concatenate([block, zeros], axis=1), jnp.concatenate([zeros, block], axis=1)], axis=0
    )


def as_column(row, copies):
    size = row.shape[1]
    across = lax.broadcasted_iota(jnp.int32, (size, size), 1)
    down = lax.broadcasted_iota(jnp.int32, (size, size), 0)
    spread = jnp.where(across == down, jnp.broadcast_to(row, (size, size)), 0.0)
    column = jnp.sum(spread, axis=1, keepdims=True)
    return jnp.concatenate([column] * copies, axis=0)


def run_block(starts, rows, dilation, hidden_of, finish):
    waiting, done = [], set()

    def complete(start, hidden):
        steps = []
        for step in range(group_of(dilation)):
            row = start + step * dilation
            if row in rows and row not in done:
                steps.append((step, row))
                done.add(row)
        finish(start, hidden, steps)

    for start in starts:
        waiting.append((start, hidden_of(start)))
        if len(waiting) > LAG:
            complete(*waiting.pop(0))
    for item in waiting:
        complete(*item)


def conv_sum(stack, start, kernel, bias, taps):
    slab = stack.parts[0][0].shape[1]
    columns = slice(taps[0] * slab, (taps[-1] + 1) * slab)
    return jnp.dot(kernel[:, columns], stack.window(start, taps), preferred_element_type=F32) + bias


def conv_hidden(stack, start, kernel, bias, groups=None, sums=None):
    count = group_of(stack.dilation) + 2
    first, place = groups[start] if groups else (count, 0)
    if first < count:
        bias = sums[place]
    inner = conv_sum(stack, start, kernel, bias, range(first))
    return jnp.maximum(inner, 0.0).astype(BF16)


def early_sums(stack, kernel, bias, groups, sums):
    count = group_of(stack.dilation) + 2
    for start, (first, place) in groups.items():
        if first < count:
            sums[place] = conv_sum(stack, start, kernel, bias, range(first, count))


def group_rows(stack, start, hidden, kernel, bias):
    half = kernel.shape[1]
    values = []
    for pair in range(hidden.shape[0] // half):
        blended = jnp.dot(kernel, hidden[pair * half : (pair + 1) * half], preferred_element_type=F32)
        residual = [stack.get(start + (2 * pair + step) * stack.dilation, 1).astype(F32) for step in range(2)]
        total = jnp.concatenate(residual, axis=0) + blended + bias
        channels = total.shape[0] // 2
        values += [total[:channels], total[channels:]]
    return values


def fetch(pairs, sems):
    copies = [pltpu.make_async_copy(source, target, sems.at[i]) for i, (source, target) in enumerate(pairs)]
    for copy in copies:
        copy.start()
    return copies


def position():
    device = lax.axis_index("row")
    size = lax.axis_size("row")
    odd = device % 2
    edge = jnp.logical_or(device == 0, device == size - 1)
    return odd, edge


def line_of(row, shard_rows, odd):
    inside = row % shard_rows
    return jnp.where(odd == 1, shard_rows - 1 - inside, inside)


def layer_steps():
    return dilations * SECTIONS + (dilations[0],)


def slot_of(steps, layer):
    return sum(1 for step in steps[:layer] if group_of(step) == group_of(steps[layer]))


def prepare(w_conv, bias_in, w_out, bias_out, small, large, small_turned, large_turned, doubled, bias, bias_last,
            conv, proj, first_bias, last_bias, sems):
    odd, _ = position()
    pairs = [(w_conv, conv), (w_out, proj), (bias_in, first_bias), (bias_out, last_bias)]
    for copy in fetch(pairs, sems):
        copy.wait()
    steps = layer_steps()
    base = len(steps) - 1 - DEPTH
    for layer, step in enumerate(steps):
        spread_conv(small if group_of(step) == 2 else large, slot_of(steps, layer), conv, layer, False, odd)
        spread_out(doubled, layer, proj, layer)
        bias[layer] = jnp.broadcast_to(as_column(first_bias[layer : layer + 1, :], 4), bias.shape[1:])
        bias_last[layer] = jnp.broadcast_to(as_column(last_bias[layer : layer + 1, :], 2), bias_last.shape[1:])
    for layer, step in enumerate(dilations):
        place = small_turned if group_of(step) == 2 else large_turned
        spread_conv(place, slot_of(dilations, layer), conv, base + layer, True, odd)


class Weights:
    def __init__(self, refs, base, width):
        self.refs, self.base, self.blocks = refs, base, width // LANES

    def conv(self, layer):
        steps = layer_steps()
        layer = self.base + layer
        return self.refs[0 if group_of(steps[layer]) == 2 else 1][slot_of(steps, layer)]

    def conv_turned(self, layer):
        return self.refs[2 if group_of(dilations[layer]) == 2 else 3][slot_of(dilations, layer)]

    def out(self, layer):
        return self.refs[4][self.base + layer]

    def bias(self, layer):
        inner = self.refs[5].shape[1] // 4
        rows = group_of(layer_steps()[self.base + layer]) * inner
        return jnp.concatenate([self.refs[5][self.base + layer, :rows]] * self.blocks, axis=1)

    def bias_out(self, layer):
        return jnp.concatenate([self.refs[6][self.base + layer]] * self.blocks, axis=1)


def block_one(weights, layer, stage, starts, rows, source, store, groups=None, sums=None):
    kernel, kernel_out = weights.conv(layer), weights.out(layer)
    bias, bias_out = weights.bias(layer), weights.bias_out(layer)

    def hidden_of(start):
        return conv_hidden(source, start, kernel, bias, groups, sums)

    def finish(start, hidden, steps):
        values = group_rows(source, start, hidden, kernel_out, bias_out)
        for step, row in steps:
            store(row, values[step])

    run_block(starts, rows, stage.dilation, hidden_of, finish)


def block_two(weights, layer, stage, starts, rows, sources, store, groups=None, sums=(None, None)):
    kernels = (weights.conv(layer), weights.conv_turned(layer))
    kernel_out, bias, bias_out = weights.out(layer), weights.bias(layer), weights.bias_out(layer)

    def hidden_of(start):
        if sources[0] is sources[1]:
            both = conv_hidden(
                sources[0], start, jnp.concatenate(kernels, axis=0), jnp.concatenate([bias, bias], axis=0),
                groups, sums[0],
            )
            half = both.shape[0] // 2
            return both[:half], both[half:]
        return tuple(
            conv_hidden(source, start, kernel, bias, groups, part)
            for source, kernel, part in zip(sources, kernels, sums)
        )

    def finish(start, hiddens, steps):
        values = [
            group_rows(source, start, hidden, kernel_out, bias_out)
            for source, hidden in zip(sources, hiddens)
        ]
        for step, row in steps:
            store(row, [value[step].astype(BF16) for value in values])

    run_block(starts, rows, stage.dilation, hidden_of, finish)


def mean_of(first, second):
    return ((first.astype(F32) + second.astype(F32)) * 0.5).astype(BF16)


def masks_for(channels, width):
    return {dilation: column_masks(channels, width, dilation) for dilation in dilations}


def rows_of_raw(shards, count, wide, shard_rows, channels, width):
    for slot in range(count):
        whole = shards[slot][...].astype(F32).reshape(channels * shard_rows, width)
        for block in range(width // LANES):
            wide[slot, block] = whole[:, block * LANES : (block + 1) * LANES]


def raw_row(wide, slot, line, shard_rows, channels, width):
    picked = pl.ds(line, channels, stride=shard_rows)
    parts = [wide[slot, block, picked, :] for block in range(width // LANES)]
    return jnp.concatenate(parts, axis=1).astype(BF16)


def one_early(chip, *refs):
    weight_refs, (stack_0, stack_1, stack_2), sums, wide = refs[:7], refs[7:10], refs[10:13], refs[13]
    _, channels, shard_rows, width = chip.shape
    odd, _ = position()
    stages = plan(shard_rows, dilations)
    weights = Weights(weight_refs, 0, width)
    masks = masks_for(channels, width)
    rows_of_raw(chip, 2, wide, shard_rows, channels, width)
    stacks = [
        Stack([(ref, stage.early_low)], stage.high, dilation, masks)
        for ref, stage, dilation in zip((stack_0, stack_1, stack_2), stages, dilations)
    ]
    for row in range(stages[0].high + 1):
        line = line_of(row, shard_rows, odd)
        slot = jnp.where(odd == 1, 1 - row // shard_rows, row // shard_rows)
        stacks[0].put(row, raw_row(wide, slot, line, shard_rows, channels, width))
    for layer in range(DEPTH - 1):
        stage = stages[layer + 1]

        def store(row, value):
            stacks[layer + 1].put(row, value.astype(BF16))

        block_one(weights, layer, stage, stage.early, range(stage.early_low, stage.high + 1), stacks[layer], store)
    for layer in range(DEPTH):
        groups, _ = late_groups(stages, layer)
        early_sums(stacks[layer], weights.conv(layer), weights.bias(layer), groups, sums[layer])


def chunks_turned(values, lines):
    values = list(values)
    chunk = lax.broadcasted_iota(jnp.int32, values[0].shape, 1) // lines
    for bit in range(3):
        step = 1 << bit
        clear = ((chunk >> bit) & 1) == 0
        for index in range(8):
            if index & step:
                continue
            first, second = values[index], values[index + step]
            values[index] = jnp.where(clear, first, pltpu.roll(second, lines * step, 1))
            values[index + step] = jnp.where(clear, pltpu.roll(first, LANES - lines * step, 1), second)
    return values


def one_late(across, kept_0, kept_1, kept_2, *refs):
    sums, weight_refs, (out, tiles, stack_0, stack_1, stack_2, wide) = refs[:3], refs[3:10], refs[10:]
    channels, shard_rows, width = across.shape
    odd, edge = position()
    stages = plan(shard_rows, dilations)
    weights = Weights(weight_refs, 0, width)
    masks = masks_for(channels, width)
    rows_of_raw([across], 1, wide, shard_rows, channels, width)
    stacks = [
        Stack([(early, stage.early_low), (late, stage.low)], stage.high, dilation, masks)
        for early, late, stage, dilation in zip(
            (kept_0, kept_1, kept_2), (stack_0, stack_1, stack_2), stages, dilations
        )
    ]
    for row in range(stages[0].low, 0):
        stacks[0].put(row, raw_row(wide, 0, line_of(row, shard_rows, odd), shard_rows, channels, width))
    for layer in range(DEPTH):
        stage = stages[layer + 1]

        def store(row, value):
            value = value.astype(BF16)
            if layer == DEPTH - 1:
                out[line_of(row, shard_rows, odd)] = value
                return
            if row < 0:
                value = jnp.where(edge, jnp.zeros_like(value), value)
            stacks[layer + 1].put(row, value)

        groups, _ = late_groups(stages, layer)
        rows = range(stage.low, stage.early_low)
        block_one(weights, layer, stage, stage.late, rows, stacks[layer], store, groups, sums[layer])

    half = channels // 2
    low_lanes = lax.broadcasted_iota(jnp.int32, (half, LANES), 1) < LANES // 2
    for block in range(width // LANES):
        values = [out[row, :, block * LANES : (block + 1) * LANES] for row in range(shard_rows)]
        for index, value in enumerate(chunks_turned(values, shard_rows)):
            top, bottom = value[:half], value[half:]
            device = block * 16 + index
            tiles[device] = jnp.where(low_lanes, top, pltpu.roll(bottom, LANES // 2, 1))
            tiles[device + 8] = jnp.where(low_lanes, pltpu.roll(top, LANES // 2, 1), bottom)


def symmetrize(tiles, own, out):
    shard_rows, channels, width = own.shape
    half = channels // 2
    low_lanes = lax.broadcasted_iota(jnp.int32, (half, LANES), 1) < LANES // 2
    lane_in = lax.broadcasted_iota(jnp.int32, (LANES, LANES), 0)
    lane_out = lax.broadcasted_iota(jnp.int32, (LANES, LANES), 1)
    size = shard_rows
    turned = (lane_out // (size * size)) * (size * size) + (lane_out % size) * size + (lane_out // size) % size
    swap = jnp.where(lane_in == turned, 1.0, 0.0).astype(BF16)
    for block in range(width // LANES):
        values = []
        for index in range(8):
            first, second = tiles[block * 16 + index], tiles[block * 16 + index + 8]
            top = jnp.where(low_lanes, first, pltpu.roll(second, LANES // 2, 1))
            bottom = jnp.where(low_lanes, pltpu.roll(first, LANES // 2, 1), second)
            values += [top, bottom]
        stacked = jnp.concatenate(values, axis=0)
        stacked = jnp.dot(stacked, swap, preferred_element_type=F32).astype(BF16)
        values = [stacked[index * channels : (index + 1) * channels] for index in range(8)]
        lanes = slice(block * LANES, (block + 1) * LANES)
        for row, value in enumerate(chunks_turned(values, shard_rows)):
            out[row, :, lanes] = mean_of(own[row, :, lanes], value)


def two_steps():
    return dilations + (dilations[0],)


LAYERS_OF = (0, 1, 1, 2, 2, 3)
SUMS_OF = (0, 1, 1, 2, 2, 3)


def two_early(chip, *refs):
    weight_refs, stack_refs, sums = refs[:7], refs[7:13], refs[13:]
    _, shard_rows, channels, width = chip.shape
    odd, _ = position()
    steps = two_steps()
    stages = plan(shard_rows, steps)
    weights = Weights(weight_refs, DEPTH, width)
    masks = masks_for(channels, width)
    stacks = [[], [], [], []]
    for ref, index in zip(stack_refs, LAYERS_OF):
        stacks[index].append(Stack([(ref, stages[index].early_low)], stages[index].high, steps[index], masks))
    for row in range(stages[0].high + 1):
        slot = jnp.where(odd == 1, 1 - row // shard_rows, row // shard_rows)
        stacks[0][0].put(row, chip[slot, line_of(row, shard_rows, odd)])
    sources = stacks[0] * 2
    for layer in range(DEPTH):
        stage = stages[layer + 1]

        def store(row, values):
            if layer == DEPTH - 1:
                values = [mean_of(*values)]
            for target, value in zip(stacks[layer + 1], values):
                target.put(row, value)

        block_two(weights, layer, stage, stage.early, range(stage.early_low, stage.high + 1), sources, store)
        sources = stacks[layer + 1]
    for ref, layer, turn in zip(sums, SUMS_OF, (0, 0, 1, 0, 1, 0)):
        groups, _ = late_groups(stages, layer)
        kernel = weights.conv_turned(layer) if turn else weights.conv(layer)
        bias = weights.bias(layer)
        if layer == 0:
            kernel = jnp.concatenate([kernel, weights.conv_turned(layer)], axis=0)
            bias = jnp.concatenate([bias, bias], axis=0)
        early_sums(stacks[layer][turn], kernel, bias, groups, ref)


def two_late(across, *refs):
    kept_refs, sums, weight_refs = refs[:6], refs[6:12], refs[12:19]
    out, stack_refs, wide = refs[19], refs[20:26], refs[26]
    shard_rows, channels, width = across.shape
    odd, edge = position()
    steps = two_steps()
    stages = plan(shard_rows, steps)
    weights = Weights(weight_refs, DEPTH, width)
    masks = masks_for(channels, width)
    stacks = [[], [], [], []]
    for early, late, index in zip(kept_refs, stack_refs, LAYERS_OF):
        stage = stages[index]
        stacks[index].append(Stack([(early, stage.early_low), (late, stage.low)], stage.high, steps[index], masks))
    for row in range(stages[0].low, 0):
        stacks[0][0].put(row, across[line_of(row, shard_rows, odd)])
    sources = stacks[0] * 2
    for layer in range(DEPTH):
        stage = stages[layer + 1]

        def store(row, values):
            if layer == DEPTH - 1:
                values = [mean_of(*values)]
            for target, value in zip(stacks[layer + 1], values):
                if row < 0:
                    value = jnp.where(edge, jnp.zeros_like(value), value)
                target.put(row, value)

        groups, _ = late_groups(stages, layer)
        parts = [ref for ref, place in zip(sums, SUMS_OF) if place == layer]
        block_two(
            weights, layer, stage, stage.late, range(stage.low, stage.early_low), sources, store, groups,
            parts if len(parts) == 2 else parts * 2,
        )
        sources = stacks[layer + 1]

    stage = stages[DEPTH + 1]

    def store_last(row, value):
        picked = pl.ds(line_of(row, shard_rows, odd), channels, stride=shard_rows)
        for block in range(width // LANES):
            wide[block, picked, :] = value[:, block * LANES : (block + 1) * LANES]

    groups, _ = late_groups(stages, DEPTH)
    rows = range(stage.low, stage.high + 1)
    block_one(weights, DEPTH, stage, stage.late, rows, sources[0], store_last, groups, sums[-1])
    whole = jnp.concatenate([wide[block] for block in range(width // LANES)], axis=1)
    out[...] = whole.reshape(channels, shard_rows, width).astype(BF16)


VMEM = pl.BlockSpec(memory_space=pltpu.VMEM)
HBM = pl.BlockSpec(memory_space=pltpu.HBM)


class Calls:
    def __init__(self, channels, shard_rows, width, inner, size):
        self.channels, self.shard_rows, self.width, self.inner, self.size = channels, shard_rows, width, inner, size
        self.one = plan(shard_rows, dilations)
        self.two = plan(shard_rows, two_steps())

    def stack(self, low, high):
        return (max(high - low + 1, 1), 3 * self.channels, self.width)

    def early(self, stage):
        return self.stack(stage.early_low, stage.high)

    def late(self, stage):
        return pltpu.VMEM(self.stack(stage.low, stage.early_low - 1), BF16)

    def sums(self, stages, layer, copies=1):
        rows = copies * group_of(stages[layer + 1].dilation) * self.inner
        return jax.ShapeDtypeStruct((max(late_groups(stages, layer)[1], 1), rows, self.width), F32)

    def wide(self, *shards):
        return pltpu.VMEM(shards + (self.width // LANES, self.channels * self.shard_rows, LANES), F32)

    def call(self, body, args, shapes, scratch, specs=None):
        shapes = [shape if isinstance(shape, jax.ShapeDtypeStruct) else jax.ShapeDtypeStruct(shape, BF16) for shape in shapes]
        single = len(shapes) == 1
        return pl.pallas_call(
            body,
            out_shape=shapes[0] if single else shapes,
            in_specs=specs or [VMEM] * len(args),
            out_specs=VMEM if single else [VMEM] * len(shapes),
            scratch_shapes=scratch,
            compiler_params=pltpu.CompilerParams(vmem_limit_bytes=(10 + 6 * self.width // LANES) * 1024 * 1024),
            name=body.__name__,
        )(*args)

    def prepare(self, w_conv, bias_in, w_out, bias_out):
        layers, inner, channels = w_conv.shape[0], self.inner, self.channels

        def banded(steps, count):
            return (sum(1 for step in steps if group_of(step) == count), count * inner, 3 * (count + 2) * channels)

        shapes = [
            banded(layer_steps(), 2), banded(layer_steps(), 4), banded(dilations, 2), banded(dilations, 4),
            (layers, 2 * channels, 2 * inner),
            jax.ShapeDtypeStruct((layers, 4 * inner, LANES), F32),
            jax.ShapeDtypeStruct((layers, 2 * channels, LANES), F32),
        ]
        scratch = [
            pltpu.VMEM(w_conv.shape, BF16), pltpu.VMEM(w_out.shape, BF16),
            pltpu.VMEM(bias_in.shape, F32), pltpu.VMEM(bias_out.shape, F32), pltpu.SemaphoreType.DMA((4,)),
        ]
        args = [pltpu.with_memory_space_constraint(arg, pltpu.HBM) for arg in (w_conv, bias_in, w_out, bias_out)]
        return self.call(
            prepare, args, shapes, scratch, [HBM] * 4
        )

    def one_early(self, *args):
        shapes = [self.early(stage) for stage in self.one[:DEPTH]]
        shapes += [self.sums(self.one, layer) for layer in range(DEPTH)]
        return self.call(one_early, args, shapes, [self.wide(2)])

    def one_late(self, *args):
        shapes = [(self.shard_rows, self.channels, self.width), (self.size, self.channels // 2, LANES)]
        return self.call(one_late, args, shapes, [self.late(stage) for stage in self.one[:DEPTH]] + [self.wide(1)])

    def symmetrize(self, *args):
        return self.call(symmetrize, args, [(self.shard_rows, self.channels, self.width)], [])

    def two_early(self, *args):
        shapes = [self.early(self.two[index]) for index in LAYERS_OF]
        shapes += [self.sums(self.two, layer, 2 if layer == 0 else 1) for layer in SUMS_OF]
        return self.call(two_early, args, shapes, [])

    def two_late(self, *args):
        scratch = [self.late(self.two[index]) for index in LAYERS_OF] + [self.wide()]
        return self.call(two_late, args, [(self.channels, self.shard_rows, self.width)], scratch)


def neighbours(array, axis):
    size = lax.axis_size(axis)
    edges = [(i, i + 1) for i in range(1, size - 1, 2)]
    edges = edges + [(j, i) for i, j in edges]
    across = lax.ppermute(array, axis, edges)
    chip = lax.all_gather(array, axis, axis_index_groups=[[i, i + 1] for i in range(0, size, 2)])
    return across, chip


def on_device(features, w_conv, bias_in, w_out, bias_out):
    channels, shard_rows, width = features.shape
    calls = Calls(channels, shard_rows, width, w_conv.shape[2], lax.axis_size("row"))
    across, chip = neighbours(features, "row")
    weights = calls.prepare(w_conv, bias_in, w_out.transpose(0, 2, 1), bias_out)
    kept = calls.one_early(chip, *weights)
    field, tiles = calls.one_late(across, *kept, *weights)
    received = lax.all_to_all(tiles, "row", split_axis=0, concat_axis=0, tiled=True)
    field = calls.symmetrize(received, field)
    across, chip = neighbours(field, "row")
    kept = calls.two_early(chip, *weights)
    return calls.two_late(across, *kept, *weights)


def solution(mesh):
    in_specs = (P("groups", "row", None), P(), P(), P(), P())
    out_specs = P("groups", "row", None)
    return jax.shard_map(
        on_device, mesh=mesh, in_specs=in_specs, out_specs=out_specs, check_vma=False
    )
```

```python
import jax
import jax.numpy as jnp
from jax import lax
from jax.experimental import pallas as pl
from jax.experimental.pallas import tpu as pltpu
from jax.sharding import PartitionSpec as P

SECTIONS = 2
DEPTH = 3

dilations = (1, 2, 4)
LANES = 128
LAG = 3
F32 = jnp.float32
BF16 = jnp.bfloat16


class Stage:
    def __init__(self, dilation, low, high, early_low, late, early):
        self.dilation, self.low, self.high, self.early_low = dilation, low, high, early_low
        self.late, self.early = late, early
        self.keep = ()


def group_of(dilation):
    return 4 if dilation == dilations[1] else 2


def cover(low, high, limit, dilation):
    covered, starts = set(), []
    count = group_of(dilation)
    for row in range(low, high + 1):
        if row in covered:
            continue
        start = row
        for back in range(count):
            candidate = row - back * dilation
            if candidate >= low and candidate + (count - 1) * dilation <= limit:
                start = candidate
                break
        starts.append(start)
        covered |= {start + step * dilation for step in range(count)}
    return starts, covered


def plan(shard_rows, steps):
    reach = sum(steps)
    ready = 0
    stages = [Stage(0, -reach, shard_rows - 1 + reach, 0, [], [])]
    for dilation in steps:
        reach, ready = reach - dilation, ready + dilation
        low, high = -reach, shard_rows - 1 + reach
        late, covered = cover(low, min(ready - 1, high), high, dilation)
        early_low = low
        while early_low in covered and early_low <= high:
            early_low += 1
        early = cover(early_low, high, high, dilation)[0] if early_low <= high else []
        stage = Stage(dilation, low, high, early_low, late, early)
        need = min(max(covered) + dilation, stages[-1].high)
        stages[-1].keep = tuple(range(stages[-1].early_low, need + 1))
        stages.append(stage)
    return stages


def column_masks(channels, width, dilation):
    column = lax.broadcasted_iota(jnp.int16, (channels, width), 1)
    return column >= jnp.int16(dilation), column < jnp.int16(width - dilation)


class Stack:
    def __init__(self, parts, top, dilation, masks):
        self.parts, self.top, self.dilation, self.masks = parts, top, dilation, masks[dilation]

    def find(self, row):
        for ref, base in self.parts:
            if row >= base:
                return ref, row - base
        raise ValueError(row)

    def put(self, row, value):
        channels, width = value.shape
        ref, index = self.find(row)
        zeros = jnp.zeros_like(value)
        ref[index, :channels, :] = jnp.where(self.masks[0], pltpu.roll(value, self.dilation, 1), zeros)
        ref[index, channels : 2 * channels, :] = value
        ref[index, 2 * channels :, :] = jnp.where(
            self.masks[1], pltpu.roll(value, width - self.dilation, 1), zeros
        )

    def get(self, row, place):
        ref, index = self.find(min(row, self.top))
        channels = ref.shape[1] // 3
        return ref[index, place * channels : (place + 1) * channels, :]

    def window(self, start, taps):
        slabs = []
        for tap in taps:
            ref, index = self.find(min(start + (tap - 1) * self.dilation, self.top))
            slabs.append(ref[index])
        return jnp.concatenate(slabs, axis=0)


def late_groups(stages, layer):
    stage, source = stages[layer + 1], stages[layer]
    count = group_of(stage.dilation) + 2
    groups = {}
    place = 0
    for start in stage.late:
        first = 0
        while first < count and start + (first - 1) * stage.dilation < source.early_low:
            first += 1
        first = min(first + first % 2, count)
        groups[start] = (first, place)
        place += first < count
    return groups, place


def spread_conv(banded, slot, w_conv, layer, turned, odd):
    inner, channels = w_conv.shape[2], w_conv.shape[3]
    count = banded.shape[1] // inner
    zeros = jnp.zeros((inner, channels), BF16)
    taps = []
    for row_tap in range(3):
        line = jnp.where(odd == 1, 2 - row_tap, row_tap)
        for col_tap in range(3):
            taps.append(w_conv[layer, col_tap * 3 + line if turned else line * 3 + col_tap])
    for row in range(count):
        parts = [zeros] * (3 * row) + taps + [zeros] * (3 * (count - 1 - row))
        banded[slot, row * inner : (row + 1) * inner, :] = jnp.concatenate(parts, axis=1)


def as_column(row, copies):
    size = row.shape[1]
    across = lax.broadcasted_iota(jnp.int32, (size, size), 1)
    down = lax.broadcasted_iota(jnp.int32, (size, size), 0)
    spread = jnp.where(across == down, jnp.broadcast_to(row, (size, size)), 0.0)
    column = jnp.sum(spread, axis=1, keepdims=True)
    return jnp.concatenate([column] * copies, axis=0)


def run_block(starts, rows, dilation, hidden_of, finish):
    waiting, done = [], set()

    def complete(start, hidden):
        steps = []
        for step in range(group_of(dilation)):
            row = start + step * dilation
            if row in rows and row not in done:
                steps.append((step, row))
                done.add(row)
        finish(start, hidden, steps)

    for start in starts:
        waiting.append((start, hidden_of(start)))
        if len(waiting) > LAG:
            complete(*waiting.pop(0))
    for item in waiting:
        complete(*item)


def conv_sum(stack, start, kernel, bias, taps):
    slab = stack.parts[0][0].shape[1]
    columns = slice(taps[0] * slab, (taps[-1] + 1) * slab)
    return jnp.dot(kernel[:, columns], stack.window(start, taps), preferred_element_type=F32) + bias


def conv_hidden(stack, start, kernel, bias, groups=None, sums=None):
    count = group_of(stack.dilation) + 2
    first, place = groups[start] if groups else (count, 0)
    if first < count:
        bias = sums[place]
    inner = conv_sum(stack, start, kernel, bias, range(first))
    return jnp.maximum(inner, 0.0).astype(BF16)


def early_sums(stack, kernel, bias, groups, sums):
    count = group_of(stack.dilation) + 2
    for start, (first, place) in groups.items():
        if first < count:
            sums[place] = conv_sum(stack, start, kernel, bias, range(first, count))


def group_rows(stack, start, hidden, kernel, bias):
    inner = kernel.shape[1]
    values = []
    for step in range(hidden.shape[0] // inner):
        blended = jnp.dot(kernel, hidden[step * inner : (step + 1) * inner], preferred_element_type=F32)
        values.append(stack.get(start + step * stack.dilation, 1).astype(F32) + blended + bias)
    return values


def fetch(pairs, sems):
    copies = [pltpu.make_async_copy(source, target, sems.at[i]) for i, (source, target) in enumerate(pairs)]
    for copy in copies:
        copy.start()
    return copies


def position():
    device = lax.axis_index("row")
    size = lax.axis_size("row")
    odd = device % 2
    edge = jnp.logical_or(device == 0, device == size - 1)
    return odd, edge


def line_of(row, shard_rows, odd):
    inside = row % shard_rows
    return jnp.where(odd == 1, shard_rows - 1 - inside, inside)


def layer_steps():
    return dilations * SECTIONS + (dilations[0],)


def slot_of(steps, layer):
    return sum(1 for step in steps[:layer] if group_of(step) == group_of(steps[layer]))


def prepare(w_conv, bias_in, w_out, bias_out, small, large, small_turned, large_turned, project, bias, bias_last,
            conv, proj, first_bias, last_bias, sems):
    odd, _ = position()
    pairs = [(w_conv, conv), (w_out, proj), (bias_in, first_bias), (bias_out, last_bias)]
    for copy in fetch(pairs, sems):
        copy.wait()
    steps = layer_steps()
    base = len(steps) - 1 - DEPTH
    for layer, step in enumerate(steps):
        spread_conv(small if group_of(step) == 2 else large, slot_of(steps, layer), conv, layer, False, odd)
        project[layer] = proj[layer].astype(F32).T.astype(BF16)
        bias[layer] = jnp.broadcast_to(as_column(first_bias[layer : layer + 1, :], 4), bias.shape[1:])
        bias_last[layer] = jnp.broadcast_to(as_column(last_bias[layer : layer + 1, :], 1), bias_last.shape[1:])
    for layer, step in enumerate(dilations):
        place = small_turned if group_of(step) == 2 else large_turned
        spread_conv(place, slot_of(dilations, layer), conv, base + layer, True, odd)


class Weights:
    def __init__(self, refs, base, width):
        self.refs, self.base, self.blocks = refs, base, width // LANES

    def conv(self, layer):
        steps = layer_steps()
        layer = self.base + layer
        return self.refs[0 if group_of(steps[layer]) == 2 else 1][slot_of(steps, layer)]

    def conv_turned(self, layer):
        return self.refs[2 if group_of(dilations[layer]) == 2 else 3][slot_of(dilations, layer)]

    def out(self, layer):
        return self.refs[4][self.base + layer]

    def bias(self, layer):
        inner = self.refs[5].shape[1] // 4
        rows = group_of(layer_steps()[self.base + layer]) * inner
        return jnp.concatenate([self.refs[5][self.base + layer, :rows]] * self.blocks, axis=1)

    def bias_out(self, layer):
        return jnp.concatenate([self.refs[6][self.base + layer]] * self.blocks, axis=1)


def block_one(weights, layer, stage, starts, rows, source, store, groups=None, sums=None):
    kernel, kernel_out = weights.conv(layer), weights.out(layer)
    bias, bias_out = weights.bias(layer), weights.bias_out(layer)

    def hidden_of(start):
        return conv_hidden(source, start, kernel, bias, groups, sums)

    def finish(start, hidden, steps):
        values = group_rows(source, start, hidden, kernel_out, bias_out)
        for step, row in steps:
            store(row, values[step])

    run_block(starts, rows, stage.dilation, hidden_of, finish)


def block_two(weights, layer, stage, starts, rows, sources, store, groups=None, sums=(None, None)):
    kernels = (weights.conv(layer), weights.conv_turned(layer))
    kernel_out, bias, bias_out = weights.out(layer), weights.bias(layer), weights.bias_out(layer)

    def hidden_of(start):
        if sources[0] is sources[1]:
            both = conv_hidden(
                sources[0], start, jnp.concatenate(kernels, axis=0), jnp.concatenate([bias, bias], axis=0),
                groups, sums[0],
            )
            half = both.shape[0] // 2
            return both[:half], both[half:]
        return tuple(
            conv_hidden(source, start, kernel, bias, groups, part)
            for source, kernel, part in zip(sources, kernels, sums)
        )

    def finish(start, hiddens, steps):
        values = [
            group_rows(source, start, hidden, kernel_out, bias_out)
            for source, hidden in zip(sources, hiddens)
        ]
        for step, row in steps:
            store(row, [value[step].astype(BF16) for value in values])

    run_block(starts, rows, stage.dilation, hidden_of, finish)


def mean_of(first, second):
    return ((first.astype(F32) + second.astype(F32)) * 0.5).astype(BF16)


def masks_for(channels, width):
    return {dilation: column_masks(channels, width, dilation) for dilation in dilations}


def rows_of_raw(shards, count, wide, shard_rows, channels, width):
    for slot in range(count):
        whole = shards[slot][...].astype(F32).reshape(channels * shard_rows, width)
        for block in range(width // LANES):
            wide[slot, block] = whole[:, block * LANES : (block + 1) * LANES]


def raw_row(wide, slot, line, shard_rows, channels, width):
    picked = pl.ds(line, channels, stride=shard_rows)
    parts = [wide[slot, block, picked, :] for block in range(width // LANES)]
    return jnp.concatenate(parts, axis=1).astype(BF16)


def one_early(chip, *refs):
    weight_refs, (stack_0, stack_1, stack_2), sums, wide = refs[:7], refs[7:10], refs[10:13], refs[13]
    _, channels, shard_rows, width = chip.shape
    odd, _ = position()
    stages = plan(shard_rows, dilations)
    weights = Weights(weight_refs, 0, width)
    masks = masks_for(channels, width)
    rows_of_raw(chip, 2, wide, shard_rows, channels, width)
    stacks = [
        Stack([(ref, stage.early_low)], stage.high, dilation, masks)
        for ref, stage, dilation in zip((stack_0, stack_1, stack_2), stages, dilations)
    ]
    for row in range(stages[0].high + 1):
        line = line_of(row, shard_rows, odd)
        slot = jnp.where(odd == 1, 1 - row // shard_rows, row // shard_rows)
        stacks[0].put(row, raw_row(wide, slot, line, shard_rows, channels, width))
    for layer in range(DEPTH - 1):
        stage = stages[layer + 1]

        def store(row, value):
            stacks[layer + 1].put(row, value.astype(BF16))

        block_one(weights, layer, stage, stage.early, range(stage.early_low, stage.high + 1), stacks[layer], store)
    for layer in range(DEPTH):
        groups, _ = late_groups(stages, layer)
        early_sums(stacks[layer], weights.conv(layer), weights.bias(layer), groups, sums[layer])


def chunks_turned(values, lines):
    values = list(values)
    chunk = lax.broadcasted_iota(jnp.int32, values[0].shape, 1) // lines
    for bit in range(3):
        step = 1 << bit
        clear = ((chunk >> bit) & 1) == 0
        for index in range(8):
            if index & step:
                continue
            first, second = values[index], values[index + step]
            values[index] = jnp.where(clear, first, pltpu.roll(second, lines * step, 1))
            values[index + step] = jnp.where(clear, pltpu.roll(first, LANES - lines * step, 1), second)
    return values


def one_late(across, kept_0, kept_1, kept_2, *refs):
    sums, weight_refs, (out, tiles, stack_0, stack_1, stack_2, wide) = refs[:3], refs[3:10], refs[10:]
    channels, shard_rows, width = across.shape
    odd, edge = position()
    stages = plan(shard_rows, dilations)
    weights = Weights(weight_refs, 0, width)
    masks = masks_for(channels, width)
    rows_of_raw([across], 1, wide, shard_rows, channels, width)
    stacks = [
        Stack([(early, stage.early_low), (late, stage.low)], stage.high, dilation, masks)
        for early, late, stage, dilation in zip(
            (kept_0, kept_1, kept_2), (stack_0, stack_1, stack_2), stages, dilations
        )
    ]
    for row in range(stages[0].low, 0):
        stacks[0].put(row, raw_row(wide, 0, line_of(row, shard_rows, odd), shard_rows, channels, width))
    for layer in range(DEPTH):
        stage = stages[layer + 1]

        def store(row, value):
            value = value.astype(BF16)
            if layer == DEPTH - 1:
                out[line_of(row, shard_rows, odd)] = value
                return
            if row < 0:
                value = jnp.where(edge, jnp.zeros_like(value), value)
            stacks[layer + 1].put(row, value)

        groups, _ = late_groups(stages, layer)
        rows = range(stage.low, stage.early_low)
        block_one(weights, layer, stage, stage.late, rows, stacks[layer], store, groups, sums[layer])

    half = channels // 2
    low_lanes = lax.broadcasted_iota(jnp.int32, (half, LANES), 1) < LANES // 2
    for block in range(width // LANES):
        values = [out[row, :, block * LANES : (block + 1) * LANES] for row in range(shard_rows)]
        for index, value in enumerate(chunks_turned(values, shard_rows)):
            top, bottom = value[:half], value[half:]
            device = block * 16 + index
            tiles[device] = jnp.where(low_lanes, top, pltpu.roll(bottom, LANES // 2, 1))
            tiles[device + 8] = jnp.where(low_lanes, pltpu.roll(top, LANES // 2, 1), bottom)


def symmetrize(tiles, own, out):
    shard_rows, channels, width = own.shape
    half = channels // 2
    low_lanes = lax.broadcasted_iota(jnp.int32, (half, LANES), 1) < LANES // 2
    lane_in = lax.broadcasted_iota(jnp.int32, (LANES, LANES), 0)
    lane_out = lax.broadcasted_iota(jnp.int32, (LANES, LANES), 1)
    size = shard_rows
    turned = (lane_out // (size * size)) * (size * size) + (lane_out % size) * size + (lane_out // size) % size
    swap = jnp.where(lane_in == turned, 1.0, 0.0).astype(BF16)
    for block in range(width // LANES):
        values = []
        for index in range(8):
            first, second = tiles[block * 16 + index], tiles[block * 16 + index + 8]
            top = jnp.where(low_lanes, first, pltpu.roll(second, LANES // 2, 1))
            bottom = jnp.where(low_lanes, pltpu.roll(first, LANES // 2, 1), second)
            values += [top, bottom]
        stacked = jnp.concatenate(values, axis=0)
        stacked = jnp.dot(stacked, swap, preferred_element_type=F32).astype(BF16)
        values = [stacked[index * channels : (index + 1) * channels] for index in range(8)]
        lanes = slice(block * LANES, (block + 1) * LANES)
        for row, value in enumerate(chunks_turned(values, shard_rows)):
            out[row, :, lanes] = mean_of(own[row, :, lanes], value)


def two_steps():
    return dilations + (dilations[0],)


LAYERS_OF = (0, 1, 1, 2, 2, 3)
SUMS_OF = (0, 1, 1, 2, 2, 3)


def two_early(chip, *refs):
    weight_refs, stack_refs, sums = refs[:7], refs[7:13], refs[13:]
    _, shard_rows, channels, width = chip.shape
    odd, _ = position()
    steps = two_steps()
    stages = plan(shard_rows, steps)
    weights = Weights(weight_refs, DEPTH, width)
    masks = masks_for(channels, width)
    stacks = [[], [], [], []]
    for ref, index in zip(stack_refs, LAYERS_OF):
        stacks[index].append(Stack([(ref, stages[index].early_low)], stages[index].high, steps[index], masks))
    for row in range(stages[0].high + 1):
        slot = jnp.where(odd == 1, 1 - row // shard_rows, row // shard_rows)
        stacks[0][0].put(row, chip[slot, line_of(row, shard_rows, odd)])
    sources = stacks[0] * 2
    for layer in range(DEPTH):
        stage = stages[layer + 1]

        def store(row, values):
            if layer == DEPTH - 1:
                values = [mean_of(*values)]
            for target, value in zip(stacks[layer + 1], values):
                target.put(row, value)

        block_two(weights, layer, stage, stage.early, range(stage.early_low, stage.high + 1), sources, store)
        sources = stacks[layer + 1]
    for ref, layer, turn in zip(sums, SUMS_OF, (0, 0, 1, 0, 1, 0)):
        groups, _ = late_groups(stages, layer)
        kernel = weights.conv_turned(layer) if turn else weights.conv(layer)
        bias = weights.bias(layer)
        if layer == 0:
            kernel = jnp.concatenate([kernel, weights.conv_turned(layer)], axis=0)
            bias = jnp.concatenate([bias, bias], axis=0)
        early_sums(stacks[layer][turn], kernel, bias, groups, ref)


def two_late(across, *refs):
    kept_refs, sums, weight_refs = refs[:6], refs[6:12], refs[12:19]
    out, stack_refs, wide = refs[19], refs[20:26], refs[26]
    shard_rows, channels, width = across.shape
    odd, edge = position()
    steps = two_steps()
    stages = plan(shard_rows, steps)
    weights = Weights(weight_refs, DEPTH, width)
    masks = masks_for(channels, width)
    stacks = [[], [], [], []]
    for early, late, index in zip(kept_refs, stack_refs, LAYERS_OF):
        stage = stages[index]
        stacks[index].append(Stack([(early, stage.early_low), (late, stage.low)], stage.high, steps[index], masks))
    for row in range(stages[0].low, 0):
        stacks[0][0].put(row, across[line_of(row, shard_rows, odd)])
    sources = stacks[0] * 2
    for layer in range(DEPTH):
        stage = stages[layer + 1]

        def store(row, values):
            if layer == DEPTH - 1:
                values = [mean_of(*values)]
            for target, value in zip(stacks[layer + 1], values):
                if row < 0:
                    value = jnp.where(edge, jnp.zeros_like(value), value)
                target.put(row, value)

        groups, _ = late_groups(stages, layer)
        parts = [ref for ref, place in zip(sums, SUMS_OF) if place == layer]
        block_two(
            weights, layer, stage, stage.late, range(stage.low, stage.early_low), sources, store, groups,
            parts if len(parts) == 2 else parts * 2,
        )
        sources = stacks[layer + 1]

    stage = stages[DEPTH + 1]

    def store_last(row, value):
        picked = pl.ds(line_of(row, shard_rows, odd), channels, stride=shard_rows)
        for block in range(width // LANES):
            wide[block, picked, :] = value[:, block * LANES : (block + 1) * LANES]

    groups, _ = late_groups(stages, DEPTH)
    rows = range(stage.low, stage.high + 1)
    block_one(weights, DEPTH, stage, stage.late, rows, sources[0], store_last, groups, sums[-1])
    whole = jnp.concatenate([wide[block] for block in range(width // LANES)], axis=1)
    out[...] = whole.reshape(channels, shard_rows, width).astype(BF16)


VMEM = pl.BlockSpec(memory_space=pltpu.VMEM)
HBM = pl.BlockSpec(memory_space=pltpu.HBM)


class Calls:
    def __init__(self, channels, shard_rows, width, inner, size):
        self.channels, self.shard_rows, self.width, self.inner, self.size = channels, shard_rows, width, inner, size
        self.one = plan(shard_rows, dilations)
        self.two = plan(shard_rows, two_steps())

    def stack(self, low, high):
        return (max(high - low + 1, 1), 3 * self.channels, self.width)

    def early(self, stage):
        return self.stack(stage.early_low, stage.high)

    def late(self, stage):
        return pltpu.VMEM(self.stack(stage.low, stage.early_low - 1), BF16)

    def sums(self, stages, layer, copies=1):
        rows = copies * group_of(stages[layer + 1].dilation) * self.inner
        return jax.ShapeDtypeStruct((max(late_groups(stages, layer)[1], 1), rows, self.width), F32)

    def wide(self, *shards):
        return pltpu.VMEM(shards + (self.width // LANES, self.channels * self.shard_rows, LANES), F32)

    def call(self, body, args, shapes, scratch, specs=None):
        shapes = [shape if isinstance(shape, jax.ShapeDtypeStruct) else jax.ShapeDtypeStruct(shape, BF16) for shape in shapes]
        single = len(shapes) == 1
        return pl.pallas_call(
            body,
            out_shape=shapes[0] if single else shapes,
            in_specs=specs or [VMEM] * len(args),
            out_specs=VMEM if single else [VMEM] * len(shapes),
            scratch_shapes=scratch,
            compiler_params=pltpu.CompilerParams(vmem_limit_bytes=(10 + 6 * self.width // LANES) * 1024 * 1024),
            name=body.__name__,
        )(*args)

    def prepare(self, w_conv, bias_in, w_out, bias_out):
        layers, inner, channels = w_conv.shape[0], self.inner, self.channels

        def banded(steps, count):
            return (sum(1 for step in steps if group_of(step) == count), count * inner, 3 * (count + 2) * channels)

        shapes = [
            banded(layer_steps(), 2), banded(layer_steps(), 4), banded(dilations, 2), banded(dilations, 4),
            (layers, channels, inner),
            jax.ShapeDtypeStruct((layers, 4 * inner, LANES), F32),
            jax.ShapeDtypeStruct((layers, channels, LANES), F32),
        ]
        scratch = [
            pltpu.VMEM(w_conv.shape, BF16), pltpu.VMEM(w_out.shape, BF16),
            pltpu.VMEM(bias_in.shape, F32), pltpu.VMEM(bias_out.shape, F32), pltpu.SemaphoreType.DMA((4,)),
        ]
        args = [pltpu.with_memory_space_constraint(arg, pltpu.HBM) for arg in (w_conv, bias_in, w_out, bias_out)]
        return self.call(
            prepare, args, shapes, scratch, [HBM] * 4
        )

    def one_early(self, *args):
        shapes = [self.early(stage) for stage in self.one[:DEPTH]]
        shapes += [self.sums(self.one, layer) for layer in range(DEPTH)]
        return self.call(one_early, args, shapes, [self.wide(2)])

    def one_late(self, *args):
        shapes = [(self.shard_rows, self.channels, self.width), (self.size, self.channels // 2, LANES)]
        return self.call(one_late, args, shapes, [self.late(stage) for stage in self.one[:DEPTH]] + [self.wide(1)])

    def symmetrize(self, *args):
        return self.call(symmetrize, args, [(self.shard_rows, self.channels, self.width)], [])

    def two_early(self, *args):
        shapes = [self.early(self.two[index]) for index in LAYERS_OF]
        shapes += [self.sums(self.two, layer, 2 if layer == 0 else 1) for layer in SUMS_OF]
        return self.call(two_early, args, shapes, [])

    def two_late(self, *args):
        scratch = [self.late(self.two[index]) for index in LAYERS_OF] + [self.wide()]
        return self.call(two_late, args, [(self.channels, self.shard_rows, self.width)], scratch)


def neighbours(array, axis):
    size = lax.axis_size(axis)
    edges = [(i, i + 1) for i in range(1, size - 1, 2)]
    edges = edges + [(j, i) for i, j in edges]
    across = lax.ppermute(array, axis, edges)
    chip = lax.all_gather(array, axis, axis_index_groups=[[i, i + 1] for i in range(0, size, 2)])
    return across, chip


def on_device(features, w_conv, bias_in, w_out, bias_out):
    channels, shard_rows, width = features.shape
    calls = Calls(channels, shard_rows, width, w_conv.shape[2], lax.axis_size("row"))
    across, chip = neighbours(features, "row")
    weights = calls.prepare(w_conv, bias_in, w_out.transpose(0, 2, 1), bias_out)
    kept = calls.one_early(chip, *weights)
    field, tiles = calls.one_late(across, *kept, *weights)
    received = lax.all_to_all(tiles, "row", split_axis=0, concat_axis=0, tiled=True)
    field = calls.symmetrize(received, field)
    across, chip = neighbours(field, "row")
    kept = calls.two_early(chip, *weights)
    return calls.two_late(across, *kept, *weights)


def solution(mesh):
    in_specs = (P("groups", "row", None), P(), P(), P(), P())
    out_specs = P("groups", "row", None)
    return jax.shard_map(
        on_device, mesh=mesh, in_specs=in_specs, out_specs=out_specs, check_vma=False
    )
```

```python
import jax
import jax.numpy as jnp
from jax import lax
from jax.experimental import pallas as pl
from jax.experimental.pallas import tpu as pltpu
from jax.sharding import PartitionSpec as P

SECTIONS = 2
DEPTH = 3

dilations = (1, 2, 4)
LANES = 128
LAG = 3
PARTS = 4
F32 = jnp.float32
BF16 = jnp.bfloat16


class Stage:
    def __init__(self, dilation, low, high, early_low, late, early):
        self.dilation, self.low, self.high, self.early_low = dilation, low, high, early_low
        self.late, self.early = late, early
        self.keep = ()


def group_of(dilation):
    return 4 if dilation == dilations[1] else 2


def cover(low, high, limit, dilation):
    covered, starts = set(), []
    count = group_of(dilation)
    for row in range(low, high + 1):
        if row in covered:
            continue
        start = row
        for back in range(count):
            candidate = row - back * dilation
            if candidate >= low and candidate + (count - 1) * dilation <= limit:
                start = candidate
                break
        starts.append(start)
        covered |= {start + step * dilation for step in range(count)}
    return starts, covered


def plan(shard_rows, steps):
    reach = sum(steps)
    ready = 0
    stages = [Stage(0, -reach, shard_rows - 1 + reach, 0, [], [])]
    for dilation in steps:
        reach, ready = reach - dilation, ready + dilation
        low, high = -reach, shard_rows - 1 + reach
        late, covered = cover(low, min(ready - 1, high), high, dilation)
        early_low = low
        while early_low in covered and early_low <= high:
            early_low += 1
        early = cover(early_low, high, high, dilation)[0] if early_low <= high else []
        stage = Stage(dilation, low, high, early_low, late, early)
        need = min(max(covered) + dilation, stages[-1].high)
        stages[-1].keep = tuple(range(stages[-1].early_low, need + 1))
        stages.append(stage)
    return stages


def column_masks(channels, width, dilation):
    column = lax.broadcasted_iota(jnp.int16, (channels, width), 1)
    return column >= jnp.int16(dilation), column < jnp.int16(width - dilation)


class Stack:
    def __init__(self, parts, top, dilation, masks):
        self.parts, self.top, self.dilation, self.masks = parts, top, dilation, masks[dilation]

    def find(self, row):
        for ref, base in self.parts:
            if row >= base:
                return ref, row - base
        raise ValueError(row)

    def put(self, row, value):
        channels, width = value.shape
        ref, index = self.find(row)
        zeros = jnp.zeros_like(value)
        ref[index, :channels, :] = jnp.where(self.masks[0], pltpu.roll(value, self.dilation, 1), zeros)
        ref[index, channels : 2 * channels, :] = value
        ref[index, 2 * channels :, :] = jnp.where(
            self.masks[1], pltpu.roll(value, width - self.dilation, 1), zeros
        )

    def get(self, row, place):
        ref, index = self.find(min(row, self.top))
        channels = ref.shape[1] // 3
        return ref[index, place * channels : (place + 1) * channels, :]

    def window(self, start, taps):
        slabs = []
        for tap in taps:
            ref, index = self.find(min(start + (tap - 1) * self.dilation, self.top))
            slabs.append(ref[index])
        return jnp.concatenate(slabs, axis=0)


def late_groups(stages, layer):
    stage, source = stages[layer + 1], stages[layer]
    count = group_of(stage.dilation) + 2
    groups = {}
    place = 0
    for start in stage.late:
        first = 0
        while first < count and start + (first - 1) * stage.dilation < source.early_low:
            first += 1
        first = min(first + first % 2, count)
        groups[start] = (first, place)
        place += first < count
    return groups, place


def spread_conv(banded, slot, w_conv, layer, turned, odd):
    inner, channels = w_conv.shape[2], w_conv.shape[3]
    count = banded.shape[1] // inner
    zeros = jnp.zeros((inner, channels), BF16)
    taps = []
    for row_tap in range(3):
        line = jnp.where(odd == 1, 2 - row_tap, row_tap)
        for col_tap in range(3):
            taps.append(w_conv[layer, col_tap * 3 + line if turned else line * 3 + col_tap])
    for row in range(count):
        parts = [zeros] * (3 * row) + taps + [zeros] * (3 * (count - 1 - row))
        banded[slot, row * inner : (row + 1) * inner, :] = jnp.concatenate(parts, axis=1)


def as_column(row, copies):
    size = row.shape[1]
    across = lax.broadcasted_iota(jnp.int32, (size, size), 1)
    down = lax.broadcasted_iota(jnp.int32, (size, size), 0)
    spread = jnp.where(across == down, jnp.broadcast_to(row, (size, size)), 0.0)
    column = jnp.sum(spread, axis=1, keepdims=True)
    return jnp.concatenate([column] * copies, axis=0)


def run_block(starts, rows, dilation, hidden_of, finish):
    waiting, done = [], set()

    def complete(start, hidden):
        steps = []
        for step in range(group_of(dilation)):
            row = start + step * dilation
            if row in rows and row not in done:
                steps.append((step, row))
                done.add(row)
        finish(start, hidden, steps)

    for start in starts:
        waiting.append((start, hidden_of(start)))
        if len(waiting) > LAG:
            complete(*waiting.pop(0))
    for item in waiting:
        complete(*item)


def conv_sum(stack, start, kernel, bias, taps):
    slab = stack.parts[0][0].shape[1]
    columns = slice(taps[0] * slab, (taps[-1] + 1) * slab)
    return jnp.dot(kernel[:, columns], stack.window(start, taps), preferred_element_type=F32) + bias


def conv_hidden(stack, start, kernel, bias, groups=None, sums=None):
    count = group_of(stack.dilation) + 2
    first, place = groups[start] if groups else (count, 0)
    if first < count:
        bias = sums[place]
    inner = conv_sum(stack, start, kernel, bias, range(first))
    return jnp.maximum(inner, 0.0).astype(BF16)


def early_sums(stack, kernel, bias, groups, sums):
    count = group_of(stack.dilation) + 2
    for start, (first, place) in groups.items():
        if first < count:
            sums[place] = conv_sum(stack, start, kernel, bias, range(first, count))


def group_rows(stack, start, hidden, kernel, bias):
    inner = kernel.shape[1]
    values = []
    for step in range(hidden.shape[0] // inner):
        blended = jnp.dot(kernel, hidden[step * inner : (step + 1) * inner], preferred_element_type=F32)
        values.append(stack.get(start + step * stack.dilation, 1).astype(F32) + blended + bias)
    return values


def fetch(pairs, sems):
    copies = [pltpu.make_async_copy(source, target, sems.at[i]) for i, (source, target) in enumerate(pairs)]
    for copy in copies:
        copy.start()
    return copies


def position():
    device = lax.axis_index("row")
    size = lax.axis_size("row")
    odd = device % 2
    edge = jnp.logical_or(device == 0, device == size - 1)
    return odd, edge


def line_of(row, shard_rows, odd):
    inside = row % shard_rows
    return jnp.where(odd == 1, shard_rows - 1 - inside, inside)


def layer_steps():
    return dilations * SECTIONS + (dilations[0],)


def slot_of(steps, layer):
    return sum(1 for step in steps[:layer] if group_of(step) == group_of(steps[layer]))


def prepare(w_conv, bias_in, w_out, bias_out, small, large, small_turned, large_turned, project, bias, bias_last,
            conv, proj, first_bias, last_bias, sems):
    odd, _ = position()
    pairs = [(w_conv, conv), (w_out, proj), (bias_in, first_bias), (bias_out, last_bias)]
    for copy in fetch(pairs, sems):
        copy.wait()
    steps = layer_steps()
    base = len(steps) - 1 - DEPTH
    for layer, step in enumerate(steps):
        spread_conv(small if group_of(step) == 2 else large, slot_of(steps, layer), conv, layer, False, odd)
        project[layer] = proj[layer].astype(F32).T.astype(BF16)
        bias[layer] = jnp.broadcast_to(as_column(first_bias[layer : layer + 1, :], 4), bias.shape[1:])
        bias_last[layer] = jnp.broadcast_to(as_column(last_bias[layer : layer + 1, :], 1), bias_last.shape[1:])
    for layer, step in enumerate(dilations):
        place = small_turned if group_of(step) == 2 else large_turned
        spread_conv(place, slot_of(dilations, layer), conv, base + layer, True, odd)


class Weights:
    def __init__(self, refs, base, width):
        self.refs, self.base, self.blocks = refs, base, width // LANES

    def conv(self, layer):
        steps = layer_steps()
        layer = self.base + layer
        return self.refs[0 if group_of(steps[layer]) == 2 else 1][slot_of(steps, layer)]

    def conv_turned(self, layer):
        return self.refs[2 if group_of(dilations[layer]) == 2 else 3][slot_of(dilations, layer)]

    def out(self, layer):
        return self.refs[4][self.base + layer]

    def bias(self, layer):
        inner = self.refs[5].shape[1] // 4
        rows = group_of(layer_steps()[self.base + layer]) * inner
        return jnp.concatenate([self.refs[5][self.base + layer, :rows]] * self.blocks, axis=1)

    def bias_out(self, layer):
        return jnp.concatenate([self.refs[6][self.base + layer]] * self.blocks, axis=1)


def block_one(weights, layer, stage, starts, rows, source, store, groups=None, sums=None):
    kernel, kernel_out = weights.conv(layer), weights.out(layer)
    bias, bias_out = weights.bias(layer), weights.bias_out(layer)

    def hidden_of(start):
        return conv_hidden(source, start, kernel, bias, groups, sums)

    def finish(start, hidden, steps):
        values = group_rows(source, start, hidden, kernel_out, bias_out)
        for step, row in steps:
            store(row, values[step])

    run_block(starts, rows, stage.dilation, hidden_of, finish)


def block_two(weights, layer, stage, starts, rows, sources, store, groups=None, sums=(None, None)):
    kernels = (weights.conv(layer), weights.conv_turned(layer))
    kernel_out, bias, bias_out = weights.out(layer), weights.bias(layer), weights.bias_out(layer)

    def hidden_of(start):
        if sources[0] is sources[1]:
            both = conv_hidden(
                sources[0], start, jnp.concatenate(kernels, axis=0), jnp.concatenate([bias, bias], axis=0),
                groups, sums[0],
            )
            half = both.shape[0] // 2
            return both[:half], both[half:]
        return tuple(
            conv_hidden(source, start, kernel, bias, groups, part)
            for source, kernel, part in zip(sources, kernels, sums)
        )

    def finish(start, hiddens, steps):
        values = [
            group_rows(source, start, hidden, kernel_out, bias_out)
            for source, hidden in zip(sources, hiddens)
        ]
        for step, row in steps:
            store(row, [value[step].astype(BF16) for value in values])

    run_block(starts, rows, stage.dilation, hidden_of, finish)


def mean_of(first, second):
    return ((first.astype(F32) + second.astype(F32)) * 0.5).astype(BF16)


def masks_for(channels, width):
    return {dilation: column_masks(channels, width, dilation) for dilation in dilations}


def rows_of_raw(shards, count, wide, shard_rows, channels, width):
    for slot in range(count):
        whole = shards[slot][...].astype(F32).reshape(channels * shard_rows, width)
        for block in range(width // LANES):
            wide[slot, block] = whole[:, block * LANES : (block + 1) * LANES]


def raw_row(wide, slot, line, shard_rows, channels, width):
    picked = pl.ds(line, channels, stride=shard_rows)
    parts = [wide[slot, block, picked, :] for block in range(width // LANES)]
    return jnp.concatenate(parts, axis=1).astype(BF16)


def one_early(chip, *refs):
    weight_refs, (stack_0, stack_1, stack_2), sums, wide = refs[:7], refs[7:10], refs[10:13], refs[13]
    _, channels, shard_rows, width = chip.shape
    odd, _ = position()
    stages = plan(shard_rows, dilations)
    weights = Weights(weight_refs, 0, width)
    masks = masks_for(channels, width)
    rows_of_raw(chip, 2, wide, shard_rows, channels, width)
    stacks = [
        Stack([(ref, stage.early_low)], stage.high, dilation, masks)
        for ref, stage, dilation in zip((stack_0, stack_1, stack_2), stages, dilations)
    ]
    for row in range(stages[0].high + 1):
        line = line_of(row, shard_rows, odd)
        slot = jnp.where(odd == 1, 1 - row // shard_rows, row // shard_rows)
        stacks[0].put(row, raw_row(wide, slot, line, shard_rows, channels, width))
    for layer in range(DEPTH - 1):
        stage = stages[layer + 1]

        def store(row, value):
            stacks[layer + 1].put(row, value.astype(BF16))

        block_one(weights, layer, stage, stage.early, range(stage.early_low, stage.high + 1), stacks[layer], store)
    for layer in range(DEPTH):
        groups, _ = late_groups(stages, layer)
        early_sums(stacks[layer], weights.conv(layer), weights.bias(layer), groups, sums[layer])


def chunks_turned(values, lines):
    values = list(values)
    chunk = lax.broadcasted_iota(jnp.int32, values[0].shape, 1) // lines
    for bit in range(3):
        step = 1 << bit
        clear = ((chunk >> bit) & 1) == 0
        for index in range(8):
            if index & step:
                continue
            first, second = values[index], values[index + step]
            values[index] = jnp.where(clear, first, pltpu.roll(second, lines * step, 1))
            values[index + step] = jnp.where(clear, pltpu.roll(first, LANES - lines * step, 1), second)
    return values


def one_late(across, kept_0, kept_1, kept_2, *refs):
    sums, weight_refs, (out, tiles, stack_0, stack_1, stack_2, wide) = refs[:3], refs[3:10], refs[10:]
    channels, shard_rows, width = across.shape
    odd, edge = position()
    stages = plan(shard_rows, dilations)
    weights = Weights(weight_refs, 0, width)
    masks = masks_for(channels, width)
    rows_of_raw([across], 1, wide, shard_rows, channels, width)
    stacks = [
        Stack([(early, stage.early_low), (late, stage.low)], stage.high, dilation, masks)
        for early, late, stage, dilation in zip(
            (kept_0, kept_1, kept_2), (stack_0, stack_1, stack_2), stages, dilations
        )
    ]
    for row in range(stages[0].low, 0):
        stacks[0].put(row, raw_row(wide, 0, line_of(row, shard_rows, odd), shard_rows, channels, width))
    for layer in range(DEPTH):
        stage = stages[layer + 1]

        def store(row, value):
            value = value.astype(BF16)
            if layer == DEPTH - 1:
                out[line_of(row, shard_rows, odd)] = value
                return
            if row < 0:
                value = jnp.where(edge, jnp.zeros_like(value), value)
            stacks[layer + 1].put(row, value)

        groups, _ = late_groups(stages, layer)
        rows = range(stage.low, stage.early_low)
        block_one(weights, layer, stage, stage.late, rows, stacks[layer], store, groups, sums[layer])

    half = channels // 2
    low_lanes = lax.broadcasted_iota(jnp.int32, (half, LANES), 1) < LANES // 2
    for block in range(width // LANES):
        values = [out[row, :, block * LANES : (block + 1) * LANES] for row in range(shard_rows)]
        for index, value in enumerate(chunks_turned(values, shard_rows)):
            top, bottom = value[:half], value[half:]
            device = block * 16 + index
            tiles[device] = jnp.where(low_lanes, top, pltpu.roll(bottom, LANES // 2, 1))
            tiles[device + 8] = jnp.where(low_lanes, pltpu.roll(top, LANES // 2, 1), bottom)


def symmetrize(tiles, own, out):
    shard_rows, channels, width = own.shape
    half = channels // 2
    low_lanes = lax.broadcasted_iota(jnp.int32, (half, LANES), 1) < LANES // 2
    lane_in = lax.broadcasted_iota(jnp.int32, (LANES, LANES), 0)
    lane_out = lax.broadcasted_iota(jnp.int32, (LANES, LANES), 1)
    size = shard_rows
    turned = (lane_out // (size * size)) * (size * size) + (lane_out % size) * size + (lane_out // size) % size
    swap = jnp.where(lane_in == turned, 1.0, 0.0).astype(BF16)
    for block in range(width // LANES):
        values = []
        for index in range(8):
            first, second = tiles[block * 16 + index], tiles[block * 16 + index + 8]
            top = jnp.where(low_lanes, first, pltpu.roll(second, LANES // 2, 1))
            bottom = jnp.where(low_lanes, pltpu.roll(first, LANES // 2, 1), second)
            values += [top, bottom]
        stacked = jnp.concatenate(values, axis=0)
        stacked = jnp.dot(stacked, swap, preferred_element_type=F32).astype(BF16)
        values = [stacked[index * channels : (index + 1) * channels] for index in range(8)]
        lanes = slice(block * LANES, (block + 1) * LANES)
        for row, value in enumerate(chunks_turned(values, shard_rows)):
            out[row, :, lanes] = mean_of(own[row, :, lanes], value)


def two_steps():
    return dilations + (dilations[0],)


LAYERS_OF = (0, 1, 1, 2, 2, 3)
SUMS_OF = (0, 1, 1, 2, 2, 3)


def two_early(chip, *refs):
    weight_refs, stack_refs, sums = refs[:7], refs[7:13], refs[13:]
    _, shard_rows, channels, width = chip.shape
    odd, _ = position()
    steps = two_steps()
    stages = plan(shard_rows, steps)
    weights = Weights(weight_refs, DEPTH, width)
    masks = masks_for(channels, width)
    stacks = [[], [], [], []]
    for ref, index in zip(stack_refs, LAYERS_OF):
        stacks[index].append(Stack([(ref, stages[index].early_low)], stages[index].high, steps[index], masks))
    for row in range(stages[0].high + 1):
        slot = jnp.where(odd == 1, 1 - row // shard_rows, row // shard_rows)
        stacks[0][0].put(row, chip[slot, line_of(row, shard_rows, odd)])
    sources = stacks[0] * 2
    for layer in range(DEPTH):
        stage = stages[layer + 1]

        def store(row, values):
            if layer == DEPTH - 1:
                values = [mean_of(*values)]
            for target, value in zip(stacks[layer + 1], values):
                target.put(row, value)

        block_two(weights, layer, stage, stage.early, range(stage.early_low, stage.high + 1), sources, store)
        sources = stacks[layer + 1]
    for ref, layer, turn in zip(sums, SUMS_OF, (0, 0, 1, 0, 1, 0)):
        groups, _ = late_groups(stages, layer)
        kernel = weights.conv_turned(layer) if turn else weights.conv(layer)
        bias = weights.bias(layer)
        if layer == 0:
            kernel = jnp.concatenate([kernel, weights.conv_turned(layer)], axis=0)
            bias = jnp.concatenate([bias, bias], axis=0)
        early_sums(stacks[layer][turn], kernel, bias, groups, ref)


def two_late(across, *refs):
    kept_refs, sums, weight_refs = refs[:6], refs[6:12], refs[12:19]
    out, stack_refs, (wide, buffer, sems) = refs[19], refs[20:26], refs[26:]
    shard_rows, channels, width = across.shape
    odd, edge = position()
    steps = two_steps()
    stages = plan(shard_rows, steps)
    weights = Weights(weight_refs, DEPTH, width)
    masks = masks_for(channels, width)
    stacks = [[], [], [], []]
    for early, late, index in zip(kept_refs, stack_refs, LAYERS_OF):
        stage = stages[index]
        stacks[index].append(Stack([(early, stage.early_low), (late, stage.low)], stage.high, steps[index], masks))
    for row in range(stages[0].low, 0):
        stacks[0][0].put(row, across[line_of(row, shard_rows, odd)])
    sources = stacks[0] * 2
    for layer in range(DEPTH):
        stage = stages[layer + 1]

        def store(row, values):
            if layer == DEPTH - 1:
                values = [mean_of(*values)]
            for target, value in zip(stacks[layer + 1], values):
                if row < 0:
                    value = jnp.where(edge, jnp.zeros_like(value), value)
                target.put(row, value)

        groups, _ = late_groups(stages, layer)
        parts = [ref for ref, place in zip(sums, SUMS_OF) if place == layer]
        block_two(
            weights, layer, stage, stage.late, range(stage.low, stage.early_low), sources, store, groups,
            parts if len(parts) == 2 else parts * 2,
        )
        sources = stacks[layer + 1]

    stage = stages[DEPTH + 1]

    def store_last(row, value):
        picked = pl.ds(line_of(row, shard_rows, odd), channels, stride=shard_rows)
        for block in range(width // LANES):
            wide[block, picked, :] = value[:, block * LANES : (block + 1) * LANES]

    groups, _ = late_groups(stages, DEPTH)
    rows = range(stage.low, stage.high + 1)
    block_one(weights, DEPTH, stage, stage.late, rows, sources[0], store_last, groups, sums[-1])
    copies = []
    part = channels // PARTS
    for index in range(PARTS):
        lines = slice(index * part * shard_rows, (index + 1) * part * shard_rows)
        whole = jnp.concatenate([wide[block, lines, :] for block in range(width // LANES)], axis=1)
        buffer[index * part : (index + 1) * part] = whole.reshape(part, shard_rows, width).astype(BF16)
        place = pl.ds(index * part, part)
        copies.append(pltpu.make_async_copy(buffer.at[place], out.at[place], sems.at[index]))
        copies[-1].start()
    for copy in copies:
        copy.wait()


VMEM = pl.BlockSpec(memory_space=pltpu.VMEM)
HBM = pl.BlockSpec(memory_space=pltpu.HBM)


class Calls:
    def __init__(self, channels, shard_rows, width, inner, size):
        self.channels, self.shard_rows, self.width, self.inner, self.size = channels, shard_rows, width, inner, size
        self.one = plan(shard_rows, dilations)
        self.two = plan(shard_rows, two_steps())

    def stack(self, low, high):
        return (max(high - low + 1, 1), 3 * self.channels, self.width)

    def early(self, stage):
        return self.stack(stage.early_low, stage.high)

    def late(self, stage):
        return pltpu.VMEM(self.stack(stage.low, stage.early_low - 1), BF16)

    def sums(self, stages, layer, copies=1):
        rows = copies * group_of(stages[layer + 1].dilation) * self.inner
        return jax.ShapeDtypeStruct((max(late_groups(stages, layer)[1], 1), rows, self.width), F32)

    def wide(self, *shards):
        return pltpu.VMEM(shards + (self.width // LANES, self.channels * self.shard_rows, LANES), F32)

    def call(self, body, args, shapes, scratch, specs=None, out_spec=VMEM):
        shapes = [shape if isinstance(shape, jax.ShapeDtypeStruct) else jax.ShapeDtypeStruct(shape, BF16) for shape in shapes]
        single = len(shapes) == 1
        return pl.pallas_call(
            body,
            out_shape=shapes[0] if single else shapes,
            in_specs=specs or [VMEM] * len(args),
            out_specs=out_spec if single else [VMEM] * len(shapes),
            scratch_shapes=scratch,
            compiler_params=pltpu.CompilerParams(vmem_limit_bytes=(10 + 6 * self.width // LANES) * 1024 * 1024),
            name=body.__name__,
        )(*args)

    def prepare(self, w_conv, bias_in, w_out, bias_out):
        layers, inner, channels = w_conv.shape[0], self.inner, self.channels

        def banded(steps, count):
            return (sum(1 for step in steps if group_of(step) == count), count * inner, 3 * (count + 2) * channels)

        shapes = [
            banded(layer_steps(), 2), banded(layer_steps(), 4), banded(dilations, 2), banded(dilations, 4),
            (layers, channels, inner),
            jax.ShapeDtypeStruct((layers, 4 * inner, LANES), F32),
            jax.ShapeDtypeStruct((layers, channels, LANES), F32),
        ]
        scratch = [
            pltpu.VMEM(w_conv.shape, BF16), pltpu.VMEM(w_out.shape, BF16),
            pltpu.VMEM(bias_in.shape, F32), pltpu.VMEM(bias_out.shape, F32), pltpu.SemaphoreType.DMA((4,)),
        ]
        args = [pltpu.with_memory_space_constraint(arg, pltpu.HBM) for arg in (w_conv, bias_in, w_out, bias_out)]
        return self.call(
            prepare, args, shapes, scratch, [HBM] * 4
        )

    def one_early(self, *args):
        shapes = [self.early(stage) for stage in self.one[:DEPTH]]
        shapes += [self.sums(self.one, layer) for layer in range(DEPTH)]
        return self.call(one_early, args, shapes, [self.wide(2)])

    def one_late(self, *args):
        shapes = [(self.shard_rows, self.channels, self.width), (self.size, self.channels // 2, LANES)]
        return self.call(one_late, args, shapes, [self.late(stage) for stage in self.one[:DEPTH]] + [self.wide(1)])

    def symmetrize(self, *args):
        return self.call(symmetrize, args, [(self.shard_rows, self.channels, self.width)], [])

    def two_early(self, *args):
        shapes = [self.early(self.two[index]) for index in LAYERS_OF]
        shapes += [self.sums(self.two, layer, 2 if layer == 0 else 1) for layer in SUMS_OF]
        return self.call(two_early, args, shapes, [])

    def two_late(self, *args):
        scratch = [self.late(self.two[index]) for index in LAYERS_OF] + [self.wide()]
        shape = (self.channels, self.shard_rows, self.width)
        scratch += [pltpu.VMEM(shape, BF16), pltpu.SemaphoreType.DMA((PARTS,))]
        return self.call(two_late, args, [shape], scratch, None, HBM)


def neighbours(array, axis):
    size = lax.axis_size(axis)
    edges = [(i, i + 1) for i in range(1, size - 1, 2)]
    edges = edges + [(j, i) for i, j in edges]
    across = lax.ppermute(array, axis, edges)
    chip = lax.all_gather(array, axis, axis_index_groups=[[i, i + 1] for i in range(0, size, 2)])
    return across, chip


def on_device(features, w_conv, bias_in, w_out, bias_out):
    channels, shard_rows, width = features.shape
    calls = Calls(channels, shard_rows, width, w_conv.shape[2], lax.axis_size("row"))
    across, chip = neighbours(features, "row")
    weights = calls.prepare(w_conv, bias_in, w_out.transpose(0, 2, 1), bias_out)
    kept = calls.one_early(chip, *weights)
    field, tiles = calls.one_late(across, *kept, *weights)
    received = lax.all_to_all(tiles, "row", split_axis=0, concat_axis=0, tiled=True)
    field = calls.symmetrize(received, field)
    across, chip = neighbours(field, "row")
    kept = calls.two_early(chip, *weights)
    return calls.two_late(across, *kept, *weights)


def solution(mesh):
    in_specs = (P("groups", "row", None), P(), P(), P(), P())
    out_specs = P("groups", "row", None)
    return jax.shard_map(
        on_device, mesh=mesh, in_specs=in_specs, out_specs=out_specs, check_vma=False
    )
```

```python
import jax
import jax.numpy as jnp
from jax import lax
from jax.experimental import pallas as pl
from jax.experimental.pallas import tpu as pltpu
from jax.sharding import PartitionSpec as P

SECTIONS = 2
DEPTH = 3

dilations = (1, 2, 4)
LANES = 128
LAG = 3
F32 = jnp.float32
BF16 = jnp.bfloat16


class Stage:
    def __init__(self, dilation, low, high, early_low, late, early):
        self.dilation, self.low, self.high, self.early_low = dilation, low, high, early_low
        self.late, self.early = late, early
        self.keep = ()


def group_of(dilation):
    return 4 if dilation == dilations[1] else 2


def cover(low, high, limit, dilation):
    covered, starts = set(), []
    count = group_of(dilation)
    for row in range(low, high + 1):
        if row in covered:
            continue
        start = row
        for back in range(count):
            candidate = row - back * dilation
            if candidate >= low and candidate + (count - 1) * dilation <= limit:
                start = candidate
                break
        starts.append(start)
        covered |= {start + step * dilation for step in range(count)}
    return starts, covered


def plan(shard_rows, steps):
    reach = sum(steps)
    ready = 0
    stages = [Stage(0, -reach, shard_rows - 1 + reach, 0, [], [])]
    for dilation in steps:
        reach, ready = reach - dilation, ready + dilation
        low, high = -reach, shard_rows - 1 + reach
        late, covered = cover(low, min(ready - 1, high), high, dilation)
        early_low = low
        while early_low in covered and early_low <= high:
            early_low += 1
        early = cover(early_low, high, high, dilation)[0] if early_low <= high else []
        stage = Stage(dilation, low, high, early_low, late, early)
        need = min(max(covered) + dilation, stages[-1].high)
        stages[-1].keep = tuple(range(stages[-1].early_low, need + 1))
        stages.append(stage)
    return stages


def column_masks(channels, width, dilation):
    column = lax.broadcasted_iota(jnp.int16, (channels, width), 1)
    return column >= jnp.int16(dilation), column < jnp.int16(width - dilation)


class Stack:
    def __init__(self, parts, top, dilation, masks):
        self.parts, self.top, self.dilation, self.masks = parts, top, dilation, masks[dilation]

    def find(self, row):
        for ref, base in self.parts:
            if row >= base:
                return ref, row - base
        raise ValueError(row)

    def put(self, row, value):
        channels, width = value.shape
        ref, index = self.find(row)
        zeros = jnp.zeros_like(value)
        ref[index, :channels, :] = jnp.where(self.masks[0], pltpu.roll(value, self.dilation, 1), zeros)
        ref[index, channels : 2 * channels, :] = value
        ref[index, 2 * channels :, :] = jnp.where(
            self.masks[1], pltpu.roll(value, width - self.dilation, 1), zeros
        )

    def get(self, row, place):
        ref, index = self.find(min(row, self.top))
        channels = ref.shape[1] // 3
        return ref[index, place * channels : (place + 1) * channels, :]

    def window(self, start, taps):
        slabs = []
        for tap in taps:
            ref, index = self.find(min(start + (tap - 1) * self.dilation, self.top))
            slabs.append(ref[index])
        return jnp.concatenate(slabs, axis=0)


def late_groups(stages, layer):
    stage, source = stages[layer + 1], stages[layer]
    count = group_of(stage.dilation) + 2
    groups = {}
    place = 0
    for start in stage.late:
        first = 0
        while first < count and start + (first - 1) * stage.dilation < source.early_low:
            first += 1
        first = min(first + first % 2, count)
        groups[start] = (first, place)
        place += first < count
    return groups, place


def spread_conv(banded, slot, w_conv, layer, turned, odd):
    inner, channels = w_conv.shape[2], w_conv.shape[3]
    count = banded.shape[1] // inner
    zeros = jnp.zeros((inner, channels), BF16)
    taps = []
    for row_tap in range(3):
        line = jnp.where(odd == 1, 2 - row_tap, row_tap)
        for col_tap in range(3):
            taps.append(w_conv[layer, col_tap * 3 + line if turned else line * 3 + col_tap])
    for row in range(count):
        parts = [zeros] * (3 * row) + taps + [zeros] * (3 * (count - 1 - row))
        banded[slot, row * inner : (row + 1) * inner, :] = jnp.concatenate(parts, axis=1)


def as_column(row, copies):
    size = row.shape[1]
    across = lax.broadcasted_iota(jnp.int32, (size, size), 1)
    down = lax.broadcasted_iota(jnp.int32, (size, size), 0)
    spread = jnp.where(across == down, jnp.broadcast_to(row, (size, size)), 0.0)
    column = jnp.sum(spread, axis=1, keepdims=True)
    return jnp.concatenate([column] * copies, axis=0)


def run_block(starts, rows, dilation, hidden_of, finish):
    waiting, done = [], set()

    def complete(start, hidden):
        steps = []
        for step in range(group_of(dilation)):
            row = start + step * dilation
            if row in rows and row not in done:
                steps.append((step, row))
                done.add(row)
        finish(start, hidden, steps)

    for start in starts:
        waiting.append((start, hidden_of(start)))
        if len(waiting) > LAG:
            complete(*waiting.pop(0))
    for item in waiting:
        complete(*item)


def conv_sum(stack, start, kernel, bias, taps):
    slab = stack.parts[0][0].shape[1]
    columns = slice(taps[0] * slab, (taps[-1] + 1) * slab)
    return jnp.dot(kernel[:, columns], stack.window(start, taps), preferred_element_type=F32) + bias


def conv_hidden(stack, start, kernel, bias, groups=None, sums=None):
    count = group_of(stack.dilation) + 2
    first, place = groups[start] if groups else (count, 0)
    if first < count:
        bias = sums[place]
    inner = conv_sum(stack, start, kernel, bias, range(first))
    return jnp.maximum(inner, 0.0).astype(BF16)


def early_sums(stack, kernel, bias, groups, sums):
    count = group_of(stack.dilation) + 2
    for start, (first, place) in groups.items():
        if first < count:
            sums[place] = conv_sum(stack, start, kernel, bias, range(first, count))


def group_rows(stack, start, hidden, kernel, bias):
    inner = kernel.shape[1]
    values = []
    for step in range(hidden.shape[0] // inner):
        blended = jnp.dot(kernel, hidden[step * inner : (step + 1) * inner], preferred_element_type=F32)
        values.append(stack.get(start + step * stack.dilation, 1).astype(F32) + blended + bias)
    return values


def fetch(pairs, sems):
    copies = [pltpu.make_async_copy(source, target, sems.at[i]) for i, (source, target) in enumerate(pairs)]
    for copy in copies:
        copy.start()
    return copies


def position():
    device = lax.axis_index("row")
    size = lax.axis_size("row")
    odd = device % 2
    edge = jnp.logical_or(device == 0, device == size - 1)
    return odd, edge


def line_of(row, shard_rows, odd):
    inside = row % shard_rows
    return jnp.where(odd == 1, shard_rows - 1 - inside, inside)


def layer_steps():
    return dilations * SECTIONS + (dilations[0],)


def slot_of(steps, layer):
    return sum(1 for step in steps[:layer] if group_of(step) == group_of(steps[layer]))


def prepare(w_conv, bias_in, w_out, bias_out, small, large, small_turned, large_turned, project, bias, bias_last,
            conv, proj, first_bias, last_bias, sems):
    odd, _ = position()
    pairs = [(w_conv, conv), (w_out, proj), (bias_in, first_bias), (bias_out, last_bias)]
    for copy in fetch(pairs, sems):
        copy.wait()
    steps = layer_steps()
    base = len(steps) - 1 - DEPTH
    for layer, step in enumerate(steps):
        spread_conv(small if group_of(step) == 2 else large, slot_of(steps, layer), conv, layer, False, odd)
        project[layer] = proj[layer].astype(F32).T.astype(BF16)
        bias[layer] = jnp.broadcast_to(as_column(first_bias[layer : layer + 1, :], 4), bias.shape[1:])
        bias_last[layer] = jnp.broadcast_to(as_column(last_bias[layer : layer + 1, :], 1), bias_last.shape[1:])
    for layer, step in enumerate(dilations):
        place = small_turned if group_of(step) == 2 else large_turned
        spread_conv(place, slot_of(dilations, layer), conv, base + layer, True, odd)


class Weights:
    def __init__(self, refs, base, width):
        self.refs, self.base, self.blocks = refs, base, width // LANES

    def conv(self, layer):
        steps = layer_steps()
        layer = self.base + layer
        return self.refs[0 if group_of(steps[layer]) == 2 else 1][slot_of(steps, layer)]

    def conv_turned(self, layer):
        return self.refs[2 if group_of(dilations[layer]) == 2 else 3][slot_of(dilations, layer)]

    def out(self, layer):
        return self.refs[4][self.base + layer]

    def bias(self, layer):
        inner = self.refs[5].shape[1] // 4
        rows = group_of(layer_steps()[self.base + layer]) * inner
        return jnp.concatenate([self.refs[5][self.base + layer, :rows]] * self.blocks, axis=1)

    def bias_out(self, layer):
        return jnp.concatenate([self.refs[6][self.base + layer]] * self.blocks, axis=1)


def block_one(weights, layer, stage, starts, rows, source, store, groups=None, sums=None):
    kernel, kernel_out = weights.conv(layer), weights.out(layer)
    bias, bias_out = weights.bias(layer), weights.bias_out(layer)

    def hidden_of(start):
        return conv_hidden(source, start, kernel, bias, groups, sums)

    def finish(start, hidden, steps):
        values = group_rows(source, start, hidden, kernel_out, bias_out)
        for step, row in steps:
            store(row, values[step])

    run_block(starts, rows, stage.dilation, hidden_of, finish)


def block_two(weights, layer, stage, starts, rows, sources, store, groups=None, sums=(None, None)):
    kernels = (weights.conv(layer), weights.conv_turned(layer))
    kernel_out, bias, bias_out = weights.out(layer), weights.bias(layer), weights.bias_out(layer)

    def hidden_of(start):
        if sources[0] is sources[1]:
            both = conv_hidden(
                sources[0], start, jnp.concatenate(kernels, axis=0), jnp.concatenate([bias, bias], axis=0),
                groups, sums[0],
            )
            half = both.shape[0] // 2
            return both[:half], both[half:]
        return tuple(
            conv_hidden(source, start, kernel, bias, groups, part)
            for source, kernel, part in zip(sources, kernels, sums)
        )

    def finish(start, hiddens, steps):
        values = [
            group_rows(source, start, hidden, kernel_out, bias_out)
            for source, hidden in zip(sources, hiddens)
        ]
        for step, row in steps:
            store(row, [value[step].astype(BF16) for value in values])

    run_block(starts, rows, stage.dilation, hidden_of, finish)


def mean_of(first, second):
    return ((first.astype(F32) + second.astype(F32)) * 0.5).astype(BF16)


def masks_for(channels, width):
    return {dilation: column_masks(channels, width, dilation) for dilation in dilations}


def rows_of_raw(shards, count, wide, shard_rows, channels, width):
    for slot in range(count):
        whole = shards[slot][...].astype(F32).reshape(channels * shard_rows, width)
        for block in range(width // LANES):
            wide[slot, block] = whole[:, block * LANES : (block + 1) * LANES]


def raw_row(wide, slot, line, shard_rows, channels, width):
    picked = pl.ds(line, channels, stride=shard_rows)
    parts = [wide[slot, block, picked, :] for block in range(width // LANES)]
    return jnp.concatenate(parts, axis=1).astype(BF16)


def one_early(chip, *refs):
    weight_refs, (stack_0, stack_1, stack_2), sums, wide = refs[:7], refs[7:10], refs[10:13], refs[13]
    _, channels, shard_rows, width = chip.shape
    odd, _ = position()
    stages = plan(shard_rows, dilations)
    weights = Weights(weight_refs, 0, width)
    masks = masks_for(channels, width)
    rows_of_raw(chip, 2, wide, shard_rows, channels, width)
    stacks = [
        Stack([(ref, stage.early_low)], stage.high, dilation, masks)
        for ref, stage, dilation in zip((stack_0, stack_1, stack_2), stages, dilations)
    ]
    for row in range(stages[0].high + 1):
        line = line_of(row, shard_rows, odd)
        slot = jnp.where(odd == 1, 1 - row // shard_rows, row // shard_rows)
        stacks[0].put(row, raw_row(wide, slot, line, shard_rows, channels, width))
    for layer in range(DEPTH - 1):
        stage = stages[layer + 1]

        def store(row, value):
            stacks[layer + 1].put(row, value.astype(BF16))

        block_one(weights, layer, stage, stage.early, range(stage.early_low, stage.high + 1), stacks[layer], store)
    for layer in range(DEPTH):
        groups, _ = late_groups(stages, layer)
        early_sums(stacks[layer], weights.conv(layer), weights.bias(layer), groups, sums[layer])


def chunks_turned(values, lines):
    values = list(values)
    lane = lax.broadcasted_iota(jnp.int16, values[0].shape, 1)
    for bit in range(3):
        step = 1 << bit
        clear = (lane & jnp.int16(lines * step)) == jnp.int16(0)
        for index in range(8):
            if index & step:
                continue
            first, second = values[index], values[index + step]
            values[index] = jnp.where(clear, first, pltpu.roll(second, lines * step, 1))
            values[index + step] = jnp.where(clear, pltpu.roll(first, LANES - lines * step, 1), second)
    return values


def one_late(across, kept_0, kept_1, kept_2, *refs):
    sums, weight_refs, (out, tiles, stack_0, stack_1, stack_2, wide) = refs[:3], refs[3:10], refs[10:]
    channels, shard_rows, width = across.shape
    odd, edge = position()
    stages = plan(shard_rows, dilations)
    weights = Weights(weight_refs, 0, width)
    masks = masks_for(channels, width)
    rows_of_raw([across], 1, wide, shard_rows, channels, width)
    stacks = [
        Stack([(early, stage.early_low), (late, stage.low)], stage.high, dilation, masks)
        for early, late, stage, dilation in zip(
            (kept_0, kept_1, kept_2), (stack_0, stack_1, stack_2), stages, dilations
        )
    ]
    for row in range(stages[0].low, 0):
        stacks[0].put(row, raw_row(wide, 0, line_of(row, shard_rows, odd), shard_rows, channels, width))
    for layer in range(DEPTH):
        stage = stages[layer + 1]

        def store(row, value):
            value = value.astype(BF16)
            if layer == DEPTH - 1:
                out[line_of(row, shard_rows, odd)] = value
                return
            if row < 0:
                value = jnp.where(edge, jnp.zeros_like(value), value)
            stacks[layer + 1].put(row, value)

        groups, _ = late_groups(stages, layer)
        rows = range(stage.low, stage.early_low)
        block_one(weights, layer, stage, stage.late, rows, stacks[layer], store, groups, sums[layer])

    half = channels // 2
    low_lanes = lax.broadcasted_iota(jnp.int16, (half, LANES), 1) < jnp.int16(LANES // 2)
    for block in range(width // LANES):
        values = [out[row, :, block * LANES : (block + 1) * LANES] for row in range(shard_rows)]
        for index, value in enumerate(chunks_turned(values, shard_rows)):
            top, bottom = value[:half], value[half:]
            device = block * 16 + index
            tiles[device] = jnp.where(low_lanes, top, pltpu.roll(bottom, LANES // 2, 1))
            tiles[device + 8] = jnp.where(low_lanes, pltpu.roll(top, LANES // 2, 1), bottom)


def symmetrize(tiles, own, out):
    shard_rows, channels, width = own.shape
    half = channels // 2
    low_lanes = lax.broadcasted_iota(jnp.int16, (half, LANES), 1) < jnp.int16(LANES // 2)
    lane_in = lax.broadcasted_iota(jnp.int32, (LANES, LANES), 0)
    lane_out = lax.broadcasted_iota(jnp.int32, (LANES, LANES), 1)
    size = shard_rows
    turned = (lane_out // (size * size)) * (size * size) + (lane_out % size) * size + (lane_out // size) % size
    swap = jnp.where(lane_in == turned, 1.0, 0.0).astype(BF16)
    for block in range(width // LANES):
        values = []
        for index in range(8):
            first, second = tiles[block * 16 + index], tiles[block * 16 + index + 8]
            top = jnp.where(low_lanes, first, pltpu.roll(second, LANES // 2, 1))
            bottom = jnp.where(low_lanes, pltpu.roll(first, LANES // 2, 1), second)
            values += [top, bottom]
        stacked = jnp.concatenate(values, axis=0)
        stacked = jnp.dot(stacked, swap, preferred_element_type=F32).astype(BF16)
        values = [stacked[index * channels : (index + 1) * channels] for index in range(8)]
        lanes = slice(block * LANES, (block + 1) * LANES)
        for row, value in enumerate(chunks_turned(values, shard_rows)):
            out[row, :, lanes] = mean_of(own[row, :, lanes], value)


def two_steps():
    return dilations + (dilations[0],)


LAYERS_OF = (0, 1, 1, 2, 2, 3)
SUMS_OF = (0, 1, 1, 2, 2, 3)


def two_early(chip, *refs):
    weight_refs, stack_refs, sums = refs[:7], refs[7:13], refs[13:]
    _, shard_rows, channels, width = chip.shape
    odd, _ = position()
    steps = two_steps()
    stages = plan(shard_rows, steps)
    weights = Weights(weight_refs, DEPTH, width)
    masks = masks_for(channels, width)
    stacks = [[], [], [], []]
    for ref, index in zip(stack_refs, LAYERS_OF):
        stacks[index].append(Stack([(ref, stages[index].early_low)], stages[index].high, steps[index], masks))
    for row in range(stages[0].high + 1):
        slot = jnp.where(odd == 1, 1 - row // shard_rows, row // shard_rows)
        stacks[0][0].put(row, chip[slot, line_of(row, shard_rows, odd)])
    sources = stacks[0] * 2
    for layer in range(DEPTH):
        stage = stages[layer + 1]

        def store(row, values):
            if layer == DEPTH - 1:
                values = [mean_of(*values)]
            for target, value in zip(stacks[layer + 1], values):
                target.put(row, value)

        block_two(weights, layer, stage, stage.early, range(stage.early_low, stage.high + 1), sources, store)
        sources = stacks[layer + 1]
    for ref, layer, turn in zip(sums, SUMS_OF, (0, 0, 1, 0, 1, 0)):
        groups, _ = late_groups(stages, layer)
        kernel = weights.conv_turned(layer) if turn else weights.conv(layer)
        bias = weights.bias(layer)
        if layer == 0:
            kernel = jnp.concatenate([kernel, weights.conv_turned(layer)], axis=0)
            bias = jnp.concatenate([bias, bias], axis=0)
        early_sums(stacks[layer][turn], kernel, bias, groups, ref)


def two_late(across, *refs):
    kept_refs, sums, weight_refs = refs[:6], refs[6:12], refs[12:19]
    out, stack_refs, wide = refs[19], refs[20:26], refs[26]
    shard_rows, channels, width = across.shape
    odd, edge = position()
    steps = two_steps()
    stages = plan(shard_rows, steps)
    weights = Weights(weight_refs, DEPTH, width)
    masks = masks_for(channels, width)
    stacks = [[], [], [], []]
    for early, late, index in zip(kept_refs, stack_refs, LAYERS_OF):
        stage = stages[index]
        stacks[index].append(Stack([(early, stage.early_low), (late, stage.low)], stage.high, steps[index], masks))
    for row in range(stages[0].low, 0):
        stacks[0][0].put(row, across[line_of(row, shard_rows, odd)])
    sources = stacks[0] * 2
    for layer in range(DEPTH):
        stage = stages[layer + 1]

        def store(row, values):
            if layer == DEPTH - 1:
                values = [mean_of(*values)]
            for target, value in zip(stacks[layer + 1], values):
                if row < 0:
                    value = jnp.where(edge, jnp.zeros_like(value), value)
                target.put(row, value)

        groups, _ = late_groups(stages, layer)
        parts = [ref for ref, place in zip(sums, SUMS_OF) if place == layer]
        block_two(
            weights, layer, stage, stage.late, range(stage.low, stage.early_low), sources, store, groups,
            parts if len(parts) == 2 else parts * 2,
        )
        sources = stacks[layer + 1]

    stage = stages[DEPTH + 1]

    def store_last(row, value):
        picked = pl.ds(line_of(row, shard_rows, odd), channels, stride=shard_rows)
        for block in range(width // LANES):
            wide[block, picked, :] = value[:, block * LANES : (block + 1) * LANES]

    groups, _ = late_groups(stages, DEPTH)
    rows = range(stage.low, stage.high + 1)
    block_one(weights, DEPTH, stage, stage.late, rows, sources[0], store_last, groups, sums[-1])
    whole = jnp.concatenate([wide[block] for block in range(width // LANES)], axis=1)
    out[...] = whole.reshape(channels, shard_rows, width).astype(BF16)


VMEM = pl.BlockSpec(memory_space=pltpu.VMEM)
HBM = pl.BlockSpec(memory_space=pltpu.HBM)


class Calls:
    def __init__(self, channels, shard_rows, width, inner, size):
        self.channels, self.shard_rows, self.width, self.inner, self.size = channels, shard_rows, width, inner, size
        self.one = plan(shard_rows, dilations)
        self.two = plan(shard_rows, two_steps())

    def stack(self, low, high):
        return (max(high - low + 1, 1), 3 * self.channels, self.width)

    def early(self, stage):
        return self.stack(stage.early_low, stage.high)

    def late(self, stage):
        return pltpu.VMEM(self.stack(stage.low, stage.early_low - 1), BF16)

    def sums(self, stages, layer, copies=1):
        rows = copies * group_of(stages[layer + 1].dilation) * self.inner
        return jax.ShapeDtypeStruct((max(late_groups(stages, layer)[1], 1), rows, self.width), F32)

    def wide(self, *shards):
        return pltpu.VMEM(shards + (self.width // LANES, self.channels * self.shard_rows, LANES), F32)

    def call(self, body, args, shapes, scratch, specs=None):
        shapes = [shape if isinstance(shape, jax.ShapeDtypeStruct) else jax.ShapeDtypeStruct(shape, BF16) for shape in shapes]
        single = len(shapes) == 1
        return pl.pallas_call(
            body,
            out_shape=shapes[0] if single else shapes,
            in_specs=specs or [VMEM] * len(args),
            out_specs=VMEM if single else [VMEM] * len(shapes),
            scratch_shapes=scratch,
            compiler_params=pltpu.CompilerParams(vmem_limit_bytes=(10 + 6 * self.width // LANES) * 1024 * 1024),
            name=body.__name__,
        )(*args)

    def prepare(self, w_conv, bias_in, w_out, bias_out):
        layers, inner, channels = w_conv.shape[0], self.inner, self.channels

        def banded(steps, count):
            return (sum(1 for step in steps if group_of(step) == count), count * inner, 3 * (count + 2) * channels)

        shapes = [
            banded(layer_steps(), 2), banded(layer_steps(), 4), banded(dilations, 2), banded(dilations, 4),
            (layers, channels, inner),
            jax.ShapeDtypeStruct((layers, 4 * inner, LANES), F32),
            jax.ShapeDtypeStruct((layers, channels, LANES), F32),
        ]
        scratch = [
            pltpu.VMEM(w_conv.shape, BF16), pltpu.VMEM(w_out.shape, BF16),
            pltpu.VMEM(bias_in.shape, F32), pltpu.VMEM(bias_out.shape, F32), pltpu.SemaphoreType.DMA((4,)),
        ]
        args = [pltpu.with_memory_space_constraint(arg, pltpu.HBM) for arg in (w_conv, bias_in, w_out, bias_out)]
        return self.call(
            prepare, args, shapes, scratch, [HBM] * 4
        )

    def one_early(self, *args):
        shapes = [self.early(stage) for stage in self.one[:DEPTH]]
        shapes += [self.sums(self.one, layer) for layer in range(DEPTH)]
        return self.call(one_early, args, shapes, [self.wide(2)])

    def one_late(self, *args):
        shapes = [(self.shard_rows, self.channels, self.width), (self.size, self.channels // 2, LANES)]
        return self.call(one_late, args, shapes, [self.late(stage) for stage in self.one[:DEPTH]] + [self.wide(1)])

    def symmetrize(self, *args):
        return self.call(symmetrize, args, [(self.shard_rows, self.channels, self.width)], [])

    def two_early(self, *args):
        shapes = [self.early(self.two[index]) for index in LAYERS_OF]
        shapes += [self.sums(self.two, layer, 2 if layer == 0 else 1) for layer in SUMS_OF]
        return self.call(two_early, args, shapes, [])

    def two_late(self, *args):
        scratch = [self.late(self.two[index]) for index in LAYERS_OF] + [self.wide()]
        return self.call(two_late, args, [(self.channels, self.shard_rows, self.width)], scratch)


def neighbours(array, axis):
    size = lax.axis_size(axis)
    edges = [(i, i + 1) for i in range(1, size - 1, 2)]
    edges = edges + [(j, i) for i, j in edges]
    across = lax.ppermute(array, axis, edges)
    chip = lax.all_gather(array, axis, axis_index_groups=[[i, i + 1] for i in range(0, size, 2)])
    return across, chip


def on_device(features, w_conv, bias_in, w_out, bias_out):
    channels, shard_rows, width = features.shape
    calls = Calls(channels, shard_rows, width, w_conv.shape[2], lax.axis_size("row"))
    across, chip = neighbours(features, "row")
    weights = calls.prepare(w_conv, bias_in, w_out.transpose(0, 2, 1), bias_out)
    kept = calls.one_early(chip, *weights)
    field, tiles = calls.one_late(across, *kept, *weights)
    received = lax.all_to_all(tiles, "row", split_axis=0, concat_axis=0, tiled=True)
    field = calls.symmetrize(received, field)
    across, chip = neighbours(field, "row")
    kept = calls.two_early(chip, *weights)
    return calls.two_late(across, *kept, *weights)


def solution(mesh):
    in_specs = (P("groups", "row", None), P(), P(), P(), P())
    out_specs = P("groups", "row", None)
    return jax.shard_map(
        on_device, mesh=mesh, in_specs=in_specs, out_specs=out_specs, check_vma=False
    )
```

```python
import jax
import jax.numpy as jnp
from jax import lax
from jax.experimental import pallas as pl
from jax.experimental.pallas import tpu as pltpu
from jax.sharding import PartitionSpec as P

SECTIONS = 2
DEPTH = 3

dilations = (1, 2, 4)
LANES = 128
LAG = 3
PARTS = 2
F32 = jnp.float32
BF16 = jnp.bfloat16


class Stage:
    def __init__(self, dilation, low, high, early_low, late, early):
        self.dilation, self.low, self.high, self.early_low = dilation, low, high, early_low
        self.late, self.early = late, early
        self.keep = ()


def group_of(dilation):
    return 4 if dilation == dilations[1] else 2


def cover(low, high, limit, dilation):
    covered, starts = set(), []
    count = group_of(dilation)
    for row in range(low, high + 1):
        if row in covered:
            continue
        start = row
        for back in range(count):
            candidate = row - back * dilation
            if candidate >= low and candidate + (count - 1) * dilation <= limit:
                start = candidate
                break
        starts.append(start)
        covered |= {start + step * dilation for step in range(count)}
    return starts, covered


def plan(shard_rows, steps):
    reach = sum(steps)
    ready = 0
    stages = [Stage(0, -reach, shard_rows - 1 + reach, 0, [], [])]
    for dilation in steps:
        reach, ready = reach - dilation, ready + dilation
        low, high = -reach, shard_rows - 1 + reach
        late, covered = cover(low, min(ready - 1, high), high, dilation)
        early_low = low
        while early_low in covered and early_low <= high:
            early_low += 1
        early = cover(early_low, high, high, dilation)[0] if early_low <= high else []
        stage = Stage(dilation, low, high, early_low, late, early)
        need = min(max(covered) + dilation, stages[-1].high)
        stages[-1].keep = tuple(range(stages[-1].early_low, need + 1))
        stages.append(stage)
    return stages


def column_masks(channels, width, dilation):
    column = lax.broadcasted_iota(jnp.int16, (channels, width), 1)
    return column >= jnp.int16(dilation), column < jnp.int16(width - dilation)


class Stack:
    def __init__(self, parts, top, dilation, masks):
        self.parts, self.top, self.dilation, self.masks = parts, top, dilation, masks[dilation]

    def find(self, row):
        for ref, base in self.parts:
            if row >= base:
                return ref, row - base
        raise ValueError(row)

    def put(self, row, value):
        channels, width = value.shape
        ref, index = self.find(row)
        zeros = jnp.zeros_like(value)
        ref[index, :channels, :] = jnp.where(self.masks[0], pltpu.roll(value, self.dilation, 1), zeros)
        ref[index, channels : 2 * channels, :] = value
        ref[index, 2 * channels :, :] = jnp.where(
            self.masks[1], pltpu.roll(value, width - self.dilation, 1), zeros
        )

    def get(self, row, place):
        ref, index = self.find(min(row, self.top))
        channels = ref.shape[1] // 3
        return ref[index, place * channels : (place + 1) * channels, :]

    def window(self, start, taps):
        slabs = []
        for tap in taps:
            ref, index = self.find(min(start + (tap - 1) * self.dilation, self.top))
            slabs.append(ref[index])
        return jnp.concatenate(slabs, axis=0)


def late_groups(stages, layer):
    stage, source = stages[layer + 1], stages[layer]
    count = group_of(stage.dilation) + 2
    groups = {}
    place = 0
    for start in stage.late:
        first = 0
        while first < count and start + (first - 1) * stage.dilation < source.early_low:
            first += 1
        first = min(first + first % 2, count)
        groups[start] = (first, place)
        place += first < count
    return groups, place


def spread_conv(banded, slot, w_conv, layer, turned, odd):
    inner, channels = w_conv.shape[2], w_conv.shape[3]
    count = banded.shape[1] // inner
    zeros = jnp.zeros((inner, channels), BF16)
    taps = []
    for row_tap in range(3):
        line = jnp.where(odd == 1, 2 - row_tap, row_tap)
        for col_tap in range(3):
            taps.append(w_conv[layer, col_tap * 3 + line if turned else line * 3 + col_tap])
    for row in range(count):
        parts = [zeros] * (3 * row) + taps + [zeros] * (3 * (count - 1 - row))
        banded[slot, row * inner : (row + 1) * inner, :] = jnp.concatenate(parts, axis=1)


def as_column(row, copies):
    size = row.shape[1]
    across = lax.broadcasted_iota(jnp.int32, (size, size), 1)
    down = lax.broadcasted_iota(jnp.int32, (size, size), 0)
    spread = jnp.where(across == down, jnp.broadcast_to(row, (size, size)), 0.0)
    column = jnp.sum(spread, axis=1, keepdims=True)
    return jnp.concatenate([column] * copies, axis=0)


def run_block(starts, rows, dilation, hidden_of, finish):
    waiting, done = [], set()

    def complete(start, hidden):
        steps = []
        for step in range(group_of(dilation)):
            row = start + step * dilation
            if row in rows and row not in done:
                steps.append((step, row))
                done.add(row)
        finish(start, hidden, steps)

    for start in starts:
        waiting.append((start, hidden_of(start)))
        if len(waiting) > LAG:
            complete(*waiting.pop(0))
    for item in waiting:
        complete(*item)


def conv_sum(stack, start, kernel, bias, taps):
    slab = stack.parts[0][0].shape[1]
    columns = slice(taps[0] * slab, (taps[-1] + 1) * slab)
    return jnp.dot(kernel[:, columns], stack.window(start, taps), preferred_element_type=F32) + bias


def conv_hidden(stack, start, kernel, bias, groups=None, sums=None):
    count = group_of(stack.dilation) + 2
    first, place = groups[start] if groups else (count, 0)
    if first < count:
        bias = sums[place]
    inner = conv_sum(stack, start, kernel, bias, range(first))
    return jnp.maximum(inner, 0.0).astype(BF16)


def early_sums(stack, kernel, bias, groups, sums):
    count = group_of(stack.dilation) + 2
    for start, (first, place) in groups.items():
        if first < count:
            sums[place] = conv_sum(stack, start, kernel, bias, range(first, count))


def group_rows(stack, start, hidden, kernel, bias):
    inner = kernel.shape[1]
    values = []
    for step in range(hidden.shape[0] // inner):
        blended = jnp.dot(kernel, hidden[step * inner : (step + 1) * inner], preferred_element_type=F32)
        values.append(stack.get(start + step * stack.dilation, 1).astype(F32) + blended + bias)
    return values


def fetch(pairs, sems):
    copies = [pltpu.make_async_copy(source, target, sems.at[i]) for i, (source, target) in enumerate(pairs)]
    for copy in copies:
        copy.start()
    return copies


def position():
    device = lax.axis_index("row")
    size = lax.axis_size("row")
    odd = device % 2
    edge = jnp.logical_or(device == 0, device == size - 1)
    return odd, edge


def line_of(row, shard_rows, odd):
    inside = row % shard_rows
    return jnp.where(odd == 1, shard_rows - 1 - inside, inside)


def layer_steps():
    return dilations * SECTIONS + (dilations[0],)


def slot_of(steps, layer):
    return sum(1 for step in steps[:layer] if group_of(step) == group_of(steps[layer]))


def prepare(w_conv, bias_in, w_out, bias_out, small, large, small_turned, large_turned, project, bias, bias_last,
            conv, proj, first_bias, last_bias, sems):
    odd, _ = position()
    pairs = [(w_conv, conv), (w_out, proj), (bias_in, first_bias), (bias_out, last_bias)]
    for copy in fetch(pairs, sems):
        copy.wait()
    steps = layer_steps()
    base = len(steps) - 1 - DEPTH
    for layer, step in enumerate(steps):
        spread_conv(small if group_of(step) == 2 else large, slot_of(steps, layer), conv, layer, False, odd)
        project[layer] = proj[layer].astype(F32).T.astype(BF16)
        bias[layer] = jnp.broadcast_to(as_column(first_bias[layer : layer + 1, :], 4), bias.shape[1:])
        bias_last[layer] = jnp.broadcast_to(as_column(last_bias[layer : layer + 1, :], 1), bias_last.shape[1:])
    for layer, step in enumerate(dilations):
        place = small_turned if group_of(step) == 2 else large_turned
        spread_conv(place, slot_of(dilations, layer), conv, base + layer, True, odd)


class Weights:
    def __init__(self, refs, base, width):
        self.refs, self.base, self.blocks = refs, base, width // LANES

    def conv(self, layer):
        steps = layer_steps()
        layer = self.base + layer
        return self.refs[0 if group_of(steps[layer]) == 2 else 1][slot_of(steps, layer)]

    def conv_turned(self, layer):
        return self.refs[2 if group_of(dilations[layer]) == 2 else 3][slot_of(dilations, layer)]

    def out(self, layer):
        return self.refs[4][self.base + layer]

    def bias(self, layer):
        inner = self.refs[5].shape[1] // 4
        rows = group_of(layer_steps()[self.base + layer]) * inner
        return jnp.concatenate([self.refs[5][self.base + layer, :rows]] * self.blocks, axis=1)

    def bias_out(self, layer):
        return jnp.concatenate([self.refs[6][self.base + layer]] * self.blocks, axis=1)


def block_one(weights, layer, stage, starts, rows, source, store, groups=None, sums=None):
    kernel, kernel_out = weights.conv(layer), weights.out(layer)
    bias, bias_out = weights.bias(layer), weights.bias_out(layer)

    def hidden_of(start):
        return conv_hidden(source, start, kernel, bias, groups, sums)

    def finish(start, hidden, steps):
        values = group_rows(source, start, hidden, kernel_out, bias_out)
        for step, row in steps:
            store(row, values[step])

    run_block(starts, rows, stage.dilation, hidden_of, finish)


def block_two(weights, layer, stage, starts, rows, sources, store, groups=None, sums=(None, None)):
    kernels = (weights.conv(layer), weights.conv_turned(layer))
    kernel_out, bias, bias_out = weights.out(layer), weights.bias(layer), weights.bias_out(layer)

    def hidden_of(start):
        if sources[0] is sources[1]:
            both = conv_hidden(
                sources[0], start, jnp.concatenate(kernels, axis=0), jnp.concatenate([bias, bias], axis=0),
                groups, sums[0],
            )
            half = both.shape[0] // 2
            return both[:half], both[half:]
        return tuple(
            conv_hidden(source, start, kernel, bias, groups, part)
            for source, kernel, part in zip(sources, kernels, sums)
        )

    def finish(start, hiddens, steps):
        values = [
            group_rows(source, start, hidden, kernel_out, bias_out)
            for source, hidden in zip(sources, hiddens)
        ]
        for step, row in steps:
            store(row, [value[step].astype(BF16) for value in values])

    run_block(starts, rows, stage.dilation, hidden_of, finish)


def mean_of(first, second):
    return ((first.astype(F32) + second.astype(F32)) * 0.5).astype(BF16)


def masks_for(channels, width):
    return {dilation: column_masks(channels, width, dilation) for dilation in dilations}


def rows_of_raw(shards, count, wide, shard_rows, channels, width):
    for slot in range(count):
        whole = shards[slot][...].astype(F32).reshape(channels * shard_rows, width)
        for block in range(width // LANES):
            wide[slot, block] = whole[:, block * LANES : (block + 1) * LANES]


def raw_row(wide, slot, line, shard_rows, channels, width):
    picked = pl.ds(line, channels, stride=shard_rows)
    parts = [wide[slot, block, picked, :] for block in range(width // LANES)]
    return jnp.concatenate(parts, axis=1).astype(BF16)


def one_early(chip, *refs):
    weight_refs, (stack_0, stack_1, stack_2), sums, wide = refs[:7], refs[7:10], refs[10:13], refs[13]
    _, channels, shard_rows, width = chip.shape
    odd, _ = position()
    stages = plan(shard_rows, dilations)
    weights = Weights(weight_refs, 0, width)
    masks = masks_for(channels, width)
    rows_of_raw(chip, 2, wide, shard_rows, channels, width)
    stacks = [
        Stack([(ref, stage.early_low)], stage.high, dilation, masks)
        for ref, stage, dilation in zip((stack_0, stack_1, stack_2), stages, dilations)
    ]
    for row in range(stages[0].high + 1):
        line = line_of(row, shard_rows, odd)
        slot = jnp.where(odd == 1, 1 - row // shard_rows, row // shard_rows)
        stacks[0].put(row, raw_row(wide, slot, line, shard_rows, channels, width))
    for layer in range(DEPTH - 1):
        stage = stages[layer + 1]

        def store(row, value):
            stacks[layer + 1].put(row, value.astype(BF16))

        block_one(weights, layer, stage, stage.early, range(stage.early_low, stage.high + 1), stacks[layer], store)
    for layer in range(DEPTH):
        groups, _ = late_groups(stages, layer)
        early_sums(stacks[layer], weights.conv(layer), weights.bias(layer), groups, sums[layer])


def chunks_turned(values, lines):
    values = list(values)
    chunk = lax.broadcasted_iota(jnp.int32, values[0].shape, 1) // lines
    for bit in range(3):
        step = 1 << bit
        clear = ((chunk >> bit) & 1) == 0
        for index in range(8):
            if index & step:
                continue
            first, second = values[index], values[index + step]
            values[index] = jnp.where(clear, first, pltpu.roll(second, lines * step, 1))
            values[index + step] = jnp.where(clear, pltpu.roll(first, LANES - lines * step, 1), second)
    return values


def one_late(across, kept_0, kept_1, kept_2, *refs):
    sums, weight_refs, (out, tiles, stack_0, stack_1, stack_2, wide) = refs[:3], refs[3:10], refs[10:]
    channels, shard_rows, width = across.shape
    odd, edge = position()
    stages = plan(shard_rows, dilations)
    weights = Weights(weight_refs, 0, width)
    masks = masks_for(channels, width)
    rows_of_raw([across], 1, wide, shard_rows, channels, width)
    stacks = [
        Stack([(early, stage.early_low), (late, stage.low)], stage.high, dilation, masks)
        for early, late, stage, dilation in zip(
            (kept_0, kept_1, kept_2), (stack_0, stack_1, stack_2), stages, dilations
        )
    ]
    for row in range(stages[0].low, 0):
        stacks[0].put(row, raw_row(wide, 0, line_of(row, shard_rows, odd), shard_rows, channels, width))
    for layer in range(DEPTH):
        stage = stages[layer + 1]

        def store(row, value):
            value = value.astype(BF16)
            if layer == DEPTH - 1:
                out[line_of(row, shard_rows, odd)] = value
                return
            if row < 0:
                value = jnp.where(edge, jnp.zeros_like(value), value)
            stacks[layer + 1].put(row, value)

        groups, _ = late_groups(stages, layer)
        rows = range(stage.low, stage.early_low)
        block_one(weights, layer, stage, stage.late, rows, stacks[layer], store, groups, sums[layer])

    half = channels // 2
    low_lanes = lax.broadcasted_iota(jnp.int32, (half, LANES), 1) < LANES // 2
    for block in range(width // LANES):
        values = [out[row, :, block * LANES : (block + 1) * LANES] for row in range(shard_rows)]
        for index, value in enumerate(chunks_turned(values, shard_rows)):
            top, bottom = value[:half], value[half:]
            device = block * 16 + index
            tiles[device] = jnp.where(low_lanes, top, pltpu.roll(bottom, LANES // 2, 1))
            tiles[device + 8] = jnp.where(low_lanes, pltpu.roll(top, LANES // 2, 1), bottom)


def symmetrize(tiles, own, out):
    shard_rows, channels, width = own.shape
    half = channels // 2
    low_lanes = lax.broadcasted_iota(jnp.int32, (half, LANES), 1) < LANES // 2
    lane_in = lax.broadcasted_iota(jnp.int32, (LANES, LANES), 0)
    lane_out = lax.broadcasted_iota(jnp.int32, (LANES, LANES), 1)
    size = shard_rows
    turned = (lane_out // (size * size)) * (size * size) + (lane_out % size) * size + (lane_out // size) % size
    swap = jnp.where(lane_in == turned, 1.0, 0.0).astype(BF16)
    for block in range(width // LANES):
        values = []
        for index in range(8):
            first, second = tiles[block * 16 + index], tiles[block * 16 + index + 8]
            top = jnp.where(low_lanes, first, pltpu.roll(second, LANES // 2, 1))
            bottom = jnp.where(low_lanes, pltpu.roll(first, LANES // 2, 1), second)
            values += [top, bottom]
        stacked = jnp.concatenate(values, axis=0)
        stacked = jnp.dot(stacked, swap, preferred_element_type=F32).astype(BF16)
        values = [stacked[index * channels : (index + 1) * channels] for index in range(8)]
        lanes = slice(block * LANES, (block + 1) * LANES)
        for row, value in enumerate(chunks_turned(values, shard_rows)):
            out[row, :, lanes] = mean_of(own[row, :, lanes], value)


def two_steps():
    return dilations + (dilations[0],)


LAYERS_OF = (0, 1, 1, 2, 2, 3)
SUMS_OF = (0, 1, 1, 2, 2, 3)


def two_early(chip, *refs):
    weight_refs, stack_refs, sums = refs[:7], refs[7:13], refs[13:]
    _, shard_rows, channels, width = chip.shape
    odd, _ = position()
    steps = two_steps()
    stages = plan(shard_rows, steps)
    weights = Weights(weight_refs, DEPTH, width)
    masks = masks_for(channels, width)
    stacks = [[], [], [], []]
    for ref, index in zip(stack_refs, LAYERS_OF):
        stacks[index].append(Stack([(ref, stages[index].early_low)], stages[index].high, steps[index], masks))
    for row in range(stages[0].high + 1):
        slot = jnp.where(odd == 1, 1 - row // shard_rows, row // shard_rows)
        stacks[0][0].put(row, chip[slot, line_of(row, shard_rows, odd)])
    sources = stacks[0] * 2
    for layer in range(DEPTH):
        stage = stages[layer + 1]

        def store(row, values):
            if layer == DEPTH - 1:
                values = [mean_of(*values)]
            for target, value in zip(stacks[layer + 1], values):
                target.put(row, value)

        block_two(weights, layer, stage, stage.early, range(stage.early_low, stage.high + 1), sources, store)
        sources = stacks[layer + 1]
    for ref, layer, turn in zip(sums, SUMS_OF, (0, 0, 1, 0, 1, 0)):
        groups, _ = late_groups(stages, layer)
        kernel = weights.conv_turned(layer) if turn else weights.conv(layer)
        bias = weights.bias(layer)
        if layer == 0:
            kernel = jnp.concatenate([kernel, weights.conv_turned(layer)], axis=0)
            bias = jnp.concatenate([bias, bias], axis=0)
        early_sums(stacks[layer][turn], kernel, bias, groups, ref)


def two_late(across, *refs):
    kept_refs, sums, weight_refs = refs[:6], refs[6:12], refs[12:19]
    out, stack_refs, (wide, buffer, sems) = refs[19], refs[20:26], refs[26:]
    shard_rows, channels, width = across.shape
    odd, edge = position()
    steps = two_steps()
    stages = plan(shard_rows, steps)
    weights = Weights(weight_refs, DEPTH, width)
    masks = masks_for(channels, width)
    stacks = [[], [], [], []]
    for early, late, index in zip(kept_refs, stack_refs, LAYERS_OF):
        stage = stages[index]
        stacks[index].append(Stack([(early, stage.early_low), (late, stage.low)], stage.high, steps[index], masks))
    for row in range(stages[0].low, 0):
        stacks[0][0].put(row, across[line_of(row, shard_rows, odd)])
    sources = stacks[0] * 2
    for layer in range(DEPTH):
        stage = stages[layer + 1]

        def store(row, values):
            if layer == DEPTH - 1:
                values = [mean_of(*values)]
            for target, value in zip(stacks[layer + 1], values):
                if row < 0:
                    value = jnp.where(edge, jnp.zeros_like(value), value)
                target.put(row, value)

        groups, _ = late_groups(stages, layer)
        parts = [ref for ref, place in zip(sums, SUMS_OF) if place == layer]
        block_two(
            weights, layer, stage, stage.late, range(stage.low, stage.early_low), sources, store, groups,
            parts if len(parts) == 2 else parts * 2,
        )
        sources = stacks[layer + 1]

    stage = stages[DEPTH + 1]

    def store_last(row, value):
        picked = pl.ds(line_of(row, shard_rows, odd), channels, stride=shard_rows)
        for block in range(width // LANES):
            wide[block, picked, :] = value[:, block * LANES : (block + 1) * LANES]

    groups, _ = late_groups(stages, DEPTH)
    rows = range(stage.low, stage.high + 1)
    block_one(weights, DEPTH, stage, stage.late, rows, sources[0], store_last, groups, sums[-1])
    copies = []
    part = channels // PARTS
    for index in range(PARTS):
        lines = slice(index * part * shard_rows, (index + 1) * part * shard_rows)
        whole = jnp.concatenate([wide[block, lines, :] for block in range(width // LANES)], axis=1)
        buffer[index * part : (index + 1) * part] = whole.reshape(part, shard_rows, width).astype(BF16)
        place = pl.ds(index * part, part)
        copies.append(pltpu.make_async_copy(buffer.at[place], out.at[place], sems.at[index]))
        copies[-1].start()
    for copy in copies:
        copy.wait()


VMEM = pl.BlockSpec(memory_space=pltpu.VMEM)
HBM = pl.BlockSpec(memory_space=pltpu.HBM)


class Calls:
    def __init__(self, channels, shard_rows, width, inner, size):
        self.channels, self.shard_rows, self.width, self.inner, self.size = channels, shard_rows, width, inner, size
        self.one = plan(shard_rows, dilations)
        self.two = plan(shard_rows, two_steps())

    def stack(self, low, high):
        return (max(high - low + 1, 1), 3 * self.channels, self.width)

    def early(self, stage):
        return self.stack(stage.early_low, stage.high)

    def late(self, stage):
        return pltpu.VMEM(self.stack(stage.low, stage.early_low - 1), BF16)

    def sums(self, stages, layer, copies=1):
        rows = copies * group_of(stages[layer + 1].dilation) * self.inner
        return jax.ShapeDtypeStruct((max(late_groups(stages, layer)[1], 1), rows, self.width), F32)

    def wide(self, *shards):
        return pltpu.VMEM(shards + (self.width // LANES, self.channels * self.shard_rows, LANES), F32)

    def call(self, body, args, shapes, scratch, specs=None, out_spec=VMEM):
        shapes = [shape if isinstance(shape, jax.ShapeDtypeStruct) else jax.ShapeDtypeStruct(shape, BF16) for shape in shapes]
        single = len(shapes) == 1
        return pl.pallas_call(
            body,
            out_shape=shapes[0] if single else shapes,
            in_specs=specs or [VMEM] * len(args),
            out_specs=out_spec if single else [VMEM] * len(shapes),
            scratch_shapes=scratch,
            compiler_params=pltpu.CompilerParams(vmem_limit_bytes=(10 + 6 * self.width // LANES) * 1024 * 1024),
            name=body.__name__,
        )(*args)

    def prepare(self, w_conv, bias_in, w_out, bias_out):
        layers, inner, channels = w_conv.shape[0], self.inner, self.channels

        def banded(steps, count):
            return (sum(1 for step in steps if group_of(step) == count), count * inner, 3 * (count + 2) * channels)

        shapes = [
            banded(layer_steps(), 2), banded(layer_steps(), 4), banded(dilations, 2), banded(dilations, 4),
            (layers, channels, inner),
            jax.ShapeDtypeStruct((layers, 4 * inner, LANES), F32),
            jax.ShapeDtypeStruct((layers, channels, LANES), F32),
        ]
        scratch = [
            pltpu.VMEM(w_conv.shape, BF16), pltpu.VMEM(w_out.shape, BF16),
            pltpu.VMEM(bias_in.shape, F32), pltpu.VMEM(bias_out.shape, F32), pltpu.SemaphoreType.DMA((4,)),
        ]
        args = [pltpu.with_memory_space_constraint(arg, pltpu.HBM) for arg in (w_conv, bias_in, w_out, bias_out)]
        return self.call(
            prepare, args, shapes, scratch, [HBM] * 4
        )

    def one_early(self, *args):
        shapes = [self.early(stage) for stage in self.one[:DEPTH]]
        shapes += [self.sums(self.one, layer) for layer in range(DEPTH)]
        return self.call(one_early, args, shapes, [self.wide(2)])

    def one_late(self, *args):
        shapes = [(self.shard_rows, self.channels, self.width), (self.size, self.channels // 2, LANES)]
        return self.call(one_late, args, shapes, [self.late(stage) for stage in self.one[:DEPTH]] + [self.wide(1)])

    def symmetrize(self, *args):
        return self.call(symmetrize, args, [(self.shard_rows, self.channels, self.width)], [])

    def two_early(self, *args):
        shapes = [self.early(self.two[index]) for index in LAYERS_OF]
        shapes += [self.sums(self.two, layer, 2 if layer == 0 else 1) for layer in SUMS_OF]
        return self.call(two_early, args, shapes, [])

    def two_late(self, *args):
        scratch = [self.late(self.two[index]) for index in LAYERS_OF] + [self.wide()]
        shape = (self.channels, self.shard_rows, self.width)
        scratch += [pltpu.VMEM(shape, BF16), pltpu.SemaphoreType.DMA((PARTS,))]
        return self.call(two_late, args, [shape], scratch, None, HBM)


def neighbours(array, axis):
    size = lax.axis_size(axis)
    edges = [(i, i + 1) for i in range(1, size - 1, 2)]
    edges = edges + [(j, i) for i, j in edges]
    across = lax.ppermute(array, axis, edges)
    chip = lax.all_gather(array, axis, axis_index_groups=[[i, i + 1] for i in range(0, size, 2)])
    return across, chip


def on_device(features, w_conv, bias_in, w_out, bias_out):
    channels, shard_rows, width = features.shape
    calls = Calls(channels, shard_rows, width, w_conv.shape[2], lax.axis_size("row"))
    across, chip = neighbours(features, "row")
    weights = calls.prepare(w_conv, bias_in, w_out.transpose(0, 2, 1), bias_out)
    kept = calls.one_early(chip, *weights)
    field, tiles = calls.one_late(across, *kept, *weights)
    received = lax.all_to_all(tiles, "row", split_axis=0, concat_axis=0, tiled=True)
    field = calls.symmetrize(received, field)
    across, chip = neighbours(field, "row")
    kept = calls.two_early(chip, *weights)
    return calls.two_late(across, *kept, *weights)


def solution(mesh):
    in_specs = (P("groups", "row", None), P(), P(), P(), P())
    out_specs = P("groups", "row", None)
    return jax.shard_map(
        on_device, mesh=mesh, in_specs=in_specs, out_specs=out_specs, check_vma=False
    )
```
